32 devices in a mesh: fsdp: 2 (over y), ctx: 16 (over z, x, core).
Axes of the slice: x: 2, y: 2, z: 4, core: 2. Of those that a mesh axis runs over, the one named last changes fastest.
Arguments:
- tokens: bfloat16 [4, 1024, 2048], P('fsdp', 'ctx'), may hold values from -6 to 6
- out_grad: bfloat16 [4, 1024, 2048], P('fsdp', 'ctx'), may hold values from -6 to 6
- segments: int32 [4, 1024], P('fsdp'), may hold values from 0 to 12, as said below
- path_mask: int32 [4, 13, 13], P('fsdp'), may hold values from 0 to 1, as said below
- expert_ids: int32 [4, 1024, 6], P('fsdp', 'ctx'), may hold values from 0 to 15, all different within a row; in each aligned block of 64 rows (0 to 63, 64 to 127, ..., all dimensions but the last counted through in order) at most 32 rows name the same one
- norm_attn: bfloat16 [2048], P(('fsdp', 'ctx')), may hold values from 0.5 to 1.5
- attn_q: bfloat16 [2048, 3072], P(('fsdp', 'ctx')), may hold values from -0.25 to 0.25
- attn_kva: bfloat16 [2048, 576], P(('fsdp', 'ctx')), may hold values from -0.125 to 0.125
- norm_latent: bfloat16 [512], P(('fsdp', 'ctx')), may hold values from 0.5 to 1.5
- attn_kvb: bfloat16 [512, 4096], P(('fsdp', 'ctx')), may hold values from -0.25 to 0.25
- attn_out: bfloat16 [2048, 2048], P(('fsdp', 'ctx')), may hold values from -1 to 1
- norm_ffn: bfloat16 [2048], P(('fsdp', 'ctx')), may hold values from 0.5 to 1.5
- router: bfloat16 [2048, 16], P(('fsdp', 'ctx')), may hold values from -0.0625 to 0.0625
- expert_gate: bfloat16 [2048, 22528], P('fsdp', 'ctx'), may hold values from -0.125 to 0.125
- expert_up: bfloat16 [2048, 22528], P('fsdp', 'ctx'), may hold values from -0.125 to 0.125
- expert_down: bfloat16 [2048, 22528], P('fsdp', 'ctx'), may hold values from -1.75 to 1.75
- shared_gate: bfloat16 [2048, 2816], P('fsdp', 'ctx'), may hold values from -0.125 to 0.125
- shared_up: bfloat16 [2048, 2816], P('fsdp', 'ctx'), may hold values from -0.125 to 0.125
- shared_down: bfloat16 [2048, 2816], P('fsdp', 'ctx'), may hold values from -0.1875 to 0.1875
Outputs:
- output: bfloat16 [4, 1024, 2048], P('fsdp', 'ctx')
- input_grad: float32 [4, 1024, 2048], P('fsdp', 'ctx')
- norm_attn_grad: float32 [2048], P(('fsdp', 'ctx'))
- attn_q_grad: float32 [2048, 3072], P(('fsdp', 'ctx'))
- attn_kva_grad: float32 [2048, 576], P(('fsdp', 'ctx'))
- norm_latent_grad: float32 [512], P(('fsdp', 'ctx'))
- attn_kvb_grad: float32 [512, 4096], P(('fsdp', 'ctx'))
- attn_out_grad: float32 [2048, 2048], P(('fsdp', 'ctx'))
- norm_ffn_grad: float32 [2048], P(('fsdp', 'ctx'))
- router_grad: float32 [2048, 16], P(('fsdp', 'ctx'))
- expert_gate_grad: float32 [2048, 22528], P('fsdp', 'ctx')
- expert_up_grad: float32 [2048, 22528], P('fsdp', 'ctx')
- expert_down_grad: float32 [2048, 22528], P('fsdp', 'ctx')
- shared_gate_grad: float32 [2048, 2816], P('fsdp', 'ctx')
- shared_up_grad: float32 [2048, 2816], P('fsdp', 'ctx')
- shared_down_grad: float32 [2048, 2816], P('fsdp', 'ctx')
The draws below stay inside these ranges and needn't reach their ends.
Inputs may be any that keep to these rules, and one draw needn't show every extreme that they name: `segments`: within each tree the ids never fall; id 0 is the trunk and holds the first 409 tokens, ids 1 to 4 are branches and 5 to 12 leaves, each holding one token or more. path_mask[s, u] is 1 exactly when segment u is s or an ancestor of s; the trunk is an ancestor of every segment and each branch is the parent of two leaves. `expert_ids`: A token names 6 different experts. Of the 64 tokens of one tree that one device holds, no expert is named by more than 32, a bound that some block reaches.
All inputs are finite; a program needn't handle non-finite values.
Results may differ from the reference program's by a relative error of at most 0.023.
Values may be sent and summed in bfloat16 or wider, within the bound.
A program may use at most 384 MiB of HBM per device.

```python
import math
import jax
import jax.numpy as jnp
import numpy as np
from jax import lax

D = 2048
H = 16
DN = 128
DR = 64
DV = 128
LAT = 512
F = 1408
TOP = 6
SEGS = 13
FS = 2816
EXPERTS = 16
TREE = 1024
TOK_LOC = 64
TREES = 4
CAP = 32
N_CTX = 16


def tree_layout(key):

    def one_tree(index):
        subkey = jax.random.fold_in(jax.random.fold_in(key, 7013), index)
        size_key, parent_key = jax.random.split(subkey)
        trunk = TREE * 2 // 5
        remaining = TREE - trunk
        shares = jax.random.randint(size_key, (SEGS - 1,), 2, 6).astype(jnp.int32)
        lengths = (remaining * shares // jnp.sum(shares)).astype(jnp.int32)
        lengths = lengths.at[SEGS - 2].add(remaining - jnp.sum(lengths))
        lengths = jnp.concatenate([jnp.full((1,), trunk, jnp.int32), lengths])
        ends = jnp.cumsum(lengths).astype(jnp.int32)
        places = jnp.arange(TREE, dtype=jnp.int32)
        segment = jnp.sum((places[:, None] >= ends[None, :]).astype(jnp.int32), axis=1).astype(jnp.int32)
        leaf_parent = (jax.random.permutation(parent_key, SEGS - 5) // 2 + 1).astype(jnp.int32)
        parent = jnp.concatenate([jnp.zeros((5,), jnp.int32), leaf_parent])
        labels = jnp.arange(SEGS, dtype=jnp.int32)
        on_path = (labels[None, :] == labels[:, None]) | (labels[None, :] == 0) | (labels[None, :] == parent[:, None])
        return (segment, on_path.astype(jnp.int32))
    return jax.vmap(one_tree)(jnp.arange(TREES, dtype=jnp.int32))


def draw_segments(key, part):
    return tree_layout(key)[0]


def draw_path_mask(key, part):
    return tree_layout(key)[1]


def level_of(own_key, extent, cuts, smallest, top_value):
    def one(dim, parts):
        draws = jax.random.uniform(jax.random.fold_in(jax.random.fold_in(own_key, 6), dim), (parts,), jnp.float32, smallest / len(cuts), top_value / len(cuts))
        return jnp.repeat(jnp.exp(draws), extent[dim] // parts).reshape((-1,) + (1,) * (len(extent) - dim - 1))

    factor_of = one(*cuts[0])
    for cut in cuts[1:]:
        factor_of = factor_of * one(*cut)
    return factor_of


def shared_out(own_key, own, number, rows, number_of, top, limit, skew):
    order = jax.random.permutation(own_key, number_of)
    heavy_load, common = load_shares(number_of, rows * top, limit, skew, True), load_shares(number_of, rows * top, limit, skew, False)
    places = jnp.arange(number_of)

    def named(sizes, turn):
        used = int((sizes > 0).sum())
        fixed = max(1, used // 4)
        shifted = fixed + (places - fixed + turn * (used - fixed)) % max(1, number_of - fixed)
        return jnp.zeros((number_of,), jnp.int32).at[order[jnp.where(places < fixed, places, shifted)]].set(jnp.asarray(sizes, jnp.int32))

    sizes = jnp.where(number % 4 == 0, named(heavy_load, number // 4), named(common, number - number // 4 - 1))
    mixed = jax.random.permutation(jax.random.fold_in(own, 3), number_of)
    giver, sink = mixed[0:number_of // 2 * 2:2], mixed[1:number_of // 2 * 2:2]
    slack = jnp.minimum(sizes[giver] - 1, limit - sizes[sink]) // 2
    slack = jnp.where((giver == order[0]) | (sink == order[0]) | (sizes[sink] == 0), 0, jnp.maximum(slack, 0))
    shifted = jax.random.randint(jax.random.fold_in(own, 4), (number_of // 2,), 0, 1 << 20) % (slack + 1)
    sizes = sizes.at[giver].add(-shifted).at[sink].add(shifted)
    items = jnp.searchsorted(jnp.cumsum(sizes), jnp.arange(rows * top), side="right").astype(jnp.int32)
    grid = items.reshape(top, rows).T
    grid = grid[jax.random.permutation(jax.random.fold_in(own, 1), rows)]
    turn = jax.random.randint(jax.random.fold_in(own, 2), (rows, 1), 0, top)
    return jnp.take_along_axis(grid, (jnp.arange(top)[None, :] + turn) % top, axis=1)


def load_shares(amount, total, bound, skew, full):
    portions = [(1 << 20) // math.isqrt(standing ** skew) + 1 for standing in range(1, amount + 1)]
    largest = bound if full else min(bound, max(-(-total // amount), total * portions[0] // sum(portions)))
    least = 1 if total - largest >= amount - 1 else 0
    given, surplus = [largest] + [least] * (amount - 1), total - largest - least * (amount - 1)
    while surplus > 0:
        candidates = [i for i in range(1, amount) if given[i] < largest] or [i for i in range(1, amount) if given[i] < bound]
        whole, left = sum([portions[i] for i in candidates]), surplus
        for i in candidates:
            addition = min(bound - given[i], max(1, left * portions[i] // whole), surplus)
            given[i] = given[i] + addition
            surplus = surplus - addition
    return np.array(given)


def noise(own_key, extent, spread, limit, cuts=(), kind=jnp.bfloat16):
    gain = level_of(own_key, extent, cuts, -0.22, 0.18) if cuts else 1.0
    values = jax.random.normal(own_key, extent, jnp.float32) * spread * gain
    return jnp.minimum(jnp.maximum(values, -limit), limit).astype(kind)


def setup_inputs(seed: int = 0) -> dict:
    key_list = jax.random.split(jax.random.key(seed), 20)
    tokens = noise(key_list[0], (TREES, TREE, D), 1.0, 6.0, ((0, 2), (1, 16)))
    out_grad = noise(key_list[1], (TREES, TREE, D), 1.0, 6.0, ((0, 2), (1, 16)))
    segments = draw_segments(jax.random.fold_in(key_list[19], 71), 0)
    path_mask = draw_path_mask(jax.random.fold_in(key_list[19], 71), 0)
    expert_ids_keys = jax.random.split(jax.random.fold_in(key_list[4], 1), TREES * TREE // TOK_LOC)
    expert_ids_turns = jax.random.permutation(jax.random.fold_in(key_list[4], 3), TREES * TREE // TOK_LOC)
    expert_ids = jax.vmap(lambda own, number: shared_out(jax.random.fold_in(key_list[4], 2), own, number, TOK_LOC, EXPERTS, TOP, CAP, 1))(expert_ids_keys, expert_ids_turns).reshape((TREES, TREE, TOP))
    norm_attn = jnp.clip(1.0 + 0.1 * jax.random.normal(key_list[5], (D,), jnp.float32), 0.5, 1.5).astype(jnp.bfloat16)
    attn_q = noise(key_list[6], (D, H * (DN + DR)), (D // 4) ** -0.5, 0.25, ((0, 32),))
    attn_kva = noise(key_list[7], (D, LAT + DR), D ** -0.5, 0.125, ((0, 32),))
    norm_latent = jnp.clip(1.0 + 0.1 * jax.random.normal(key_list[8], (LAT,), jnp.float32), 0.5, 1.5).astype(jnp.bfloat16)
    attn_kvb = noise(key_list[9], (LAT, H * (DN + DV)), LAT ** -0.5, 0.25, ((0, 32),))
    attn_out = noise(key_list[10], (H * DV, D), (H * DV // 64) ** -0.5, 1.0, ((0, 32),))
    norm_ffn = jnp.clip(1.0 + 0.1 * jax.random.normal(key_list[11], (D,), jnp.float32), 0.5, 1.5).astype(jnp.bfloat16)
    router = noise(key_list[12], (D, EXPERTS), (4 * D) ** -0.5, 0.0625, ((0, 32),))
    expert_gate = noise(key_list[13], (D, EXPERTS * F), D ** -0.5, 0.125, ((0, 2), (1, 16)))
    expert_up = noise(key_list[14], (D, EXPERTS * F), D ** -0.5, 0.125, ((0, 2), (1, 16)))
    expert_down = noise(key_list[15], (D, EXPERTS * F), (max(1, F * TOP // (3 * EXPERTS * EXPERTS))) ** -0.5, 1.75, ((0, 2), (1, 16)))
    shared_gate = noise(key_list[16], (D, FS), D ** -0.5, 0.125, ((0, 2), (1, 16)))
    shared_up = noise(key_list[17], (D, FS), D ** -0.5, 0.125, ((0, 2), (1, 16)))
    shared_down = noise(key_list[18], (D, FS), (FS // 3) ** -0.5, 0.1875, ((0, 2), (1, 16)))
    return dict(tokens=tokens, out_grad=out_grad, segments=segments, path_mask=path_mask, expert_ids=expert_ids, norm_attn=norm_attn, attn_q=attn_q, attn_kva=attn_kva, norm_latent=norm_latent, attn_kvb=attn_kvb, attn_out=attn_out, norm_ffn=norm_ffn, router=router, expert_gate=expert_gate, expert_up=expert_up, expert_down=expert_down, shared_gate=shared_gate, shared_up=shared_up, shared_down=shared_down)


@jax.custom_vjp
def low(v):
    return lax.optimization_barrier(v.astype(jnp.bfloat16)).astype(jnp.float32)

@jax.custom_vjp
def low_back(v):
    return v

def low_keep(v):
    return (low(v), None)

def low_pass(kept, grad):
    return (grad,)

def back_keep(v):
    return (v, None)

def back_low(kept, grad):
    return (low(grad),)
low.defvjp(low_keep, low_pass)
low_back.defvjp(back_keep, back_low)
epsilon = 1e-06
rope_base = 10000.0
highest_mode = lax.Precision.HIGHEST

def product(left, right):
    return jnp.dot(left, right, precision=highest_mode)

def normalize(tensor_in, gain_vec):
    return tensor_in * lax.rsqrt(lax.optimization_barrier(jnp.mean(tensor_in * tensor_in, axis=-1, keepdims=True)) + epsilon) * gain_vec

def rotate(tensor_in, rotation):
    half_width = tensor_in.shape[-1] // 2
    former = tensor_in[..., :half_width]
    latter = tensor_in[..., half_width:]
    cosine = jnp.cos(rotation)
    sine = jnp.sin(rotation)
    return jnp.concatenate([former * cosine - latter * sine, latter * cosine + former * sine], axis=-1)

def tree_mask(segment_ids, path_table, first_row, row_count):
    labels = jnp.arange(SEGS, dtype=jnp.int32)
    own_ids = lax.dynamic_slice_in_dim(segment_ids, first_row, row_count)
    ancestry = lax.optimization_barrier(jnp.sum(jnp.where(own_ids[:, None, None] == labels[None, :, None], path_table[None, :, :], 0), axis=1))
    related = lax.optimization_barrier(jnp.sum(jnp.where(segment_ids[None, None, :] == labels[None, :, None], ancestry[:, :, None], 0), axis=1))
    places = jnp.arange(segment_ids.shape[0], dtype=jnp.int32)
    queries = first_row + jnp.arange(row_count, dtype=jnp.int32)
    allowed = (related > 0) & (places[None, :] <= queries[:, None])
    positions = (lax.optimization_barrier(jnp.sum(allowed.astype(jnp.int32), axis=1)) - 1).astype(jnp.int32)
    return (allowed, positions)

def swiglu(row_inputs, w_gate, w_up, w_down):
    gate_pre = low_back(product(row_inputs, w_gate))
    up_pre = low_back(product(row_inputs, w_up))
    hidden_act = low(jax.nn.silu(gate_pre) * up_pre)
    return product(hidden_act, w_down.T)

def routed_experts(hidden_mid, gate_weights, chosen, expert_gate, expert_up, expert_down):
    flat_ids = chosen.reshape(-1).astype(jnp.int32)
    route_order = jnp.argsort(flat_ids, stable=True).astype(jnp.int32)
    labels = jnp.arange(EXPERTS, dtype=jnp.int32)
    counts = lax.optimization_barrier(jnp.sum((flat_ids[None, :] == labels[:, None]).astype(jnp.int32), axis=1)).astype(jnp.int32)
    starts = (jnp.cumsum(counts) - counts).astype(jnp.int32)
    slot_index = jnp.arange(N_CTX * CAP, dtype=jnp.int32)
    flat_gates = gate_weights.reshape(-1)

    def one_expert(combined, expert):
        places = jnp.minimum(starts[expert] + slot_index, TREE * TOP - 1).astype(jnp.int32)
        routes = route_order[places]
        owners = (routes // TOP).astype(jnp.int32)
        is_valid = slot_index < counts[expert]
        row_inputs = low_back(hidden_mid[owners])
        columns = (expert * F).astype(jnp.int32)
        w_gate = lax.dynamic_slice_in_dim(expert_gate, columns, F, 1)
        w_up = lax.dynamic_slice_in_dim(expert_up, columns, F, 1)
        w_down = lax.dynamic_slice_in_dim(expert_down, columns, F, 1)
        expert_rows = low(low_back(swiglu(row_inputs, w_gate, w_up, w_down)))
        weighting = jnp.where(is_valid, flat_gates[routes], 0.0)
        return (combined.at[owners].add(weighting[:, None] * expert_rows), None)
    combined, unused = lax.scan(one_expert, jnp.zeros((TREE, D), jnp.float32), labels)
    return combined

def layer(tokens_in, norm_attn, attn_q, attn_kva, norm_latent, attn_kvb, attn_out, norm_ffn, router, expert_gate, expert_up, expert_down, shared_gate, shared_up, shared_down, allowed, rotation, chosen):
    score_scale = 1.0 / math.sqrt(DN + DR)
    hidden_in = low(normalize(tokens_in, norm_attn))
    query = low_back(product(hidden_in, attn_q)).reshape(TREE, H, DN + DR)
    query_nope = low(query[..., :DN])
    query_rope = low(rotate(query[..., DN:], rotation[:, None, :]))
    latent = low_back(product(hidden_in, attn_kva))
    key_latent = low(normalize(latent[:, :LAT], norm_latent))
    key_rope = low(rotate(latent[:, LAT:], rotation))
    expand = attn_kvb.reshape(LAT, H, DN + DV)
    query_latent = low(low_back(jnp.einsum('thn,chn->thc', query_nope, expand[..., :DN], precision=highest_mode)))
    raw_scores = jnp.einsum('thc,jc->thj', query_latent, key_latent, precision=highest_mode)
    raw_scores = raw_scores + jnp.einsum('thr,jr->thj', query_rope, key_rope, precision=highest_mode)
    scores = jnp.where(allowed[:, None, :], low_back(raw_scores * score_scale), -1e+30)
    weights = low(jax.nn.softmax(scores, axis=-1))
    mixed = low(low_back(jnp.einsum('thj,jc->thc', weights, key_latent, precision=highest_mode)))
    heads = low(low_back(jnp.einsum('thc,chv->thv', mixed, expand[..., DN:], precision=highest_mode)))
    heads = heads.reshape(TREE, H * DV)
    residual = tokens_in + low_back(product(heads, attn_out))
    hidden_mid = low(normalize(residual, norm_ffn))
    expert_probs = jax.nn.softmax(low_back(product(hidden_mid, router)), axis=-1)
    gate_weights = jnp.take_along_axis(expert_probs, chosen, axis=1)
    routed = routed_experts(hidden_mid, gate_weights, chosen, expert_gate, expert_up, expert_down)
    shared = low_back(swiglu(hidden_mid, shared_gate, shared_up, shared_down))
    return residual + routed + shared

def reference(tokens, out_grad, segments, path_mask, expert_ids, norm_attn, attn_q, attn_kva, norm_latent, attn_kvb, attn_out, norm_ffn, router, expert_gate, expert_up, expert_down, shared_gate, shared_up, shared_down):
    params = tuple((w.astype(jnp.float32) for w in (norm_attn, attn_q, attn_kva, norm_latent, attn_kvb, attn_out, norm_ffn, router, expert_gate, expert_up, expert_down, shared_gate, shared_up, shared_down)))
    frequency = rope_base ** (-(jnp.arange(DR // 2, dtype=jnp.float32) * 2.0 / DR))

    def one_tree(totals, tree_data):
        tokens_in, grad_in, segment_ids, path_table, chosen = tree_data
        allowed, positions = tree_mask(segment_ids, path_table, 0, TREE)
        rotation = positions.astype(jnp.float32)[:, None] * frequency[None, :]

        def forward(tokens_f, *weights_f):
            return layer(tokens_f, *weights_f, allowed, rotation, chosen)
        result, pullback = jax.vjp(forward, tokens_in.astype(jnp.float32), *params)
        grads = pullback(grad_in.astype(jnp.float32))
        totals = tuple((former + latter for former, latter in zip(totals, grads[1:])))
        return (totals, (result.astype(jnp.bfloat16), grads[0]))
    starting = tuple((jnp.zeros(w.shape, jnp.float32) for w in params))
    totals, outs = lax.scan(one_tree, starting, (tokens, out_grad, segments, path_mask, expert_ids))
    return (outs[0], outs[1], totals[0], totals[1], totals[2], totals[3], totals[4], totals[5], totals[6], totals[7], totals[8], totals[9], totals[10], totals[11], totals[12], totals[13])
```

```python
import functools
import math

import jax
import jax.numpy as jnp
from jax import lax
from jax.experimental import pallas as pl
from jax.experimental.pallas import tpu as pltpu
from jax.sharding import PartitionSpec as P

D = 2048
H = 16
DN = 128
DR = 64
DV = 128
LAT = 512
TOP = 6
SEGS = 13
PACK = 2048

MESH = pl.DeviceIdType.MESH
BF = jnp.bfloat16
F32 = jnp.float32

epsilon = 1e-06
rope_base = 10000.0


def multiply(left, right):
    return jnp.dot(left, right, preferred_element_type=F32)


def multiply_transposed(left, right):
    return lax.dot_general(left, right, (((1,), (1,)), ((), ())), preferred_element_type=F32)


def transposed_multiply(left, right):
    return lax.dot_general(left, right, (((0,), (0,)), ((), ())), preferred_element_type=F32)


def normalize(tensor_in, gain_vec):
    inverse = lax.rsqrt(jnp.mean(tensor_in * tensor_in, axis=-1, keepdims=True) + epsilon)
    normed = tensor_in * inverse
    return (normed, inverse, normed * gain_vec)


def normalize_back(grad_out, normed, inverse, gain_vec):
    weighted = grad_out * gain_vec
    centre = jnp.mean(weighted * normed, axis=-1, keepdims=True)
    return (inverse * (weighted - normed * centre), jnp.sum(grad_out * normed, axis=0))


def rotate(tensor_in, cosine, sine):
    half_width = tensor_in.shape[-1] // 2
    former = tensor_in[..., :half_width]
    latter = tensor_in[..., half_width:]
    return jnp.concatenate(
        [former * cosine - latter * sine, latter * cosine + former * sine], axis=-1
    )


def tree_mask(segment_ids, path_table, first_row, row_count):
    labels = jnp.arange(SEGS, dtype=jnp.int32)
    own_ids = lax.dynamic_slice_in_dim(segment_ids, first_row, row_count)
    own_hot = (own_ids[:, None] == labels[None, :]).astype(BF)
    all_hot = (segment_ids[:, None] == labels[None, :]).astype(BF)
    ancestry = multiply(own_hot, path_table.astype(BF)).astype(BF)
    related = multiply_transposed(ancestry, all_hot)
    places = jnp.arange(segment_ids.shape[0], dtype=jnp.int32)
    queries = first_row + jnp.arange(row_count, dtype=jnp.int32)
    allowed = (related > 0) & (places[None, :] <= queries[:, None])
    positions = jnp.sum(allowed.astype(jnp.int32), axis=1) - 1
    return (allowed, positions)


def three_parts(value):
    first = lax.reduce_precision(value, 8, 7)
    second = lax.reduce_precision(value - first, 8, 7)
    third = value - first - second
    return (first.astype(BF), second.astype(BF), third.astype(BF))


class Ring:
    def __init__(self, nf, nc):
        self.nf, self.chips = nf, nc // 2
        half = self.chips // 2
        if nf == 2:
            self.place = lambda p: (1 - p // half) * 2 * p + (p // half) * (4 * half - 1 - 2 * p)
            self.where = lambda j: (1 - j % 2) * (j // 2) + (j % 2) * (2 * half - 1 - j // 2)
        else:
            self.place = lambda p: (1 - p // half) * p + (p // half) * (3 * half - 1 - p)
            self.where = self.place

    def here(self):
        f, c = lax.axis_index("fsdp"), lax.axis_index("ctx")
        core = c % 2
        return f, c, core, self.where(c // 2), 1 - 2 * core

    def device(self, position, core):
        return self.place((position + 2 * self.chips) % self.chips) * 2 + core


def greet(ring, f, c, core, p, way, over_fsdp):
    barrier = pltpu.get_barrier_semaphore()
    targets = [(f, ring.device(p - way, core)), (f, c + 1 - 2 * core)]
    if over_fsdp:
        targets += [((f + k) % ring.nf, c) for k in range(1, ring.nf)]
    for target in targets:
        pl.semaphore_signal(barrier, inc=1, device_id=target, device_id_type=MESH)
    pl.semaphore_wait(barrier, len(targets))


def gather_kernel(ring, wide, leads, count, *refs):
    ins, outs = refs[:count], refs[count : 2 * count]
    own_sem, yss, yrs, rss, rrs, sss, srs = refs[2 * count :]
    f, c, core, p, way = ring.here()
    n, nf = ring.chips, ring.nf
    greet(ring, f, c, core, p, way, any(wide))
    to_next = (f, ring.device(p + way, core))
    to_twin = (f, c + 1 - 2 * core)
    started, own = [], []

    def remote(src, dst, ss, rs, dev):
        return pltpu.make_async_remote_copy(
            src_ref=src, dst_ref=dst, send_sem=ss, recv_sem=rs, device_id=dev, device_id_type=MESH
        )

    streams, late = [], []
    number = 0
    for i in range(count):
        if wide[i]:
            streams.append((number, i, f, ins[i]))
            number += 1
        else:
            for a in range(leads[i]):
                streams.append((number, i, a, ins[i].at[a]))
                number += 1
    first = len(streams)
    yn = 0
    for i in range(count):
        if wide[i]:
            for k in range(1, nf):
                late.append((number, i, (f - k + nf) % nf, k, yn))
                number += 1
                yn += 1

    def send_ring(s, number, i, lead, owner, src):
        cp = remote(src, outs[i].at[lead, owner], rss.at[s, number], rrs.at[s, number], to_next)
        cp.start()
        started.append(cp)

    def send_twin(s, number, i, lead, owner, src):
        cp = remote(src, outs[i].at[lead, owner], sss.at[s, number], srs.at[s, number], to_twin)
        cp.start()
        started.append(cp)

    for number, i, lead, k, y in late:
        cp = remote(ins[i], outs[i].at[f, c], yss.at[y], yrs.at[y], ((f + k) % nf, c))
        cp.start()
        started.append(cp)
    for number, i, lead, src in streams:
        send_ring(0, number, i, lead, c, src)
    for number, i, lead, src in streams:
        send_twin(0, number, i, lead, c, src)
        cp = pltpu.make_async_copy(src, outs[i].at[lead, c], own_sem.at[number])
        cp.start()
        own.append(cp)
    everything = [(number, i, lead) for number, i, lead, _ in streams]
    everything += [(number, i, lead) for number, i, lead, _, _ in late]
    for number, i, lead, k, y in late:
        here = outs[i].at[lead, c]
        remote(here, here, yss.at[y], yrs.at[y], to_next).wait_recv()
        send_ring(0, number, i, lead, c, here)
        send_twin(0, number, i, lead, c, here)
    for s in range(1, n):
        owner = ring.device(p - way * s, core)
        for number, i, lead in everything:
            here = outs[i].at[lead, owner]
            remote(here, here, rss.at[s - 1, number], rrs.at[s - 1, number], to_next).wait_recv()
            if s < n - 1:
                send_ring(s, number, i, lead, owner, here)
            send_twin(s, number, i, lead, owner, here)
    for s in range(n):
        owner = ring.device(p + way * s, 1 - core)
        for number, i, lead in everything:
            here = outs[i].at[lead, owner]
            remote(here, here, sss.at[s, number], srs.at[s, number], to_twin).wait_recv()
    for cp in own:
        cp.wait()
    for cp in started:
        cp.wait_send()


def ring_gather(ring, number, arrays, wide):
    n, nf = ring.chips, ring.nf
    leads = [1 if w else a.shape[0] for a, w in zip(arrays, wide)]
    shapes, streams, late, size = [], 0, 0, 0
    for a, w in zip(arrays, wide):
        if w:
            shapes.append(jax.ShapeDtypeStruct((nf, 2 * n) + a.shape, a.dtype))
            streams += nf
            late += nf - 1
        else:
            shapes.append(jax.ShapeDtypeStruct((a.shape[0], 2 * n) + a.shape[1:], a.dtype))
            streams += a.shape[0]
        size += shapes[-1].size * 2
    dma = pltpu.SemaphoreType.DMA
    return pl.pallas_call(
        functools.partial(gather_kernel, ring, tuple(wide), tuple(leads), len(arrays)),
        out_shape=shapes,
        in_specs=[pl.BlockSpec(memory_space=pl.ANY)] * len(arrays),
        out_specs=[pl.BlockSpec(memory_space=pl.ANY)] * len(arrays),
        scratch_shapes=[
            dma((streams,)),
            dma((max(1, late),)),
            dma((max(1, late),)),
            dma((n - 1, streams)),
            dma((n - 1, streams)),
            dma((n, streams)),
            dma((n, streams)),
        ],
        compiler_params=pltpu.CompilerParams(collective_id=number, has_side_effects=True),
        cost_estimate=pl.CostEstimate(flops=0, bytes_accessed=2 * size, transcendentals=0),
        name="ring_gather_%d" % number,
    )(*arrays)


def add_rows(shape, work):
    rows = shape[0]
    step = 16 if rows % 16 == 0 else rows

    def one(r, carry):
        work(pl.ds(pl.multiple_of(r * step, step), step))
        return carry

    lax.fori_loop(0, rows // step, one, 0)


def reduce_kernel(ring, wide, leads, count, *refs):
    ins, outs = refs[:count], refs[count : 2 * count]
    own, twin, got = (refs[(2 + k) * count : (3 + k) * count] for k in range(3))
    refs = refs[5 * count :]
    wides = sum(wide)
    finals, ygots = refs[:wides], refs[wides : 2 * wides]
    own_sem, tss, trs, rss, rrs, yss, yrs = refs[2 * wides :]
    f, c, core, p, way = ring.here()
    n, nf = ring.chips, ring.nf
    greet(ring, f, c, core, p, way, any(wide))
    to_next = (f, ring.device(p + way, core))
    to_twin = (f, c + 1 - 2 * core)

    def remote(src, dst, ss, rs, dev):
        return pltpu.make_async_remote_copy(
            src_ref=src, dst_ref=dst, send_sem=ss, recv_sem=rs, device_id=dev, device_id_type=MESH
        )

    streams = []
    for k in range(max(leads)):
        for i in range(count):
            if k < leads[i]:
                lead = (f + 1 + k) % nf if wide[i] else k
                streams.append((len(streams), i, k, lead))
    started, loads = [], {}
    for s in range(n):
        theirs = ring.device(p + way * (1 + s), 1 - core)
        mine = ring.device(p - way * (1 + s), core)
        for number, i, k, lead in streams:
            cp = remote(
                ins[i].at[lead, theirs], twin[i].at[s, k], tss.at[s, number], trs.at[s, number], to_twin
            )
            cp.start()
            started.append(cp)
            cp = pltpu.make_async_copy(
                ins[i].at[lead, mine], own[i].at[s, k], own_sem.at[s, number]
            )
            cp.start()
            loads[s, number] = cp

    def wait_parts(s, number, i, k):
        loads[s, number].wait()
        here = twin[i].at[s, k]
        remote(here, here, tss.at[s, number], trs.at[s, number], to_twin).wait_recv()

    def pass_on(s, number, i, k, src):
        cp = remote(src, got[i].at[s, k], rss.at[s, number], rrs.at[s, number], to_next)
        cp.start()
        started.append(cp)

    for s in range(n):
        for number, i, k, lead in streams:
            wait_parts(s, number, i, k)
            mine, other = own[i].at[s, k], twin[i].at[s, k]
            if s == 0:

                def start(rows, mine=mine, other=other):
                    mine[rows, :] = (mine[rows, :].astype(F32) + other[rows, :].astype(F32)).astype(BF)

                add_rows(mine.shape, start)
                pass_on(0, number, i, k, mine)
                continue
            came = got[i].at[s - 1, k]
            remote(came, came, rss.at[s - 1, number], rrs.at[s - 1, number], to_next).wait_recv()
            if s < n - 1:

                def middle(rows, mine=mine, other=other, came=came):
                    total = mine[rows, :].astype(F32) + other[rows, :].astype(F32)
                    came[rows, :] = (came[rows, :].astype(F32) + total).astype(BF)

                add_rows(mine.shape, middle)
                pass_on(s, number, i, k, came)
                continue
            if not wide[i]:
                target = outs[i].at[k]
            elif k == nf - 1:
                target = outs[i]
            else:
                target = finals[sum(wide[:i])].at[k]

            def last(rows, mine=mine, other=other, came=came, target=target):
                total = mine[rows, :].astype(F32) + other[rows, :].astype(F32)
                target[rows, :] = (came[rows, :].astype(F32) + total).astype(target.dtype)

            add_rows(mine.shape, last)
            if wide[i] and k < nf - 1:
                w = sum(wide[:i])
                cp = remote(target, ygots[w].at[k], yss.at[w, k], yrs.at[w, k], ((f + 1 + k) % nf, c))
                cp.start()
                started.append(cp)
    for i in range(count):
        if wide[i]:
            w = sum(wide[:i])
            for k in range(nf - 1):
                here = ygots[w].at[k]
                remote(here, here, yss.at[w, k], yrs.at[w, k], to_next).wait_recv()

                def finish(rows, here=here, target=outs[i]):
                    target[rows, :] = target[rows, :] + here[rows, :].astype(F32)

                add_rows(here.shape, finish)
    for cp in started:
        cp.wait_send()


def ring_reduce(ring, number, arrays, wide):
    n, nf = ring.chips, ring.nf
    leads = [a.shape[0] for a in arrays]
    streams = sum(leads)
    block = [a.shape[2:] for a in arrays]
    shapes = [
        jax.ShapeDtypeStruct(b if w else (l,) + b, F32) for b, w, l in zip(block, wide, leads)
    ]
    dma = pltpu.SemaphoreType.DMA
    scratch = [pltpu.VMEM((n, l) + b, BF) for b, l in zip(block, leads)] * 2
    scratch += [pltpu.VMEM((n - 1, l) + b, BF) for b, l in zip(block, leads)]
    scratch += [pltpu.VMEM((nf - 1,) + b, BF) for b, w in zip(block, wide) if w] * 2
    wides = max(1, sum(wide))
    size = sum(a.size * 2 for a in arrays)
    return pl.pallas_call(
        functools.partial(reduce_kernel, ring, tuple(wide), tuple(leads), len(arrays)),
        out_shape=shapes,
        in_specs=[pl.BlockSpec(memory_space=pl.ANY)] * len(arrays),
        out_specs=[pl.BlockSpec(memory_space=pltpu.VMEM)] * len(arrays),
        scratch_shapes=scratch
        + [
            dma((n, streams)),
            dma((n, streams)),
            dma((n, streams)),
            dma((n - 1, streams)),
            dma((n - 1, streams)),
            dma((wides, max(1, nf - 1))),
            dma((wides, max(1, nf - 1))),
        ],
        compiler_params=pltpu.CompilerParams(
            collective_id=number, has_side_effects=True, vmem_limit_bytes=56 << 20
        ),
        cost_estimate=pl.CostEstimate(flops=0, bytes_accessed=2 * size, transcendentals=0),
        name="ring_reduce_%d" % number,
    )(*arrays)


def body(
    tokens,
    out_grad,
    segments,
    path_mask,
    expert_ids,
    norm_attn,
    attn_q,
    attn_kva,
    norm_latent,
    attn_kvb,
    attn_out,
    norm_ffn,
    router,
    expert_gate,
    expert_up,
    expert_down,
    shared_gate,
    shared_up,
    shared_down,
):
    trees, tok_loc = tokens.shape[:2]
    row_total = trees * tok_loc
    nc, nf = lax.axis_size("ctx"), lax.axis_size("fsdp")
    mine, group = lax.axis_index("ctx"), lax.axis_index("fsdp")
    experts = nc
    ring = Ring(nf, nc)
    tree_len = tok_loc * nc
    group_rows = trees * tree_len
    first_row = mine * tok_loc
    capacity = min(tok_loc, tok_loc * TOP * 4 // (3 * experts))
    slot_total = nc * trees * capacity
    score_scale = 1.0 / math.sqrt(DN + DR)
    frequency = rope_base ** (-(jnp.arange(DR // 2, dtype=F32) * 2.0 / DR))
    labels = jnp.arange(experts, dtype=jnp.int32)
    both = ("fsdp", "ctx")
    part = D // nf

    def roll_in(x):
        return lax.dynamic_slice_in_dim(jnp.concatenate([x, x], axis=-1), group * part, D, x.ndim - 1)

    def roll_out(x):
        return lax.dynamic_slice_in_dim(
            jnp.concatenate([x, x], axis=-1), (nf - group) % nf * part, D, x.ndim - 1
        )

    def fetch(w):
        pieces = [w]
        for k in range(1, nf):
            pieces.append(lax.ppermute(w, "fsdp", [(i, (i - k) % nf) for i in range(nf)]))
        return pieces

    shared_w = jnp.concatenate([shared_gate, shared_up, shared_down], axis=1)
    fs = shared_gate.shape[1]
    e_gate, e_up, e_down = fetch(expert_gate), fetch(expert_up), fetch(expert_down)
    s_all = fetch(shared_w)

    small = jnp.concatenate(
        [
            norm_attn,
            norm_ffn,
            norm_latent,
            router.reshape(-1),
            expert_ids.astype(BF).reshape(-1),
        ]
    )
    small = jnp.pad(small, (0, PACK - small.shape[0])).reshape(16, PACK // 16)
    if nf == 2:
        w_latent, w_query, w_expand, small_all = ring_gather(
            ring, 0, [attn_kva, attn_q, attn_kvb, small], [True] * 4
        )
    else:
        w_latent, w_query, w_expand, small_all = (
            lax.all_gather(w, both, axis=0) for w in (attn_kva, attn_q, attn_kvb, small)
        )
    w_output = lax.all_gather(attn_out, both, axis=0, tiled=True)
    w_latent, w_query = w_latent.reshape(D, -1), w_query.reshape(D, -1)
    w_expand = w_expand.reshape(LAT, -1)
    small_all = small_all.reshape(nf * nc, PACK)
    r_one, r_lat, r_router = norm_attn.shape[0], norm_latent.shape[0], router.size
    cuts = [0, r_one, 2 * r_one, 2 * r_one + r_lat, 2 * r_one + r_lat + r_router]
    gain_attn = small_all[:, cuts[0] : cuts[1]].reshape(-1).astype(F32)
    gain_ffn = small_all[:, cuts[1] : cuts[2]].reshape(-1).astype(F32)
    gain_latent = small_all[:, cuts[2] : cuts[3]].reshape(-1).astype(F32)
    w_router = small_all[:, cuts[3] : cuts[4]].reshape(D, experts)
    ids_all = lax.dynamic_slice_in_dim(small_all.reshape(nf, nc, PACK), group, 1, 0)[0]
    ids_all = ids_all[:, cuts[4] : cuts[4] + expert_ids.size].reshape(nc, trees, tok_loc, TOP)
    ids_all = ids_all.transpose(1, 0, 2, 3).reshape(group_rows, TOP)

    upstream_low = out_grad.reshape(row_total, D)
    upstream = upstream_low.astype(F32)
    tree_grads = lax.all_gather(roll_in(out_grad), "ctx", axis=1, tiled=True).reshape(group_rows, D)

    def one_mask(segment_ids, path_table):
        return tree_mask(segment_ids, path_table, first_row, tok_loc)

    allowed, positions = jax.vmap(one_mask)(segments, path_mask)
    rotation = positions.astype(F32)[:, :, None] * frequency[None, None, :]
    cosine, sine = jnp.cos(rotation), jnp.sin(rotation)
    inputs = tokens.astype(F32).reshape(row_total, D)
    normed_in, inverse_in, gained_in = normalize(inputs, gain_attn)
    hidden_in = gained_in.astype(BF)
    latent_all = multiply(hidden_in, w_latent)
    latent_normed, latent_inverse, latent_gained = normalize(latent_all[:, :LAT], gain_latent)
    key_latent = latent_gained.astype(BF).reshape(trees, tok_loc, LAT)
    key_rope = rotate(latent_all[:, LAT:].reshape(trees, tok_loc, DR), cosine, sine).astype(BF)
    (keys,) = ring_gather(
        ring, 1, [jnp.concatenate([key_latent, key_rope], axis=-1)], [False]
    )
    keys = keys.reshape(trees, tree_len, LAT + DR)
    keys_latent = keys[:, :, :LAT]
    query_all = multiply(hidden_in, w_query).reshape(trees, tok_loc, H, DN + DR)
    query_nope = query_all[..., :DN].astype(BF)
    query_rope = rotate(
        query_all[..., DN:], cosine[:, :, None, :], sine[:, :, None, :]
    ).astype(BF)
    expand = w_expand.reshape(LAT, H, DN + DV)
    expand_key = expand[..., :DN]
    expand_value = expand[..., DN:]
    query_latent = jnp.einsum(
        "bthn,chn->bthc", query_nope, expand_key, preferred_element_type=F32
    ).astype(BF)
    query_cat = jnp.concatenate([query_latent, query_rope], axis=-1).reshape(
        trees, tok_loc * H, LAT + DR
    )

    def attention_scores():
        raw_scores = jnp.einsum("bqc,bjc->bqj", query_cat, keys, preferred_element_type=F32)
        raw_scores = raw_scores.reshape(trees, tok_loc, H, tree_len)
        scores = jnp.where(allowed[:, :, None, :], raw_scores * score_scale, -1e30)
        return scores.reshape(trees, tok_loc * H, tree_len)

    scores = attention_scores()
    highest = jnp.max(scores, axis=-1, keepdims=True)
    exp_total = jnp.sum(jnp.exp(scores - highest), axis=-1, keepdims=True)
    log_total = highest + jnp.log(exp_total)
    weights_low = jnp.exp(scores - log_total).astype(BF)
    mixed = jnp.einsum("bqj,bjc->bqc", weights_low, keys_latent, preferred_element_type=F32)
    mixed = mixed.astype(BF).reshape(trees, tok_loc, H, LAT)
    heads = (
        jnp.einsum("bthc,chv->bthv", mixed, expand_value, preferred_element_type=F32)
        .astype(BF)
        .reshape(row_total, H * DV)
    )
    residual = inputs + multiply(heads, w_output)
    normed_mid, inverse_mid, gained_mid = normalize(residual, gain_ffn)
    hidden_mid = gained_mid.astype(BF)
    expert_probs = jax.nn.softmax(multiply(hidden_mid, w_router), axis=-1)

    probs_parts = jnp.concatenate(three_parts(expert_probs), axis=-1)
    probs_parts = jnp.pad(probs_parts, ((0, 0), (0, 128 - 3 * experts)))
    tree_rows, tree_probs = ring_gather(
        ring,
        2,
        [roll_in(hidden_mid).reshape(trees, tok_loc, D), probs_parts.reshape(trees, tok_loc, 128)],
        [False, False],
    )
    tree_rows = tree_rows.reshape(group_rows, D)
    tree_probs = tree_probs.reshape(group_rows, 128)

    member = jnp.any(ids_all == mine.astype(BF), axis=1)
    lanes = 128
    blocks = group_rows // lanes
    grid = member.astype(BF).reshape(blocks, lanes)
    upper = (jnp.arange(lanes)[:, None] <= jnp.arange(lanes)[None, :]).astype(BF)
    within = multiply(grid, upper)
    lower = (jnp.arange(blocks)[:, None] > jnp.arange(blocks)[None, :]).astype(BF)
    before = multiply(lower, within[:, lanes - 1 :].astype(BF))
    slot = (within + before).astype(jnp.int32).reshape(-1) - 1
    slot = jnp.where(member, slot, -1)
    select = (slot[None, :] == jnp.arange(slot_total, dtype=jnp.int32)[:, None]).astype(BF)

    is_mine = labels[None, :] == mine
    own_parts = jnp.sum(
        jnp.where(
            is_mine[:, None, :], tree_probs[:, : 3 * experts].reshape(group_rows, 3, experts), 0
        ).astype(F32),
        axis=-1,
    )
    row_gate = jnp.sum(own_parts, axis=-1)
    slot_gate = jnp.sum(multiply(select, own_parts.astype(BF)), axis=-1)

    e_rows = multiply(select, tree_rows).astype(BF)
    e_raw = multiply(select, tree_grads).astype(BF)
    e_grads = (slot_gate[:, None] * e_raw.astype(F32)).astype(BF)

    def into(rows, pieces):
        total = multiply(rows[:, :part], pieces[0])
        for k in range(1, nf):
            total = total + multiply(rows[:, k * part : (k + 1) * part], pieces[k])
        return total

    def feed_forward(rows, grads, gate, up, down):
        gate_pre, up_pre = into(rows, gate), into(rows, up)
        sigmoid_gate = jax.nn.sigmoid(gate_pre)
        activated = gate_pre * sigmoid_gate
        hidden_act = (activated * up_pre).astype(BF)
        inner_grad = into(grads, down)
        gate_grad = (
            inner_grad * up_pre * sigmoid_gate * (1.0 + gate_pre * (1.0 - sigmoid_gate))
        ).astype(BF)
        up_grad = (inner_grad * activated).astype(BF)
        return hidden_act, gate_grad, up_grad

    def weight_grads(rows, grads, hidden_act, gate_grad, up_grad):
        def one(k):
            cut = slice(k * part, (k + 1) * part)
            return (
                transposed_multiply(rows[:, cut], gate_grad),
                transposed_multiply(rows[:, cut], up_grad),
                transposed_multiply(grads[:, cut], hidden_act),
            )

        return one

    s_gate = [w[:, :fs] for w in s_all]
    s_up = [w[:, fs : 2 * fs] for w in s_all]
    s_down = [w[:, 2 * fs :] for w in s_all]

    e_hidden, e_gg, e_ug = feed_forward(e_rows, e_grads, e_gate, e_up, e_down)
    s_hidden, s_gg, s_ug = feed_forward(tree_rows, tree_grads, s_gate, s_up, s_down)

    back_parts, out_parts, slot_delta = [], [], 0.0
    for k in range(nf):
        cut = slice(k * part, (k + 1) * part)
        e_back = (multiply_transposed(e_gg, e_gate[k]) + multiply_transposed(e_ug, e_up[k])).astype(BF)
        s_back = multiply_transposed(s_gg, s_gate[k]) + multiply_transposed(s_ug, s_up[k])
        back_parts.append((transposed_multiply(select, e_back) + s_back).astype(BF))
        e_out = multiply_transposed(e_hidden, e_down[k]).astype(BF)
        slot_delta = slot_delta + jnp.sum(
            e_raw[:, cut].astype(F32) * e_out.astype(F32), axis=-1
        )
        s_out = multiply_transposed(s_hidden, s_down[k])
        out_parts.append((row_gate[:, None] * transposed_multiply(select, e_out) + s_out).astype(BF))
    delta_parts = jnp.stack(three_parts(slot_delta), axis=-1)
    row_delta = transposed_multiply(select, delta_parts).astype(BF)
    delta_out = jnp.where(is_mine[:, None, :], row_delta[:, :, None], 0).reshape(group_rows, 3 * experts)
    delta_out = jnp.pad(delta_out, ((0, 0), (0, 128 - 3 * experts)))

    def by_owner(x):
        return x.reshape(trees, nc, tok_loc, x.shape[-1])

    sums = ring_reduce(
        ring, 3, [by_owner(x) for x in back_parts] + [by_owner(delta_out)], [False] * (nf + 1)
    )
    back_sum = roll_out(jnp.concatenate(sums[:nf], axis=-1).reshape(row_total, D))
    prob_delta = jnp.sum(
        sums[nf].reshape(row_total, 128)[:, : 3 * experts].reshape(row_total, 3, experts), axis=1
    )
    out_sum = lax.psum_scatter(
        jnp.concatenate(out_parts, axis=-1).reshape(trees, tree_len, D),
        "ctx",
        scatter_dimension=1,
        tiled=True,
    )
    out_sum = roll_out(out_sum.reshape(row_total, D).astype(F32))
    output = (residual + out_sum).astype(BF).reshape(trees, tok_loc, D)

    e_one = weight_grads(e_rows, e_grads, e_hidden, e_gg, e_ug)
    s_one = weight_grads(tree_rows, tree_grads, s_hidden, s_gg, s_ug)
    e_came, s_came = [], []
    for k in range(1, nf):
        perm = [(i, (i + k) % nf) for i in range(nf)]
        e_came.append([lax.ppermute(g.astype(BF), "fsdp", perm) for g in e_one(k)])
        s_came.append(
            lax.ppermute(jnp.concatenate(s_one(k), axis=1).astype(BF), "fsdp", perm)
        )
    e_sums, s_sum = list(e_one(0)), jnp.concatenate(s_one(0), axis=1)
    for k in range(nf - 1):
        e_sums = [a + b.astype(F32) for a, b in zip(e_sums, e_came[k])]
        s_sum = s_sum + s_came[k].astype(F32)
    s_sums = [s_sum[:, :fs], s_sum[:, fs : 2 * fs], s_sum[:, 2 * fs :]]

    logit_grad = (
        expert_probs * (prob_delta - jnp.sum(expert_probs * prob_delta, axis=-1, keepdims=True))
    ).astype(BF)
    grad_router = transposed_multiply(hidden_mid, logit_grad)
    mid_grad = back_sum + multiply_transposed(logit_grad, w_router)
    mid_input, grad_gain_ffn = normalize_back(mid_grad, normed_mid, inverse_mid, gain_ffn)
    residual_grad = upstream + mid_input
    residual_low = residual_grad.astype(BF)
    grad_output = transposed_multiply(heads, residual_low).astype(BF)
    out_total = lax.psum_scatter(grad_output, both, scatter_dimension=0, tiled=True).astype(F32)
    heads_grad = (
        multiply_transposed(residual_low, w_output).astype(BF).reshape(trees, tok_loc, H, DV)
    )
    mixed_grad = jnp.einsum(
        "bthv,chv->bthc", heads_grad, expand_value, preferred_element_type=F32
    ).astype(BF)
    mixed_grad_flat = mixed_grad.reshape(trees, tok_loc * H, LAT)
    scores = attention_scores()
    weights_full = jnp.exp(scores - log_total)
    prob_grad = jnp.einsum(
        "bqc,bjc->bqj", mixed_grad_flat, keys_latent, preferred_element_type=F32
    )
    score_grad = (
        weights_full * (prob_grad - jnp.sum(weights_full * prob_grad, axis=-1, keepdims=True))
    ).astype(BF)
    keys_grad = (
        jnp.einsum("bqj,bqc->bjc", score_grad, query_cat, preferred_element_type=F32) * score_scale
    )
    latent_part = jnp.einsum(
        "bqj,bqc->bjc", weights_full.astype(BF), mixed_grad_flat, preferred_element_type=F32
    )
    keys_grad = jnp.concatenate(
        [keys_grad[..., :LAT] + latent_part, keys_grad[..., LAT:]], axis=-1
    ).astype(BF)
    (own_keys_grad,) = ring_reduce(
        ring, 4, [keys_grad.reshape(trees, nc, tok_loc, LAT + DR)], [False]
    )
    query_cat_grad = (
        jnp.einsum("bqj,bjc->bqc", score_grad, keys, preferred_element_type=F32) * score_scale
    ).reshape(trees, tok_loc, H, LAT + DR)
    qlat_grad = query_cat_grad[..., :LAT].astype(BF)
    qrope_grad = query_cat_grad[..., LAT:]
    qnope_grad = jnp.einsum("bthc,chn->bthn", qlat_grad, expand_key, preferred_element_type=F32)
    grad_key = jnp.einsum("bthc,bthn->chn", qlat_grad, query_nope, preferred_element_type=F32)
    grad_value = jnp.einsum("bthc,bthv->chv", mixed, heads_grad, preferred_element_type=F32)
    grad_expand = jnp.concatenate([grad_key, grad_value], axis=-1).reshape(LAT, H * (DN + DV))
    query_grad = jnp.concatenate(
        [qnope_grad, rotate(qrope_grad, cosine[:, :, None, :], -sine[:, :, None, :])], axis=-1
    )
    query_grad = query_grad.astype(BF).reshape(row_total, H * (DN + DR))
    grad_query = transposed_multiply(hidden_in, query_grad)
    hidden_grad = multiply_transposed(query_grad, w_query)
    latent_in_grad, grad_gain_latent = normalize_back(
        own_keys_grad[..., :LAT].reshape(row_total, LAT), latent_normed, latent_inverse, gain_latent
    )
    rope_back = rotate(own_keys_grad[..., LAT:], cosine, -sine).reshape(row_total, DR)
    latent_grad = jnp.concatenate([latent_in_grad, rope_back], axis=-1).astype(BF)
    grad_latent = transposed_multiply(hidden_in, latent_grad)
    hidden_grad = hidden_grad + multiply_transposed(latent_grad, w_latent)
    input_part, grad_gain_attn = normalize_back(hidden_grad, normed_in, inverse_in, gain_attn)
    input_grad = (input_part + residual_grad).reshape(trees, tok_loc, D)

    grad_small = jnp.concatenate(
        [
            grad_gain_attn.reshape(nf * nc, r_one),
            grad_gain_ffn.reshape(nf * nc, r_one),
            grad_gain_latent.reshape(nf * nc, r_lat),
            grad_router.reshape(nf * nc, r_router),
        ],
        axis=1,
    ).astype(BF)
    grad_small = jnp.pad(grad_small, ((0, 0), (0, PACK - grad_small.shape[1])))
    parts = [
        grad_query.astype(BF).reshape(nf, nc, -1, w_query.shape[1]),
        grad_expand.astype(BF).reshape(nf, nc, -1, w_expand.shape[1]),
        grad_latent.astype(BF).reshape(nf, nc, -1, w_latent.shape[1]),
        grad_small.reshape(nf, nc, 16, PACK // 16),
    ]
    if nf == 2:
        t_query, t_expand, t_latent, t_small = ring_reduce(ring, 5, parts, [True] * 4)
    else:
        t_query, t_expand, t_latent, t_small = (
            lax.psum_scatter(
                x.reshape((nf * nc,) + x.shape[2:]), both, scatter_dimension=0, tiled=True
            )[0].astype(F32)
            for x in parts
        )
    t_small = t_small.reshape(PACK)
    return (
        output,
        input_grad,
        t_small[cuts[0] : cuts[1]],
        t_query,
        t_latent,
        t_small[cuts[2] : cuts[3]],
        t_expand,
        out_total,
        t_small[cuts[1] : cuts[2]],
        t_small[cuts[3] : cuts[4]].reshape(-1, experts),
        *e_sums,
        *s_sums,
    )


def solution(mesh):
    placed = (
        P("fsdp", "ctx", None),
        P("fsdp", "ctx", None),
        P("fsdp", None),
        P("fsdp", None, None),
        P("fsdp", "ctx", None),
        P(("fsdp", "ctx")),
        P(("fsdp", "ctx"), None),
        P(("fsdp", "ctx"), None),
        P(("fsdp", "ctx")),
        P(("fsdp", "ctx"), None),
        P(("fsdp", "ctx"), None),
        P(("fsdp", "ctx")),
        P(("fsdp", "ctx"), None),
        P("fsdp", "ctx"),
        P("fsdp", "ctx"),
        P("fsdp", "ctx"),
        P("fsdp", "ctx"),
        P("fsdp", "ctx"),
        P("fsdp", "ctx"),
    )
    return jax.shard_map(
        body,
        mesh=mesh,
        in_specs=placed,
        out_specs=(
            P("fsdp", "ctx", None),
            P("fsdp", "ctx", None),
            P(("fsdp", "ctx")),
            P(("fsdp", "ctx"), None),
            P(("fsdp", "ctx"), None),
            P(("fsdp", "ctx")),
            P(("fsdp", "ctx"), None),
            P(("fsdp", "ctx"), None),
            P(("fsdp", "ctx")),
            P(("fsdp", "ctx"), None),
            P("fsdp", "ctx"),
            P("fsdp", "ctx"),
            P("fsdp", "ctx"),
            P("fsdp", "ctx"),
            P("fsdp", "ctx"),
            P("fsdp", "ctx"),
        ),
        check_vma=False,
    )
```

```python
import functools
import math

import jax
import jax.numpy as jnp
from jax import lax
from jax.experimental import pallas as pl
from jax.experimental.pallas import tpu as pltpu
from jax.sharding import PartitionSpec as P

D = 2048
H = 16
DN = 128
DR = 64
DV = 128
LAT = 512
TOP = 6
SEGS = 13
PACK = 2048

MESH = pl.DeviceIdType.MESH
BF = jnp.bfloat16
F32 = jnp.float32

epsilon = 1e-06
rope_base = 10000.0


def multiply(left, right):
    return jnp.dot(left, right, preferred_element_type=F32)


def multiply_transposed(left, right):
    return lax.dot_general(left, right, (((1,), (1,)), ((), ())), preferred_element_type=F32)


def transposed_multiply(left, right):
    return lax.dot_general(left, right, (((0,), (0,)), ((), ())), preferred_element_type=F32)


def normalize(tensor_in, gain_vec):
    inverse = lax.rsqrt(jnp.mean(tensor_in * tensor_in, axis=-1, keepdims=True) + epsilon)
    normed = tensor_in * inverse
    return (normed, inverse, normed * gain_vec)


def normalize_back(grad_out, normed, inverse, gain_vec):
    weighted = grad_out * gain_vec
    centre = jnp.mean(weighted * normed, axis=-1, keepdims=True)
    return (inverse * (weighted - normed * centre), jnp.sum(grad_out * normed, axis=0))


def rotate(tensor_in, cosine, sine):
    half_width = tensor_in.shape[-1] // 2
    former = tensor_in[..., :half_width]
    latter = tensor_in[..., half_width:]
    return jnp.concatenate(
        [former * cosine - latter * sine, latter * cosine + former * sine], axis=-1
    )


def tree_mask(segment_ids, path_table, first_row, row_count):
    labels = jnp.arange(SEGS, dtype=jnp.int32)
    own_ids = lax.dynamic_slice_in_dim(segment_ids, first_row, row_count)
    own_hot = (own_ids[:, None] == labels[None, :]).astype(BF)
    all_hot = (segment_ids[:, None] == labels[None, :]).astype(BF)
    ancestry = multiply(own_hot, path_table.astype(BF)).astype(BF)
    related = multiply_transposed(ancestry, all_hot)
    places = jnp.arange(segment_ids.shape[0], dtype=jnp.int32)
    queries = first_row + jnp.arange(row_count, dtype=jnp.int32)
    allowed = (related > 0) & (places[None, :] <= queries[:, None])
    positions = jnp.sum(allowed.astype(jnp.int32), axis=1) - 1
    return (allowed, positions)


def three_parts(value):
    first = lax.reduce_precision(value, 8, 7)
    second = lax.reduce_precision(value - first, 8, 7)
    third = value - first - second
    return (first.astype(BF), second.astype(BF), third.astype(BF))


class Ring:
    def __init__(self, nf, nc):
        self.nf, self.chips = nf, nc // 2
        half = self.chips // 2
        if nf == 2:
            self.place = lambda p: (1 - p // half) * 2 * p + (p // half) * (4 * half - 1 - 2 * p)
            self.where = lambda j: (1 - j % 2) * (j // 2) + (j % 2) * (2 * half - 1 - j // 2)
        else:
            self.place = lambda p: (1 - p // half) * p + (p // half) * (3 * half - 1 - p)
            self.where = self.place

    def here(self):
        f, c = lax.axis_index("fsdp"), lax.axis_index("ctx")
        core = c % 2
        return f, c, core, self.where(c // 2), 1 - 2 * core

    def device(self, position, core):
        return self.place((position + 2 * self.chips) % self.chips) * 2 + core


def greet(ring, f, c, core, p, way, over_fsdp):
    barrier = pltpu.get_barrier_semaphore()
    targets = [(f, ring.device(p - way, core)), (f, c + 1 - 2 * core)]
    if over_fsdp:
        targets += [((f + k) % ring.nf, c) for k in range(1, ring.nf)]
    for target in targets:
        pl.semaphore_signal(barrier, inc=1, device_id=target, device_id_type=MESH)
    pl.semaphore_wait(barrier, len(targets))


def gather_kernel(ring, wide, leads, count, swaps, *refs):
    swap_ins, swap_outs = refs[count : count + swaps], refs[2 * count + swaps : 2 * (count + swaps)]
    ins, outs = refs[:count], refs[count + swaps : 2 * count + swaps]
    own_sem, yss, yrs, rss, rrs, sss, srs, wss, wrs = refs[2 * (count + swaps) :]
    f, c, core, p, way = ring.here()
    n, nf = ring.chips, ring.nf
    greet(ring, f, c, core, p, way, any(wide))
    to_next = (f, ring.device(p + way, core))
    to_twin = (f, c + 1 - 2 * core)
    started, own = [], []

    def remote(src, dst, ss, rs, dev):
        return pltpu.make_async_remote_copy(
            src_ref=src, dst_ref=dst, send_sem=ss, recv_sem=rs, device_id=dev, device_id_type=MESH
        )

    streams, late = [], []
    number = 0
    for i in range(count):
        if wide[i]:
            streams.append((number, i, f, ins[i]))
            number += 1
        else:
            for a in range(leads[i]):
                streams.append((number, i, a, ins[i].at[a]))
                number += 1
    first = len(streams)
    yn = 0
    for i in range(count):
        if wide[i]:
            for k in range(1, nf):
                late.append((number, i, (f - k + nf) % nf, k, yn))
                number += 1
                yn += 1

    def send_ring(s, number, i, lead, owner, src):
        cp = remote(src, outs[i].at[lead, owner], rss.at[s, number], rrs.at[s, number], to_next)
        cp.start()
        started.append(cp)

    def send_twin(s, number, i, lead, owner, src):
        cp = remote(src, outs[i].at[lead, owner], sss.at[s, number], srs.at[s, number], to_twin)
        cp.start()
        started.append(cp)

    for number, i, lead, k, y in late:
        cp = remote(ins[i], outs[i].at[f, c], yss.at[y], yrs.at[y], ((f + k) % nf, c))
        cp.start()
        started.append(cp)
    for number, i, lead, src in streams:
        send_ring(0, number, i, lead, c, src)
    for number, i, lead, src in streams:
        send_twin(0, number, i, lead, c, src)
        cp = pltpu.make_async_copy(src, outs[i].at[lead, c], own_sem.at[number])
        cp.start()
        own.append(cp)
    everything = [(number, i, lead) for number, i, lead, _ in streams]
    everything += [(number, i, lead) for number, i, lead, _, _ in late]
    for number, i, lead, k, y in late:
        here = outs[i].at[lead, c]
        remote(here, here, yss.at[y], yrs.at[y], to_next).wait_recv()
        send_ring(0, number, i, lead, c, here)
        send_twin(0, number, i, lead, c, here)
    swapped = []
    for i in range(swaps):
        cp = remote(swap_ins[i], swap_outs[i], wss.at[i], wrs.at[i], ((f + 1) % nf, c))
        cp.start()
        swapped.append(cp)
    for s in range(1, n):
        owner = ring.device(p - way * s, core)
        for number, i, lead in everything:
            here = outs[i].at[lead, owner]
            remote(here, here, rss.at[s - 1, number], rrs.at[s - 1, number], to_next).wait_recv()
            if s < n - 1:
                send_ring(s, number, i, lead, owner, here)
            send_twin(s, number, i, lead, owner, here)
    for s in range(n):
        owner = ring.device(p + way * s, 1 - core)
        for number, i, lead in everything:
            here = outs[i].at[lead, owner]
            remote(here, here, sss.at[s, number], srs.at[s, number], to_twin).wait_recv()
    for cp in own:
        cp.wait()
    for cp in started:
        cp.wait_send()
    for cp in swapped:
        cp.wait()


def ring_gather(ring, number, arrays, wide, swaps=()):
    n, nf = ring.chips, ring.nf
    leads = [1 if w else a.shape[0] for a, w in zip(arrays, wide)]
    shapes, streams, late, size = [], 0, 0, 0
    for a, w in zip(arrays, wide):
        if w:
            shapes.append(jax.ShapeDtypeStruct((nf, 2 * n) + a.shape, a.dtype))
            streams += nf
            late += nf - 1
        else:
            shapes.append(jax.ShapeDtypeStruct((a.shape[0], 2 * n) + a.shape[1:], a.dtype))
            streams += a.shape[0]
        size += shapes[-1].size * 2
    dma = pltpu.SemaphoreType.DMA
    shapes += [jax.ShapeDtypeStruct(a.shape, a.dtype) for a in swaps]
    return pl.pallas_call(
        functools.partial(
            gather_kernel, ring, tuple(wide), tuple(leads), len(arrays), len(swaps)
        ),
        out_shape=shapes,
        in_specs=[pl.BlockSpec(memory_space=pl.ANY)] * len(shapes),
        out_specs=[pl.BlockSpec(memory_space=pl.ANY)] * len(shapes),
        scratch_shapes=[
            dma((streams,)),
            dma((max(1, late),)),
            dma((max(1, late),)),
            dma((n - 1, streams)),
            dma((n - 1, streams)),
            dma((n, streams)),
            dma((n, streams)),
            dma((max(1, len(swaps)),)),
            dma((max(1, len(swaps)),)),
        ],
        compiler_params=pltpu.CompilerParams(collective_id=number, has_side_effects=True),
        cost_estimate=pl.CostEstimate(flops=0, bytes_accessed=2 * size, transcendentals=0),
        name="ring_gather_%d" % number,
    )(*arrays, *swaps)


def add_rows(shape, work):
    rows = shape[0]
    step = 16 if rows % 16 == 0 else rows

    def one(r, carry):
        work(pl.ds(pl.multiple_of(r * step, step), step))
        return carry

    lax.fori_loop(0, rows // step, one, 0)


def reduce_kernel(ring, wide, leads, count, *refs):
    ins, outs = refs[:count], refs[count : 2 * count]
    own, twin, got = (refs[(2 + k) * count : (3 + k) * count] for k in range(3))
    refs = refs[5 * count :]
    wides = sum(wide)
    finals, ygots = refs[:wides], refs[wides : 2 * wides]
    own_sem, tss, trs, rss, rrs, yss, yrs = refs[2 * wides :]
    f, c, core, p, way = ring.here()
    n, nf = ring.chips, ring.nf
    greet(ring, f, c, core, p, way, any(wide))
    to_next = (f, ring.device(p + way, core))
    to_twin = (f, c + 1 - 2 * core)

    def remote(src, dst, ss, rs, dev):
        return pltpu.make_async_remote_copy(
            src_ref=src, dst_ref=dst, send_sem=ss, recv_sem=rs, device_id=dev, device_id_type=MESH
        )

    streams = []
    for k in range(max(leads)):
        for i in range(count):
            if k < leads[i]:
                lead = (f + 1 + k) % nf if wide[i] else k
                streams.append((len(streams), i, k, lead))
    started, loads = [], {}
    for s in range(n):
        theirs = ring.device(p + way * (1 + s), 1 - core)
        mine = ring.device(p - way * (1 + s), core)
        for number, i, k, lead in streams:
            cp = remote(
                ins[i].at[lead, theirs], twin[i].at[s, k], tss.at[s, number], trs.at[s, number], to_twin
            )
            cp.start()
            started.append(cp)
            cp = pltpu.make_async_copy(
                ins[i].at[lead, mine], own[i].at[s, k], own_sem.at[s, number]
            )
            cp.start()
            loads[s, number] = cp

    def wait_parts(s, number, i, k):
        loads[s, number].wait()
        here = twin[i].at[s, k]
        remote(here, here, tss.at[s, number], trs.at[s, number], to_twin).wait_recv()

    def pass_on(s, number, i, k, src):
        cp = remote(src, got[i].at[s, k], rss.at[s, number], rrs.at[s, number], to_next)
        cp.start()
        started.append(cp)

    for s in range(n):
        for number, i, k, lead in streams:
            wait_parts(s, number, i, k)
            mine, other = own[i].at[s, k], twin[i].at[s, k]
            if s == 0:

                def start(rows, mine=mine, other=other):
                    mine[rows, :] = (mine[rows, :].astype(F32) + other[rows, :].astype(F32)).astype(BF)

                add_rows(mine.shape, start)
                pass_on(0, number, i, k, mine)
                continue
            came = got[i].at[s - 1, k]
            remote(came, came, rss.at[s - 1, number], rrs.at[s - 1, number], to_next).wait_recv()
            if s < n - 1:

                def middle(rows, mine=mine, other=other, came=came):
                    total = mine[rows, :].astype(F32) + other[rows, :].astype(F32)
                    came[rows, :] = (came[rows, :].astype(F32) + total).astype(BF)

                add_rows(mine.shape, middle)
                pass_on(s, number, i, k, came)
                continue
            if not wide[i]:
                target = outs[i].at[k]
            elif k == nf - 1:
                target = outs[i]
            else:
                target = finals[sum(wide[:i])].at[k]

            def last(rows, mine=mine, other=other, came=came, target=target):
                total = mine[rows, :].astype(F32) + other[rows, :].astype(F32)
                target[rows, :] = (came[rows, :].astype(F32) + total).astype(target.dtype)

            add_rows(mine.shape, last)
            if wide[i] and k < nf - 1:
                w = sum(wide[:i])
                cp = remote(target, ygots[w].at[k], yss.at[w, k], yrs.at[w, k], ((f + 1 + k) % nf, c))
                cp.start()
                started.append(cp)
    for i in range(count):
        if wide[i]:
            w = sum(wide[:i])
            for k in range(nf - 1):
                here = ygots[w].at[k]
                remote(here, here, yss.at[w, k], yrs.at[w, k], to_next).wait_recv()

                def finish(rows, here=here, target=outs[i]):
                    target[rows, :] = target[rows, :] + here[rows, :].astype(F32)

                add_rows(here.shape, finish)
    for cp in started:
        cp.wait_send()


def ring_reduce(ring, number, arrays, wide):
    n, nf = ring.chips, ring.nf
    leads = [a.shape[0] for a in arrays]
    streams = sum(leads)
    block = [a.shape[2:] for a in arrays]
    shapes = [
        jax.ShapeDtypeStruct(b if w else (l,) + b, F32) for b, w, l in zip(block, wide, leads)
    ]
    dma = pltpu.SemaphoreType.DMA
    scratch = [pltpu.VMEM((n, l) + b, BF) for b, l in zip(block, leads)] * 2
    scratch += [pltpu.VMEM((n - 1, l) + b, BF) for b, l in zip(block, leads)]
    scratch += [pltpu.VMEM((nf - 1,) + b, BF) for b, w in zip(block, wide) if w] * 2
    wides = max(1, sum(wide))
    size = sum(a.size * 2 for a in arrays)
    return pl.pallas_call(
        functools.partial(reduce_kernel, ring, tuple(wide), tuple(leads), len(arrays)),
        out_shape=shapes,
        in_specs=[pl.BlockSpec(memory_space=pl.ANY)] * len(arrays),
        out_specs=[pl.BlockSpec(memory_space=pltpu.VMEM)] * len(arrays),
        scratch_shapes=scratch
        + [
            dma((n, streams)),
            dma((n, streams)),
            dma((n, streams)),
            dma((n - 1, streams)),
            dma((n - 1, streams)),
            dma((wides, max(1, nf - 1))),
            dma((wides, max(1, nf - 1))),
        ],
        compiler_params=pltpu.CompilerParams(
            collective_id=number, has_side_effects=True, vmem_limit_bytes=56 << 20
        ),
        cost_estimate=pl.CostEstimate(flops=0, bytes_accessed=2 * size, transcendentals=0),
        name="ring_reduce_%d" % number,
    )(*arrays)


def body(
    tokens,
    out_grad,
    segments,
    path_mask,
    expert_ids,
    norm_attn,
    attn_q,
    attn_kva,
    norm_latent,
    attn_kvb,
    attn_out,
    norm_ffn,
    router,
    expert_gate,
    expert_up,
    expert_down,
    shared_gate,
    shared_up,
    shared_down,
):
    trees, tok_loc = tokens.shape[:2]
    row_total = trees * tok_loc
    nc, nf = lax.axis_size("ctx"), lax.axis_size("fsdp")
    mine, group = lax.axis_index("ctx"), lax.axis_index("fsdp")
    experts = nc
    ring = Ring(nf, nc)
    tree_len = tok_loc * nc
    group_rows = trees * tree_len
    first_row = mine * tok_loc
    capacity = min(tok_loc, tok_loc * TOP * 4 // (3 * experts))
    slot_total = nc * trees * capacity
    score_scale = 1.0 / math.sqrt(DN + DR)
    frequency = rope_base ** (-(jnp.arange(DR // 2, dtype=F32) * 2.0 / DR))
    labels = jnp.arange(experts, dtype=jnp.int32)
    both = ("fsdp", "ctx")
    part = D // nf

    def roll_in(x):
        return lax.dynamic_slice_in_dim(jnp.concatenate([x, x], axis=-1), group * part, D, x.ndim - 1)

    def roll_out(x):
        return lax.dynamic_slice_in_dim(
            jnp.concatenate([x, x], axis=-1), (nf - group) % nf * part, D, x.ndim - 1
        )

    def fetch(w):
        pieces = [w]
        for k in range(1, nf):
            pieces.append(lax.ppermute(w, "fsdp", [(i, (i - k) % nf) for i in range(nf)]))
        return pieces

    shared_w = jnp.concatenate([shared_gate, shared_up, shared_down], axis=1)
    fs = shared_gate.shape[1]
    small = jnp.concatenate(
        [
            norm_attn,
            norm_ffn,
            norm_latent,
            router.reshape(-1),
            expert_ids.astype(BF).reshape(-1),
        ]
    )
    small = jnp.pad(small, (0, PACK - small.shape[0])).reshape(16, PACK // 16)
    if nf == 2:
        w_latent, w_query, w_expand, small_all, w_output, other_gate, other_shared = ring_gather(
            ring, 0, [attn_kva, attn_q, attn_kvb, small, attn_out], [True] * 5, [expert_gate, shared_w]
        )
        e_gate, s_all = [expert_gate, other_gate], [shared_w, other_shared]
        later_up, later_down, later_grads, small_all = lax.optimization_barrier(
            (expert_up, expert_down, out_grad, small_all)
        )
    else:
        w_latent, w_query, w_expand, small_all, w_output = (
            lax.all_gather(w, both, axis=0) for w in (attn_kva, attn_q, attn_kvb, small, attn_out)
        )
        e_gate, s_all = fetch(expert_gate), fetch(shared_w)
        later_up, later_down, later_grads = expert_up, expert_down, out_grad
    e_up, e_down = fetch(later_up), fetch(later_down)
    w_output = w_output.reshape(H * DV, D)
    w_latent, w_query = w_latent.reshape(D, -1), w_query.reshape(D, -1)
    w_expand = w_expand.reshape(LAT, -1)
    small_all = small_all.reshape(nf * nc, PACK)
    r_one, r_lat, r_router = norm_attn.shape[0], norm_latent.shape[0], router.size
    cuts = [0, r_one, 2 * r_one, 2 * r_one + r_lat, 2 * r_one + r_lat + r_router]
    gain_attn = small_all[:, cuts[0] : cuts[1]].reshape(-1).astype(F32)
    gain_ffn = small_all[:, cuts[1] : cuts[2]].reshape(-1).astype(F32)
    gain_latent = small_all[:, cuts[2] : cuts[3]].reshape(-1).astype(F32)
    w_router = small_all[:, cuts[3] : cuts[4]].reshape(D, experts)
    ids_all = lax.dynamic_slice_in_dim(small_all.reshape(nf, nc, PACK), group, 1, 0)[0]
    ids_all = ids_all[:, cuts[4] : cuts[4] + expert_ids.size].reshape(nc, trees, tok_loc, TOP)
    ids_all = ids_all.transpose(1, 0, 2, 3).reshape(group_rows, TOP)

    upstream_low = out_grad.reshape(row_total, D)
    upstream = upstream_low.astype(F32)
    tree_grads = lax.all_gather(roll_in(later_grads), "ctx", axis=1, tiled=True).reshape(group_rows, D)

    def one_mask(segment_ids, path_table):
        return tree_mask(segment_ids, path_table, first_row, tok_loc)

    allowed, positions = jax.vmap(one_mask)(segments, path_mask)
    rotation = positions.astype(F32)[:, :, None] * frequency[None, None, :]
    cosine, sine = jnp.cos(rotation), jnp.sin(rotation)
    inputs = tokens.astype(F32).reshape(row_total, D)
    normed_in, inverse_in, gained_in = normalize(inputs, gain_attn)
    hidden_in = gained_in.astype(BF)
    latent_all = multiply(hidden_in, w_latent)
    latent_normed, latent_inverse, latent_gained = normalize(latent_all[:, :LAT], gain_latent)
    key_latent = latent_gained.astype(BF).reshape(trees, tok_loc, LAT)
    key_rope = rotate(latent_all[:, LAT:].reshape(trees, tok_loc, DR), cosine, sine).astype(BF)
    (keys,) = ring_gather(
        ring, 1, [jnp.concatenate([key_latent, key_rope], axis=-1)], [False]
    )
    keys = keys.reshape(trees, tree_len, LAT + DR)
    keys_latent = keys[:, :, :LAT]
    query_all = lax.optimization_barrier(multiply(hidden_in, w_query))
    query_all = query_all.reshape(trees, tok_loc, H, DN + DR)
    query_nope = query_all[..., :DN].astype(BF)
    query_rope = rotate(
        query_all[..., DN:], cosine[:, :, None, :], sine[:, :, None, :]
    ).astype(BF)
    expand = w_expand.reshape(LAT, H, DN + DV)
    expand_key = expand[..., :DN]
    expand_value = expand[..., DN:]
    query_latent = jnp.einsum(
        "bthn,chn->bthc", query_nope, expand_key, preferred_element_type=F32
    ).astype(BF)
    query_cat = jnp.concatenate([query_latent, query_rope], axis=-1).reshape(
        trees, tok_loc * H, LAT + DR
    )

    def attention_scores():
        raw_scores = jnp.einsum("bqc,bjc->bqj", query_cat, keys, preferred_element_type=F32)
        raw_scores = raw_scores.reshape(trees, tok_loc, H, tree_len)
        scores = jnp.where(allowed[:, :, None, :], raw_scores * score_scale, -1e30)
        return scores.reshape(trees, tok_loc * H, tree_len)

    scores = attention_scores()
    highest = jnp.max(scores, axis=-1, keepdims=True)
    exp_total = jnp.sum(jnp.exp(scores - highest), axis=-1, keepdims=True)
    log_total = highest + jnp.log(exp_total)
    weights_low = jnp.exp(scores - log_total).astype(BF)
    mixed = jnp.einsum("bqj,bjc->bqc", weights_low, keys_latent, preferred_element_type=F32)
    mixed = mixed.astype(BF).reshape(trees, tok_loc, H, LAT)
    heads = (
        jnp.einsum("bthc,chv->bthv", mixed, expand_value, preferred_element_type=F32)
        .astype(BF)
        .reshape(row_total, H * DV)
    )
    residual = inputs + multiply(heads, w_output)
    normed_mid, inverse_mid, gained_mid = normalize(residual, gain_ffn)
    hidden_mid = gained_mid.astype(BF)
    expert_probs = jax.nn.softmax(multiply(hidden_mid, w_router), axis=-1)

    probs_parts = jnp.concatenate(three_parts(expert_probs), axis=-1)
    probs_parts = jnp.pad(probs_parts, ((0, 0), (0, 128 - 3 * experts)))
    tree_rows, tree_probs = ring_gather(
        ring,
        2,
        [roll_in(hidden_mid).reshape(trees, tok_loc, D), probs_parts.reshape(trees, tok_loc, 128)],
        [False, False],
    )
    tree_rows = tree_rows.reshape(group_rows, D)
    tree_probs = tree_probs.reshape(group_rows, 128)

    member = jnp.any(ids_all == mine.astype(BF), axis=1)
    blocks = trees * nc
    bundle = 4 if blocks % 4 == 0 else 1
    bundles = blocks // bundle
    grid = member.astype(BF).reshape(blocks, tok_loc)
    upper = (jnp.arange(tok_loc)[:, None] <= jnp.arange(tok_loc)[None, :]).astype(BF)
    slot = multiply(grid, upper).astype(jnp.int32) - 1
    slot = slot + (jnp.arange(blocks, dtype=jnp.int32) % bundle * capacity)[:, None]
    slot = jnp.where(grid > 0, slot, -1).reshape(bundles, bundle * tok_loc)
    spots = jnp.arange(bundle * capacity, dtype=jnp.int32)
    select = (slot[:, None, :] == spots[None, :, None]).astype(BF)

    def take(x):
        x = x.reshape(bundles, bundle * tok_loc, x.shape[-1])
        y = jnp.einsum("gst,gtd->gsd", select, x, preferred_element_type=F32)
        return y.reshape(slot_total, x.shape[-1])

    def put(x):
        x = x.reshape(bundles, bundle * capacity, x.shape[-1])
        y = jnp.einsum("gst,gsd->gtd", select, x, preferred_element_type=F32)
        return y.reshape(group_rows, x.shape[-1])

    is_mine = labels[None, :] == mine
    own_parts = jnp.sum(
        jnp.where(
            is_mine[:, None, :], tree_probs[:, : 3 * experts].reshape(group_rows, 3, experts), 0
        ).astype(F32),
        axis=-1,
    )
    row_gate = jnp.sum(own_parts, axis=-1)
    slot_gate = jnp.sum(take(own_parts.astype(BF)), axis=-1)

    e_rows = take(tree_rows).astype(BF)
    e_raw = take(tree_grads).astype(BF)
    e_grads = (slot_gate[:, None] * e_raw.astype(F32)).astype(BF)

    def into(rows, pieces):
        total = multiply(rows[:, :part], pieces[0])
        for k in range(1, nf):
            total = total + multiply(rows[:, k * part : (k + 1) * part], pieces[k])
        return total

    def feed_forward(rows, grads, gate, up, down):
        gate_pre, up_pre = into(rows, gate), into(rows, up)
        sigmoid_gate = jax.nn.sigmoid(gate_pre)
        activated = gate_pre * sigmoid_gate
        hidden_act = (activated * up_pre).astype(BF)
        inner_grad = into(grads, down)
        gate_grad = (
            inner_grad * up_pre * sigmoid_gate * (1.0 + gate_pre * (1.0 - sigmoid_gate))
        ).astype(BF)
        up_grad = (inner_grad * activated).astype(BF)
        return hidden_act, gate_grad, up_grad

    def weight_grads(rows, grads, hidden_act, gate_grad, up_grad):
        def one(k):
            cut = slice(k * part, (k + 1) * part)
            return (
                transposed_multiply(rows[:, cut], gate_grad),
                transposed_multiply(rows[:, cut], up_grad),
                transposed_multiply(grads[:, cut], hidden_act),
            )

        return one

    s_gate = [w[:, :fs] for w in s_all]
    s_up = [w[:, fs : 2 * fs] for w in s_all]
    s_down = [w[:, 2 * fs :] for w in s_all]

    e_hidden, e_gg, e_ug = feed_forward(e_rows, e_grads, e_gate, e_up, e_down)
    s_hidden, s_gg, s_ug = feed_forward(tree_rows, tree_grads, s_gate, s_up, s_down)

    back_parts, out_parts, slot_delta = [], [], 0.0
    for k in range(nf):
        cut = slice(k * part, (k + 1) * part)
        e_back = (multiply_transposed(e_gg, e_gate[k]) + multiply_transposed(e_ug, e_up[k])).astype(BF)
        s_back = multiply_transposed(s_gg, s_gate[k]) + multiply_transposed(s_ug, s_up[k])
        back_parts.append((put(e_back) + s_back).astype(BF))
        e_out = multiply_transposed(e_hidden, e_down[k]).astype(BF)
        slot_delta = slot_delta + jnp.sum(
            e_raw[:, cut].astype(F32) * e_out.astype(F32), axis=-1
        )
        s_out = multiply_transposed(s_hidden, s_down[k])
        out_parts.append((row_gate[:, None] * put(e_out) + s_out).astype(BF))
    delta_parts = jnp.stack(three_parts(slot_delta), axis=-1)
    row_delta = put(delta_parts).astype(BF)
    delta_out = jnp.where(is_mine[:, None, :], row_delta[:, :, None], 0).reshape(group_rows, 3 * experts)
    delta_out = jnp.pad(delta_out, ((0, 0), (0, 128 - 3 * experts)))

    def by_owner(x):
        return x.reshape(trees, nc, tok_loc, x.shape[-1])

    sums = ring_reduce(
        ring, 3, [by_owner(x) for x in back_parts] + [by_owner(delta_out)], [False] * (nf + 1)
    )
    back_sum = roll_out(jnp.concatenate(sums[:nf], axis=-1).reshape(row_total, D))
    prob_delta = jnp.sum(
        sums[nf].reshape(row_total, 128)[:, : 3 * experts].reshape(row_total, 3, experts), axis=1
    )
    out_sum = [
        lax.psum_scatter(x.reshape(trees, tree_len, part), "ctx", scatter_dimension=1, tiled=True)
        for x in out_parts
    ]
    out_sum = jnp.concatenate(out_sum, axis=-1).reshape(row_total, D).astype(F32)
    out_sum = roll_out(out_sum)
    output = (residual + out_sum).astype(BF).reshape(trees, tok_loc, D)

    e_one = weight_grads(e_rows, e_grads, e_hidden, e_gg, e_ug)
    s_one = weight_grads(tree_rows, tree_grads, s_hidden, s_gg, s_ug)
    e_came, s_came = [], []
    for k in range(1, nf):
        perm = [(i, (i + k) % nf) for i in range(nf)]
        e_came.append([lax.ppermute(g.astype(BF), "fsdp", perm) for g in e_one(k)])
        s_came.append(
            lax.ppermute(jnp.concatenate(s_one(k), axis=1).astype(BF), "fsdp", perm)
        )
    logit_grad = (
        expert_probs * (prob_delta - jnp.sum(expert_probs * prob_delta, axis=-1, keepdims=True))
    ).astype(BF)
    grad_router = transposed_multiply(hidden_mid, logit_grad)
    mid_grad = back_sum + multiply_transposed(logit_grad, w_router)
    mid_input, grad_gain_ffn = normalize_back(mid_grad, normed_mid, inverse_mid, gain_ffn)
    residual_grad = upstream + mid_input
    residual_low = residual_grad.astype(BF)
    grad_output = transposed_multiply(heads, residual_low).astype(BF)
    out_total = lax.psum_scatter(grad_output, both, scatter_dimension=0, tiled=True).astype(F32)
    heads_grad = (
        multiply_transposed(residual_low, w_output).astype(BF).reshape(trees, tok_loc, H, DV)
    )
    mixed_grad = jnp.einsum(
        "bthv,chv->bthc", heads_grad, expand_value, preferred_element_type=F32
    ).astype(BF)
    mixed_grad_flat = mixed_grad.reshape(trees, tok_loc * H, LAT)
    scores = attention_scores()
    weights_full = jnp.exp(scores - log_total)
    prob_grad = jnp.einsum(
        "bqc,bjc->bqj", mixed_grad_flat, keys_latent, preferred_element_type=F32
    )
    score_grad = (
        weights_full * (prob_grad - jnp.sum(weights_full * prob_grad, axis=-1, keepdims=True))
    ).astype(BF)
    keys_grad = (
        jnp.einsum("bqj,bqc->bjc", score_grad, query_cat, preferred_element_type=F32) * score_scale
    )
    latent_part = jnp.einsum(
        "bqj,bqc->bjc", weights_full.astype(BF), mixed_grad_flat, preferred_element_type=F32
    )
    keys_grad = jnp.concatenate(
        [keys_grad[..., :LAT] + latent_part, keys_grad[..., LAT:]], axis=-1
    ).astype(BF)
    (own_keys_grad,) = ring_reduce(
        ring, 4, [keys_grad.reshape(trees, nc, tok_loc, LAT + DR)], [False]
    )
    query_cat_grad = (
        jnp.einsum("bqj,bjc->bqc", score_grad, keys, preferred_element_type=F32) * score_scale
    ).reshape(trees, tok_loc, H, LAT + DR)
    qlat_grad = query_cat_grad[..., :LAT].astype(BF)
    qrope_grad = query_cat_grad[..., LAT:]
    qnope_grad = jnp.einsum("bthc,chn->bthn", qlat_grad, expand_key, preferred_element_type=F32)
    grad_key = jnp.einsum("bthc,bthn->chn", qlat_grad, query_nope, preferred_element_type=F32)
    grad_value = jnp.einsum("bthc,bthv->chv", mixed, heads_grad, preferred_element_type=F32)
    grad_expand = jnp.concatenate([grad_key, grad_value], axis=-1).reshape(LAT, H * (DN + DV))
    query_grad = jnp.concatenate(
        [qnope_grad, rotate(qrope_grad, cosine[:, :, None, :], -sine[:, :, None, :])], axis=-1
    )
    query_grad = query_grad.astype(BF).reshape(row_total, H * (DN + DR))
    grad_query = transposed_multiply(hidden_in, query_grad)
    hidden_grad = multiply_transposed(query_grad, w_query)
    latent_in_grad, grad_gain_latent = normalize_back(
        own_keys_grad[..., :LAT].reshape(row_total, LAT), latent_normed, latent_inverse, gain_latent
    )
    rope_back = rotate(own_keys_grad[..., LAT:], cosine, -sine).reshape(row_total, DR)
    latent_grad = jnp.concatenate([latent_in_grad, rope_back], axis=-1).astype(BF)
    grad_latent = transposed_multiply(hidden_in, latent_grad)
    hidden_grad = hidden_grad + multiply_transposed(latent_grad, w_latent)
    input_part, grad_gain_attn = normalize_back(hidden_grad, normed_in, inverse_in, gain_attn)
    input_grad = (input_part + residual_grad).reshape(trees, tok_loc, D)

    grad_small = jnp.concatenate(
        [
            grad_gain_attn.reshape(nf * nc, r_one),
            grad_gain_ffn.reshape(nf * nc, r_one),
            grad_gain_latent.reshape(nf * nc, r_lat),
            grad_router.reshape(nf * nc, r_router),
        ],
        axis=1,
    ).astype(BF)
    grad_small = jnp.pad(grad_small, ((0, 0), (0, PACK - grad_small.shape[1])))
    parts = [
        grad_query.astype(BF).reshape(nf, nc, -1, w_query.shape[1]),
        grad_expand.astype(BF).reshape(nf, nc, -1, w_expand.shape[1]),
        grad_latent.astype(BF).reshape(nf, nc, -1, w_latent.shape[1]),
        grad_small.reshape(nf, nc, 16, PACK // 16),
    ]
    if nf == 2:
        t_query, t_expand, t_latent, t_small = ring_reduce(ring, 5, parts, [True] * 4)
    else:
        t_query, t_expand, t_latent, t_small = (
            lax.psum_scatter(
                x.reshape((nf * nc,) + x.shape[2:]), both, scatter_dimension=0, tiled=True
            )[0].astype(F32)
            for x in parts
        )
    t_small = t_small.reshape(PACK)
    t_small, e_came, s_came, e_gg, e_ug, e_hidden, s_gg, s_ug, s_hidden = lax.optimization_barrier(
        (t_small, e_came, s_came, e_gg, e_ug, e_hidden, s_gg, s_ug, s_hidden)
    )
    e_one = weight_grads(e_rows, e_grads, e_hidden, e_gg, e_ug)
    s_one = weight_grads(tree_rows, tree_grads, s_hidden, s_gg, s_ug)
    e_sums, s_sum = list(e_one(0)), jnp.concatenate(s_one(0), axis=1)
    for k in range(nf - 1):
        e_sums = [a + b.astype(F32) for a, b in zip(e_sums, e_came[k])]
        s_sum = s_sum + s_came[k].astype(F32)
    s_sums = [s_sum[:, :fs], s_sum[:, fs : 2 * fs], s_sum[:, 2 * fs :]]

    return (
        output,
        input_grad,
        t_small[cuts[0] : cuts[1]],
        t_query,
        t_latent,
        t_small[cuts[2] : cuts[3]],
        t_expand,
        out_total,
        t_small[cuts[1] : cuts[2]],
        t_small[cuts[3] : cuts[4]].reshape(-1, experts),
        *e_sums,
        *s_sums,
    )


def solution(mesh):
    placed = (
        P("fsdp", "ctx", None),
        P("fsdp", "ctx", None),
        P("fsdp", None),
        P("fsdp", None, None),
        P("fsdp", "ctx", None),
        P(("fsdp", "ctx")),
        P(("fsdp", "ctx"), None),
        P(("fsdp", "ctx"), None),
        P(("fsdp", "ctx")),
        P(("fsdp", "ctx"), None),
        P(("fsdp", "ctx"), None),
        P(("fsdp", "ctx")),
        P(("fsdp", "ctx"), None),
        P("fsdp", "ctx"),
        P("fsdp", "ctx"),
        P("fsdp", "ctx"),
        P("fsdp", "ctx"),
        P("fsdp", "ctx"),
        P("fsdp", "ctx"),
    )
    return jax.shard_map(
        body,
        mesh=mesh,
        in_specs=placed,
        out_specs=(
            P("fsdp", "ctx", None),
            P("fsdp", "ctx", None),
            P(("fsdp", "ctx")),
            P(("fsdp", "ctx"), None),
            P(("fsdp", "ctx"), None),
            P(("fsdp", "ctx")),
            P(("fsdp", "ctx"), None),
            P(("fsdp", "ctx"), None),
            P(("fsdp", "ctx")),
            P(("fsdp", "ctx"), None),
            P("fsdp", "ctx"),
            P("fsdp", "ctx"),
            P("fsdp", "ctx"),
            P("fsdp", "ctx"),
            P("fsdp", "ctx"),
            P("fsdp", "ctx"),
        ),
        check_vma=False,
    )
```

```python
import functools
import math

import jax
import jax.numpy as jnp
from jax import lax
from jax.experimental import pallas as pl
from jax.experimental.pallas import tpu as pltpu
from jax.sharding import PartitionSpec as P

D = 2048
H = 16
DN = 128
DR = 64
DV = 128
LAT = 512
TOP = 6
SEGS = 13
PACK = 2048

MESH = pl.DeviceIdType.MESH
BF = jnp.bfloat16
F32 = jnp.float32

epsilon = 1e-06
rope_base = 10000.0


def multiply(left, right):
    return jnp.dot(left, right, preferred_element_type=F32)


def multiply_transposed(left, right):
    return lax.dot_general(left, right, (((1,), (1,)), ((), ())), preferred_element_type=F32)


def transposed_multiply(left, right):
    return lax.dot_general(left, right, (((0,), (0,)), ((), ())), preferred_element_type=F32)


def normalize(tensor_in, gain_vec):
    inverse = lax.rsqrt(jnp.mean(tensor_in * tensor_in, axis=-1, keepdims=True) + epsilon)
    normed = tensor_in * inverse
    return (normed, inverse, normed * gain_vec)


def normalize_back(grad_out, normed, inverse, gain_vec):
    weighted = grad_out * gain_vec
    centre = jnp.mean(weighted * normed, axis=-1, keepdims=True)
    return (inverse * (weighted - normed * centre), jnp.sum(grad_out * normed, axis=0))


def rotate(tensor_in, cosine, sine):
    half_width = tensor_in.shape[-1] // 2
    former = tensor_in[..., :half_width]
    latter = tensor_in[..., half_width:]
    return jnp.concatenate(
        [former * cosine - latter * sine, latter * cosine + former * sine], axis=-1
    )


def tree_mask(segment_ids, path_table, first_row, row_count):
    labels = jnp.arange(SEGS, dtype=jnp.int32)
    own_ids = lax.dynamic_slice_in_dim(segment_ids, first_row, row_count)
    own_hot = (own_ids[:, None] == labels[None, :]).astype(BF)
    all_hot = (segment_ids[:, None] == labels[None, :]).astype(BF)
    ancestry = multiply(own_hot, path_table.astype(BF)).astype(BF)
    related = multiply_transposed(ancestry, all_hot)
    places = jnp.arange(segment_ids.shape[0], dtype=jnp.int32)
    queries = first_row + jnp.arange(row_count, dtype=jnp.int32)
    allowed = (related > 0) & (places[None, :] <= queries[:, None])
    positions = jnp.sum(allowed.astype(jnp.int32), axis=1) - 1
    return (allowed, positions)


def three_parts(value):
    first = lax.reduce_precision(value, 8, 7)
    second = lax.reduce_precision(value - first, 8, 7)
    third = value - first - second
    return (first.astype(BF), second.astype(BF), third.astype(BF))


class Ring:
    def __init__(self, nf, nc):
        self.nf, self.chips = nf, nc // 2
        half = self.chips // 2
        if nf == 2:
            self.place = lambda p: (1 - p // half) * 2 * p + (p // half) * (4 * half - 1 - 2 * p)
            self.where = lambda j: (1 - j % 2) * (j // 2) + (j % 2) * (2 * half - 1 - j // 2)
        else:
            self.place = lambda p: (1 - p // half) * p + (p // half) * (3 * half - 1 - p)
            self.where = self.place

    def here(self):
        f, c = lax.axis_index("fsdp"), lax.axis_index("ctx")
        core = c % 2
        return f, c, core, self.where(c // 2), 1 - 2 * core

    def device(self, position, core):
        return self.place((position + 2 * self.chips) % self.chips) * 2 + core


def greet(ring, f, c, core, p, way, over_fsdp):
    barrier = pltpu.get_barrier_semaphore()
    targets = [(f, ring.device(p - way, core)), (f, c + 1 - 2 * core)]
    if over_fsdp:
        targets += [((f + k) % ring.nf, c) for k in range(1, ring.nf)]
    for target in targets:
        pl.semaphore_signal(barrier, inc=1, device_id=target, device_id_type=MESH)
    pl.semaphore_wait(barrier, len(targets))


def gather_kernel(ring, wide, leads, count, swaps, *refs):
    swap_ins, swap_outs = refs[count : count + swaps], refs[2 * count + swaps : 2 * (count + swaps)]
    ins, outs = refs[:count], refs[count + swaps : 2 * count + swaps]
    own_sem, yss, yrs, rss, rrs, sss, srs, wss, wrs = refs[2 * (count + swaps) :]
    f, c, core, p, way = ring.here()
    n, nf = ring.chips, ring.nf
    greet(ring, f, c, core, p, way, any(wide))
    to_next = (f, ring.device(p + way, core))
    to_twin = (f, c + 1 - 2 * core)
    started, own = [], []

    def remote(src, dst, ss, rs, dev):
        return pltpu.make_async_remote_copy(
            src_ref=src, dst_ref=dst, send_sem=ss, recv_sem=rs, device_id=dev, device_id_type=MESH
        )

    streams, late = [], []
    number = 0
    for i in range(count):
        if wide[i]:
            streams.append((number, i, f, ins[i]))
            number += 1
        else:
            for a in range(leads[i]):
                streams.append((number, i, a, ins[i].at[a]))
                number += 1
    first = len(streams)
    yn = 0
    for i in range(count):
        if wide[i]:
            for k in range(1, nf):
                late.append((number, i, (f - k + nf) % nf, k, yn))
                number += 1
                yn += 1

    def send_ring(s, number, i, lead, owner, src):
        cp = remote(src, outs[i].at[lead, owner], rss.at[s, number], rrs.at[s, number], to_next)
        cp.start()
        started.append(cp)

    def send_twin(s, number, i, lead, owner, src):
        cp = remote(src, outs[i].at[lead, owner], sss.at[s, number], srs.at[s, number], to_twin)
        cp.start()
        started.append(cp)

    for number, i, lead, k, y in late:
        cp = remote(ins[i], outs[i].at[f, c], yss.at[y], yrs.at[y], ((f + k) % nf, c))
        cp.start()
        started.append(cp)
    for number, i, lead, src in streams:
        send_ring(0, number, i, lead, c, src)
    for number, i, lead, src in streams:
        send_twin(0, number, i, lead, c, src)
        cp = pltpu.make_async_copy(src, outs[i].at[lead, c], own_sem.at[number])
        cp.start()
        own.append(cp)
    everything = [(number, i, lead) for number, i, lead, _ in streams]
    everything += [(number, i, lead) for number, i, lead, _, _ in late]
    for number, i, lead, k, y in late:
        here = outs[i].at[lead, c]
        remote(here, here, yss.at[y], yrs.at[y], to_next).wait_recv()
        send_ring(0, number, i, lead, c, here)
        send_twin(0, number, i, lead, c, here)
    swapped = []
    for i in range(swaps):
        cp = remote(swap_ins[i], swap_outs[i], wss.at[i], wrs.at[i], ((f + 1) % nf, c))
        cp.start()
        swapped.append(cp)
    for s in range(1, n):
        owner = ring.device(p - way * s, core)
        for number, i, lead in everything:
            here = outs[i].at[lead, owner]
            remote(here, here, rss.at[s - 1, number], rrs.at[s - 1, number], to_next).wait_recv()
            if s < n - 1:
                send_ring(s, number, i, lead, owner, here)
            send_twin(s, number, i, lead, owner, here)
    for s in range(n):
        owner = ring.device(p + way * s, 1 - core)
        for number, i, lead in everything:
            here = outs[i].at[lead, owner]
            remote(here, here, sss.at[s, number], srs.at[s, number], to_twin).wait_recv()
    for cp in own:
        cp.wait()
    for cp in started:
        cp.wait_send()
    for cp in swapped:
        cp.wait()


def ring_gather(ring, number, arrays, wide, swaps=()):
    n, nf = ring.chips, ring.nf
    leads = [1 if w else a.shape[0] for a, w in zip(arrays, wide)]
    shapes, streams, late, size = [], 0, 0, 0
    for a, w in zip(arrays, wide):
        if w:
            shapes.append(jax.ShapeDtypeStruct((nf, 2 * n) + a.shape, a.dtype))
            streams += nf
            late += nf - 1
        else:
            shapes.append(jax.ShapeDtypeStruct((a.shape[0], 2 * n) + a.shape[1:], a.dtype))
            streams += a.shape[0]
        size += shapes[-1].size * 2
    dma = pltpu.SemaphoreType.DMA
    shapes += [jax.ShapeDtypeStruct(a.shape, a.dtype) for a in swaps]
    return pl.pallas_call(
        functools.partial(
            gather_kernel, ring, tuple(wide), tuple(leads), len(arrays), len(swaps)
        ),
        out_shape=shapes,
        in_specs=[pl.BlockSpec(memory_space=pl.ANY)] * len(shapes),
        out_specs=[pl.BlockSpec(memory_space=pl.ANY)] * len(shapes),
        scratch_shapes=[
            dma((streams,)),
            dma((max(1, late),)),
            dma((max(1, late),)),
            dma((n - 1, streams)),
            dma((n - 1, streams)),
            dma((n, streams)),
            dma((n, streams)),
            dma((max(1, len(swaps)),)),
            dma((max(1, len(swaps)),)),
        ],
        compiler_params=pltpu.CompilerParams(collective_id=number, has_side_effects=True),
        cost_estimate=pl.CostEstimate(flops=0, bytes_accessed=2 * size, transcendentals=0),
        name="ring_gather_%d" % number,
    )(*arrays, *swaps)


def add_rows(shape, work):
    rows = shape[0]
    step = 16 if rows % 16 == 0 else rows

    def one(r, carry):
        work(pl.ds(pl.multiple_of(r * step, step), step))
        return carry

    lax.fori_loop(0, rows // step, one, 0)


def reduce_kernel(ring, wide, leads, count, *refs):
    ins, outs = refs[:count], refs[count : 2 * count]
    own, twin, got = (refs[(2 + k) * count : (3 + k) * count] for k in range(3))
    refs = refs[5 * count :]
    wides = sum(wide)
    finals, ygots = refs[:wides], refs[wides : 2 * wides]
    own_sem, tss, trs, rss, rrs, yss, yrs = refs[2 * wides :]
    f, c, core, p, way = ring.here()
    n, nf = ring.chips, ring.nf
    greet(ring, f, c, core, p, way, any(wide))
    to_next = (f, ring.device(p + way, core))
    to_twin = (f, c + 1 - 2 * core)

    def remote(src, dst, ss, rs, dev):
        return pltpu.make_async_remote_copy(
            src_ref=src, dst_ref=dst, send_sem=ss, recv_sem=rs, device_id=dev, device_id_type=MESH
        )

    streams = []
    for k in range(max(leads)):
        for i in range(count):
            if k < leads[i]:
                lead = (f + 1 + k) % nf if wide[i] else k
                streams.append((len(streams), i, k, lead))
    started, loads = [], {}
    for s in range(n):
        theirs = ring.device(p + way * (1 + s), 1 - core)
        mine = ring.device(p - way * (1 + s), core)
        for number, i, k, lead in streams:
            cp = remote(
                ins[i].at[lead, theirs], twin[i].at[s, k], tss.at[s, number], trs.at[s, number], to_twin
            )
            cp.start()
            started.append(cp)
            cp = pltpu.make_async_copy(
                ins[i].at[lead, mine], own[i].at[s, k], own_sem.at[s, number]
            )
            cp.start()
            loads[s, number] = cp

    def wait_parts(s, number, i, k):
        loads[s, number].wait()
        here = twin[i].at[s, k]
        remote(here, here, tss.at[s, number], trs.at[s, number], to_twin).wait_recv()

    def pass_on(s, number, i, k, src):
        cp = remote(src, got[i].at[s, k], rss.at[s, number], rrs.at[s, number], to_next)
        cp.start()
        started.append(cp)

    for s in range(n):
        for number, i, k, lead in streams:
            wait_parts(s, number, i, k)
            mine, other = own[i].at[s, k], twin[i].at[s, k]
            if s == 0:

                def start(rows, mine=mine, other=other):
                    mine[rows, :] = (mine[rows, :].astype(F32) + other[rows, :].astype(F32)).astype(BF)

                add_rows(mine.shape, start)
                pass_on(0, number, i, k, mine)
                continue
            came = got[i].at[s - 1, k]
            remote(came, came, rss.at[s - 1, number], rrs.at[s - 1, number], to_next).wait_recv()
            if s < n - 1:

                def middle(rows, mine=mine, other=other, came=came):
                    total = mine[rows, :].astype(F32) + other[rows, :].astype(F32)
                    came[rows, :] = (came[rows, :].astype(F32) + total).astype(BF)

                add_rows(mine.shape, middle)
                pass_on(s, number, i, k, came)
                continue
            if not wide[i]:
                target = outs[i].at[k]
            elif k == nf - 1:
                target = outs[i]
            else:
                target = finals[sum(wide[:i])].at[k]

            def last(rows, mine=mine, other=other, came=came, target=target):
                total = mine[rows, :].astype(F32) + other[rows, :].astype(F32)
                target[rows, :] = (came[rows, :].astype(F32) + total).astype(target.dtype)

            add_rows(mine.shape, last)
            if wide[i] and k < nf - 1:
                w = sum(wide[:i])
                cp = remote(target, ygots[w].at[k], yss.at[w, k], yrs.at[w, k], ((f + 1 + k) % nf, c))
                cp.start()
                started.append(cp)
    for i in range(count):
        if wide[i]:
            w = sum(wide[:i])
            for k in range(nf - 1):
                here = ygots[w].at[k]
                remote(here, here, yss.at[w, k], yrs.at[w, k], to_next).wait_recv()

                def finish(rows, here=here, target=outs[i]):
                    target[rows, :] = target[rows, :] + here[rows, :].astype(F32)

                add_rows(here.shape, finish)
    for cp in started:
        cp.wait_send()


def ring_reduce(ring, number, arrays, wide):
    n, nf = ring.chips, ring.nf
    leads = [a.shape[0] for a in arrays]
    streams = sum(leads)
    block = [a.shape[2:] for a in arrays]
    shapes = [
        jax.ShapeDtypeStruct(b if w else (l,) + b, F32) for b, w, l in zip(block, wide, leads)
    ]
    dma = pltpu.SemaphoreType.DMA
    scratch = [pltpu.VMEM((n, l) + b, BF) for b, l in zip(block, leads)] * 2
    scratch += [pltpu.VMEM((n - 1, l) + b, BF) for b, l in zip(block, leads)]
    scratch += [pltpu.VMEM((nf - 1,) + b, BF) for b, w in zip(block, wide) if w] * 2
    wides = max(1, sum(wide))
    size = sum(a.size * 2 for a in arrays)
    return pl.pallas_call(
        functools.partial(reduce_kernel, ring, tuple(wide), tuple(leads), len(arrays)),
        out_shape=shapes,
        in_specs=[pl.BlockSpec(memory_space=pl.ANY)] * len(arrays),
        out_specs=[pl.BlockSpec(memory_space=pltpu.VMEM)] * len(arrays),
        scratch_shapes=scratch
        + [
            dma((n, streams)),
            dma((n, streams)),
            dma((n, streams)),
            dma((n - 1, streams)),
            dma((n - 1, streams)),
            dma((wides, max(1, nf - 1))),
            dma((wides, max(1, nf - 1))),
        ],
        compiler_params=pltpu.CompilerParams(
            collective_id=number, has_side_effects=True, vmem_limit_bytes=56 << 20
        ),
        cost_estimate=pl.CostEstimate(flops=0, bytes_accessed=2 * size, transcendentals=0),
        name="ring_reduce_%d" % number,
    )(*arrays)


def expert_kernel(nf, experts, fp, bundle_slots, *refs):
    x_ref, g_ref, probs_ref, slot_ref, column_ref = refs[:5]
    weights, refs = refs[5 : 5 + 4 * nf], refs[5 + 4 * nf :]
    back_ref, out_ref, delta_ref, rows_ref, grads_ref, hid_ref, gg_ref, ug_ref, act_ref = refs[:9]
    w_gate, w_up, w_down, w_shared, pre_gate, pre_up, pre_in, pre_s, raw, sems = refs[9:]
    mine = lax.axis_index("ctx")
    held = (w_gate, w_up, w_down, w_shared)
    part = w_gate.shape[0] // nf
    wide = w_gate.shape[0]
    copies = [
        [
            pltpu.make_async_copy(
                weights[4 * k + i], held[i].at[pl.ds(k * part, part)], sems.at[i, k]
            )
            for k in range(nf)
        ]
        for i in range(4)
    ]
    first = pl.program_id(0) == 0

    def ready(i):
        @pl.when(first)
        def _():
            for cp in copies[i]:
                cp.wait()

    @pl.when(first)
    def _():
        for i in (3, 0, 1, 2):
            for cp in copies[i]:
                cp.start()

    def nt(left, right):
        return lax.dot_general(left, right, (((1,), (1,)), ((), ())), preferred_element_type=F32)

    bundles, _, rows = slot_ref.shape
    lane = lax.broadcasted_iota(jnp.int32, (rows, 128), 1)
    own_lane = (lane % experts == mine) & (lane < 3 * experts)
    puts, row_gates = [], []
    for b in range(bundles):
        cut, spot = pl.ds(b * rows, rows), pl.ds(b * bundle_slots, bundle_slots)
        takes = (
            slot_ref[b] == lax.broadcasted_iota(jnp.int32, (bundle_slots, rows), 0)
        ).astype(F32).astype(BF)
        puts.append(
            (
                column_ref[cut, :] == lax.broadcasted_iota(jnp.int32, (rows, bundle_slots), 1)
            ).astype(F32).astype(BF)
        )
        own = jnp.where(own_lane, probs_ref[cut, :].astype(F32), 0.0)
        row_gates.append(jnp.sum(own, axis=1, keepdims=True))
        gate = jnp.sum(multiply(takes, own.astype(BF)), axis=1, keepdims=True)
        for start in range(0, wide, 512):
            piece = pl.ds(start, 512)
            rows_ref[spot, piece] = multiply(takes, x_ref[cut, piece]).astype(BF)
            taken = multiply(takes, g_ref[cut, piece])
            raw[spot, piece] = taken.astype(BF)
            grads_ref[spot, piece] = (gate * taken).astype(BF)

    ready(3)
    pre_s[:, : 2 * fp] = multiply(x_ref[...], w_shared[:, : 2 * fp])
    pre_s[:, 2 * fp :] = multiply(g_ref[...], w_shared[:, 2 * fp :])

    def activate(gate_pre, up_pre, inner):
        sig = jax.nn.sigmoid(gate_pre)
        activated = gate_pre * sig
        hidden = activated * up_pre
        gate_grad = inner * up_pre * sig * (1.0 + gate_pre * (1.0 - sig))
        return hidden.astype(BF), gate_grad.astype(BF), (inner * activated).astype(BF)

    step = 32

    def shared_rows(r, carry):
        at = pl.ds(pl.multiple_of(r * step, step), step)
        for start in range(0, fp, 128):
            cuts = [pl.ds(i * fp + start, 128) for i in range(3)]
            hidden, gate_grad, up_grad = activate(*(pre_s[at, c] for c in cuts))
            act_ref[at, cuts[0]] = gate_grad
            act_ref[at, cuts[1]] = up_grad
            act_ref[at, cuts[2]] = hidden
        return carry

    lax.fori_loop(0, pre_s.shape[0] // step, shared_rows, 0)

    ready(0)
    pre_gate[...] = multiply(rows_ref[...], w_gate[...])
    ready(1)
    pre_up[...] = multiply(rows_ref[...], w_up[...])
    ready(2)
    pre_in[...] = multiply(grads_ref[...], w_down[...])

    def expert_rows(r, carry):
        at = pl.ds(pl.multiple_of(r * step, step), step)
        for start in range(0, hid_ref.shape[1], 128):
            c = pl.ds(start, 128)
            hidden, gate_grad, up_grad = activate(pre_gate[at, c], pre_up[at, c], pre_in[at, c])
            hid_ref[at, c] = hidden
            gg_ref[at, c] = gate_grad
            ug_ref[at, c] = up_grad
        return carry

    lax.fori_loop(0, hid_ref.shape[0] // step, expert_rows, 0)

    delta = 0.0
    for start in range(0, wide, 512):
        piece = pl.ds(start, 512)
        e_back = nt(gg_ref[...], w_gate[piece, :]) + nt(ug_ref[...], w_up[piece, :])
        e_back = e_back.astype(BF)
        e_out = nt(hid_ref[...], w_down[piece, :]).astype(BF)
        delta = delta + jnp.sum(
            raw[:, piece].astype(F32) * e_out.astype(F32), axis=1, keepdims=True
        )
        for b in range(bundles):
            cut = pl.ds(b * rows, rows)
            spot = slice(b * bundle_slots, (b + 1) * bundle_slots)
            s_back = nt(act_ref[cut, : 2 * fp], w_shared[piece, : 2 * fp])
            back_ref[cut, piece] = (multiply(puts[b], e_back[spot]) + s_back).astype(BF)
            s_out = nt(act_ref[cut, 2 * fp :], w_shared[piece, 2 * fp :])
            out_ref[cut, piece] = (row_gates[b] * multiply(puts[b], e_out[spot]) + s_out).astype(BF)
    for b in range(bundles):
        own = delta[b * bundle_slots : (b + 1) * bundle_slots]
        high = own.astype(BF).astype(F32)
        middle = (own - high).astype(BF).astype(F32)
        low = own - high - middle
        spread = jnp.where(lane[:bundle_slots] < experts, high, jnp.where(lane[:bundle_slots] < 2 * experts, middle, low))
        spread = jnp.where(own_lane[:bundle_slots], spread, 0.0).astype(BF)
        delta_ref[pl.ds(b * rows, rows), :] = multiply(puts[b], spread).astype(BF)


def run_experts(nf, experts, capacity, tok_loc, tree_rows, tree_grads, tree_probs, slot, weights):
    rows, wide = tree_rows.shape
    bundles, per = slot.shape
    bundle_slots = capacity * (per // tok_loc)
    hidden, fp = weights[0][0].shape[1], weights[0][3].shape[1] // 3
    group = 2 if bundles % 2 == 0 else 1
    steps = bundles // group
    block, slots = rows // steps, group * bundle_slots
    flat = [w for piece in weights for w in piece]
    by_row = lambda width: pl.BlockSpec((block, width), lambda i: (i, 0))
    by_slot = lambda width: pl.BlockSpec((slots, width), lambda i: (i, 0))
    any_spec = pl.BlockSpec(memory_space=pl.ANY)
    shape = lambda n, width: jax.ShapeDtypeStruct((n, width), BF)
    total = steps * slots
    flops = 2 * (6 * total * wide * hidden + 6 * rows * wide * fp + 4 * rows * bundle_slots * wide)
    return pl.pallas_call(
        functools.partial(expert_kernel, nf, experts, fp, bundle_slots),
        grid=(steps,),
        out_shape=[shape(rows, wide), shape(rows, wide), shape(rows, 128)]
        + [shape(total, wide)] * 2
        + [shape(total, hidden)] * 3
        + [shape(rows, 3 * fp)],
        in_specs=[
            by_row(wide),
            by_row(wide),
            by_row(128),
            pl.BlockSpec((group, 1, per), lambda i: (i, 0, 0)),
            pl.BlockSpec((block, 1), lambda i: (i, 0)),
        ]
        + [any_spec] * len(flat),
        out_specs=[by_row(wide), by_row(wide), by_row(128)]
        + [by_slot(wide)] * 2
        + [by_slot(hidden)] * 3
        + [by_row(3 * fp)],
        scratch_shapes=[pltpu.VMEM((wide, hidden), BF)] * 3
        + [pltpu.VMEM((wide, 3 * fp), BF)]
        + [pltpu.VMEM((slots, hidden), F32)] * 3
        + [pltpu.VMEM((block, 3 * fp), F32), pltpu.VMEM((slots, wide), BF)]
        + [pltpu.SemaphoreType.DMA((4, nf))],
        compiler_params=pltpu.CompilerParams(vmem_limit_bytes=61 << 20),
        cost_estimate=pl.CostEstimate(
            flops=flops, bytes_accessed=10 * rows * wide, transcendentals=total * hidden
        ),
        name="experts",
    )(tree_rows, tree_grads, tree_probs, slot[:, None, :], slot.reshape(rows, 1), *flat)


def body(
    tokens,
    out_grad,
    segments,
    path_mask,
    expert_ids,
    norm_attn,
    attn_q,
    attn_kva,
    norm_latent,
    attn_kvb,
    attn_out,
    norm_ffn,
    router,
    expert_gate,
    expert_up,
    expert_down,
    shared_gate,
    shared_up,
    shared_down,
):
    trees, tok_loc = tokens.shape[:2]
    row_total = trees * tok_loc
    nc, nf = lax.axis_size("ctx"), lax.axis_size("fsdp")
    mine, group = lax.axis_index("ctx"), lax.axis_index("fsdp")
    experts = nc
    ring = Ring(nf, nc)
    tree_len = tok_loc * nc
    group_rows = trees * tree_len
    first_row = mine * tok_loc
    capacity = min(tok_loc, tok_loc * TOP * 4 // (3 * experts))
    slot_total = nc * trees * capacity
    score_scale = 1.0 / math.sqrt(DN + DR)
    frequency = rope_base ** (-(jnp.arange(DR // 2, dtype=F32) * 2.0 / DR))
    labels = jnp.arange(experts, dtype=jnp.int32)
    both = ("fsdp", "ctx")
    part = D // nf

    def roll_in(x):
        return lax.dynamic_slice_in_dim(jnp.concatenate([x, x], axis=-1), group * part, D, x.ndim - 1)

    def roll_out(x):
        return lax.dynamic_slice_in_dim(
            jnp.concatenate([x, x], axis=-1), (nf - group) % nf * part, D, x.ndim - 1
        )

    def fetch(w):
        pieces = [w]
        for k in range(1, nf):
            pieces.append(lax.ppermute(w, "fsdp", [(i, (i - k) % nf) for i in range(nf)]))
        return pieces

    fs = shared_gate.shape[1]
    fp = -(-fs // 128) * 128
    shared_w = jnp.concatenate(
        [jnp.pad(w, ((0, 0), (0, fp - fs))) for w in (shared_gate, shared_up, shared_down)], axis=1
    )
    small = jnp.concatenate(
        [
            norm_attn,
            norm_ffn,
            norm_latent,
            router.reshape(-1),
            expert_ids.astype(BF).reshape(-1),
        ]
    )
    small = jnp.pad(small, (0, PACK - small.shape[0])).reshape(16, PACK // 16)
    if nf == 2:
        w_latent, w_query, w_expand, small_all, w_output, other_gate, other_shared = ring_gather(
            ring, 0, [attn_kva, attn_q, attn_kvb, small, attn_out], [True] * 5, [expert_gate, shared_w]
        )
        e_gate, s_all = [expert_gate, other_gate], [shared_w, other_shared]
        later_up, later_down, later_grads, small_all = lax.optimization_barrier(
            (expert_up, expert_down, out_grad, small_all)
        )
    else:
        w_latent, w_query, w_expand, small_all, w_output = (
            lax.all_gather(w, both, axis=0) for w in (attn_kva, attn_q, attn_kvb, small, attn_out)
        )
        e_gate, s_all = fetch(expert_gate), fetch(shared_w)
        later_up, later_down, later_grads = expert_up, expert_down, out_grad
    e_up, e_down = fetch(later_up), fetch(later_down)
    w_output = w_output.reshape(H * DV, D)
    w_latent, w_query = w_latent.reshape(D, -1), w_query.reshape(D, -1)
    w_expand = w_expand.reshape(LAT, -1)
    small_all = small_all.reshape(nf * nc, PACK)
    r_one, r_lat, r_router = norm_attn.shape[0], norm_latent.shape[0], router.size
    cuts = [0, r_one, 2 * r_one, 2 * r_one + r_lat, 2 * r_one + r_lat + r_router]
    gain_attn = small_all[:, cuts[0] : cuts[1]].reshape(-1).astype(F32)
    gain_ffn = small_all[:, cuts[1] : cuts[2]].reshape(-1).astype(F32)
    gain_latent = small_all[:, cuts[2] : cuts[3]].reshape(-1).astype(F32)
    w_router = small_all[:, cuts[3] : cuts[4]].reshape(D, experts)
    ids_all = lax.dynamic_slice_in_dim(small_all.reshape(nf, nc, PACK), group, 1, 0)[0]
    ids_all = ids_all[:, cuts[4] : cuts[4] + expert_ids.size].reshape(nc, trees, tok_loc, TOP)
    ids_all = ids_all.transpose(1, 0, 2, 3).reshape(group_rows, TOP)

    upstream_low = out_grad.reshape(row_total, D)
    upstream = upstream_low.astype(F32)
    tree_grads = lax.all_gather(roll_in(later_grads), "ctx", axis=1, tiled=True).reshape(group_rows, D)

    def one_mask(segment_ids, path_table):
        return tree_mask(segment_ids, path_table, first_row, tok_loc)

    allowed, positions = jax.vmap(one_mask)(segments, path_mask)
    rotation = positions.astype(F32)[:, :, None] * frequency[None, None, :]
    cosine, sine = jnp.cos(rotation), jnp.sin(rotation)
    inputs = tokens.astype(F32).reshape(row_total, D)
    normed_in, inverse_in, gained_in = normalize(inputs, gain_attn)
    hidden_in = gained_in.astype(BF)
    latent_all = multiply(hidden_in, w_latent)
    latent_normed, latent_inverse, latent_gained = normalize(latent_all[:, :LAT], gain_latent)
    key_latent = latent_gained.astype(BF).reshape(trees, tok_loc, LAT)
    key_rope = rotate(latent_all[:, LAT:].reshape(trees, tok_loc, DR), cosine, sine).astype(BF)
    (keys,) = ring_gather(
        ring, 1, [jnp.concatenate([key_latent, key_rope], axis=-1)], [False]
    )
    keys = keys.reshape(trees, tree_len, LAT + DR)
    keys_latent = keys[:, :, :LAT]
    query_all = lax.optimization_barrier(multiply(hidden_in, w_query))
    query_all = query_all.reshape(trees, tok_loc, H, DN + DR)
    query_nope = query_all[..., :DN].astype(BF)
    query_rope = rotate(
        query_all[..., DN:], cosine[:, :, None, :], sine[:, :, None, :]
    ).astype(BF)
    expand = w_expand.reshape(LAT, H, DN + DV)
    expand_key = expand[..., :DN]
    expand_value = expand[..., DN:]
    query_latent = jnp.einsum(
        "bthn,chn->bthc", query_nope, expand_key, preferred_element_type=F32
    ).astype(BF)
    query_cat = jnp.concatenate([query_latent, query_rope], axis=-1).reshape(
        trees, tok_loc * H, LAT + DR
    )

    def attention_scores():
        raw_scores = jnp.einsum("bqc,bjc->bqj", query_cat, keys, preferred_element_type=F32)
        raw_scores = raw_scores.reshape(trees, tok_loc, H, tree_len)
        scores = jnp.where(allowed[:, :, None, :], raw_scores * score_scale, -1e30)
        return scores.reshape(trees, tok_loc * H, tree_len)

    scores = attention_scores()
    highest = jnp.max(scores, axis=-1, keepdims=True)
    exp_total = jnp.sum(jnp.exp(scores - highest), axis=-1, keepdims=True)
    log_total = highest + jnp.log(exp_total)
    weights_low = jnp.exp(scores - log_total).astype(BF)
    mixed = jnp.einsum("bqj,bjc->bqc", weights_low, keys_latent, preferred_element_type=F32)
    mixed = mixed.astype(BF).reshape(trees, tok_loc, H, LAT)
    heads = (
        jnp.einsum("bthc,chv->bthv", mixed, expand_value, preferred_element_type=F32)
        .astype(BF)
        .reshape(row_total, H * DV)
    )
    residual = inputs + multiply(heads, w_output)
    normed_mid, inverse_mid, gained_mid = normalize(residual, gain_ffn)
    hidden_mid = gained_mid.astype(BF)
    expert_probs = jax.nn.softmax(multiply(hidden_mid, w_router), axis=-1)

    probs_parts = jnp.concatenate(three_parts(expert_probs), axis=-1)
    probs_parts = jnp.pad(probs_parts, ((0, 0), (0, 128 - 3 * experts)))
    tree_rows, tree_probs = ring_gather(
        ring,
        2,
        [roll_in(hidden_mid).reshape(trees, tok_loc, D), probs_parts.reshape(trees, tok_loc, 128)],
        [False, False],
    )
    tree_rows = tree_rows.reshape(group_rows, D)
    tree_probs = tree_probs.reshape(group_rows, 128)

    member = jnp.any(ids_all == mine.astype(BF), axis=1)
    blocks = trees * nc
    bundle = 4 if blocks % 4 == 0 else 1
    bundles = blocks // bundle
    grid = member.astype(BF).reshape(blocks, tok_loc)
    upper = (jnp.arange(tok_loc)[:, None] <= jnp.arange(tok_loc)[None, :]).astype(BF)
    slot = multiply(grid, upper).astype(jnp.int32) - 1
    slot = slot + (jnp.arange(blocks, dtype=jnp.int32) % bundle * capacity)[:, None]
    slot = jnp.where(grid > 0, slot, -1).reshape(bundles, bundle * tok_loc)
    back, out_part, delta_out, e_rows, e_grads, e_hidden, e_gg, e_ug, s_act = run_experts(
        nf,
        experts,
        capacity,
        tok_loc,
        tree_rows,
        tree_grads,
        tree_probs,
        slot,
        list(zip(e_gate, e_up, e_down, s_all)),
    )

    def weight_grads(k, e_gg, e_ug, e_hidden, s_act):
        cut = slice(k * part, (k + 1) * part)
        return (
            transposed_multiply(e_rows[:, cut], e_gg),
            transposed_multiply(e_rows[:, cut], e_ug),
            transposed_multiply(e_grads[:, cut], e_hidden),
            transposed_multiply(tree_rows[:, cut], s_act[:, : 2 * fp]),
            transposed_multiply(tree_grads[:, cut], s_act[:, 2 * fp :]),
        )

    def by_owner(x):
        return x.reshape(trees, nc, tok_loc, x.shape[-1])

    back_sum, delta_sum = ring_reduce(
        ring, 3, [by_owner(back), by_owner(delta_out)], [False] * 2
    )
    back_sum, out_part = lax.optimization_barrier((back_sum, out_part))
    back_sum = roll_out(back_sum.reshape(row_total, D))
    prob_delta = jnp.sum(
        delta_sum.reshape(row_total, 128)[:, : 3 * experts].reshape(row_total, 3, experts), axis=1
    )
    out_sum = lax.psum_scatter(
        out_part.reshape(trees, tree_len, D), "ctx", scatter_dimension=1, tiled=True
    )
    out_sum = roll_out(out_sum.reshape(row_total, D).astype(F32))
    output = (residual + out_sum).astype(BF).reshape(trees, tok_loc, D)

    came = []
    for k in range(1, nf):
        perm = [(i, (i + k) % nf) for i in range(nf)]
        grads = weight_grads(k, e_gg, e_ug, e_hidden, s_act)
        came.append([lax.ppermute(g.astype(BF), "fsdp", perm) for g in grads])

    logit_grad = (
        expert_probs * (prob_delta - jnp.sum(expert_probs * prob_delta, axis=-1, keepdims=True))
    ).astype(BF)
    grad_router = transposed_multiply(hidden_mid, logit_grad)
    mid_grad = back_sum + multiply_transposed(logit_grad, w_router)
    mid_input, grad_gain_ffn = normalize_back(mid_grad, normed_mid, inverse_mid, gain_ffn)
    residual_grad = upstream + mid_input
    residual_low = residual_grad.astype(BF)
    grad_output = transposed_multiply(heads, residual_low).astype(BF)
    out_total = lax.psum_scatter(grad_output, both, scatter_dimension=0, tiled=True).astype(F32)
    heads_grad = (
        multiply_transposed(residual_low, w_output).astype(BF).reshape(trees, tok_loc, H, DV)
    )
    mixed_grad = jnp.einsum(
        "bthv,chv->bthc", heads_grad, expand_value, preferred_element_type=F32
    ).astype(BF)
    mixed_grad_flat = mixed_grad.reshape(trees, tok_loc * H, LAT)
    scores = attention_scores()
    weights_full = jnp.exp(scores - log_total)
    prob_grad = jnp.einsum(
        "bqc,bjc->bqj", mixed_grad_flat, keys_latent, preferred_element_type=F32
    )
    score_grad = (
        weights_full * (prob_grad - jnp.sum(weights_full * prob_grad, axis=-1, keepdims=True))
    ).astype(BF)
    keys_grad = (
        jnp.einsum("bqj,bqc->bjc", score_grad, query_cat, preferred_element_type=F32) * score_scale
    )
    latent_part = jnp.einsum(
        "bqj,bqc->bjc", weights_full.astype(BF), mixed_grad_flat, preferred_element_type=F32
    )
    keys_grad = jnp.concatenate(
        [keys_grad[..., :LAT] + latent_part, keys_grad[..., LAT:]], axis=-1
    ).astype(BF)
    (own_keys_grad,) = ring_reduce(
        ring, 4, [keys_grad.reshape(trees, nc, tok_loc, LAT + DR)], [False]
    )
    query_cat_grad = (
        jnp.einsum("bqj,bjc->bqc", score_grad, keys, preferred_element_type=F32) * score_scale
    ).reshape(trees, tok_loc, H, LAT + DR)
    qlat_grad = query_cat_grad[..., :LAT].astype(BF)
    qrope_grad = query_cat_grad[..., LAT:]
    qnope_grad = jnp.einsum("bthc,chn->bthn", qlat_grad, expand_key, preferred_element_type=F32)
    grad_key = jnp.einsum("bthc,bthn->chn", qlat_grad, query_nope, preferred_element_type=F32)
    grad_value = jnp.einsum("bthc,bthv->chv", mixed, heads_grad, preferred_element_type=F32)
    grad_expand = jnp.concatenate([grad_key, grad_value], axis=-1).reshape(LAT, H * (DN + DV))
    query_grad = jnp.concatenate(
        [qnope_grad, rotate(qrope_grad, cosine[:, :, None, :], -sine[:, :, None, :])], axis=-1
    )
    query_grad = query_grad.astype(BF).reshape(row_total, H * (DN + DR))
    grad_query = transposed_multiply(hidden_in, query_grad)
    hidden_grad = multiply_transposed(query_grad, w_query)
    latent_in_grad, grad_gain_latent = normalize_back(
        own_keys_grad[..., :LAT].reshape(row_total, LAT), latent_normed, latent_inverse, gain_latent
    )
    rope_back = rotate(own_keys_grad[..., LAT:], cosine, -sine).reshape(row_total, DR)
    latent_grad = jnp.concatenate([latent_in_grad, rope_back], axis=-1).astype(BF)
    grad_latent = transposed_multiply(hidden_in, latent_grad)
    hidden_grad = hidden_grad + multiply_transposed(latent_grad, w_latent)
    input_part, grad_gain_attn = normalize_back(hidden_grad, normed_in, inverse_in, gain_attn)
    input_grad = (input_part + residual_grad).reshape(trees, tok_loc, D)

    grad_small = jnp.concatenate(
        [
            grad_gain_attn.reshape(nf * nc, r_one),
            grad_gain_ffn.reshape(nf * nc, r_one),
            grad_gain_latent.reshape(nf * nc, r_lat),
            grad_router.reshape(nf * nc, r_router),
        ],
        axis=1,
    ).astype(BF)
    grad_small = jnp.pad(grad_small, ((0, 0), (0, PACK - grad_small.shape[1])))
    parts = [
        grad_query.astype(BF).reshape(nf, nc, -1, w_query.shape[1]),
        grad_expand.astype(BF).reshape(nf, nc, -1, w_expand.shape[1]),
        grad_latent.astype(BF).reshape(nf, nc, -1, w_latent.shape[1]),
        grad_small.reshape(nf, nc, 16, PACK // 16),
    ]
    if nf == 2:
        t_query, t_expand, t_latent, t_small = ring_reduce(ring, 5, parts, [True] * 4)
    else:
        t_query, t_expand, t_latent, t_small = (
            lax.psum_scatter(
                x.reshape((nf * nc,) + x.shape[2:]), both, scatter_dimension=0, tiled=True
            )[0].astype(F32)
            for x in parts
        )
    t_small = t_small.reshape(PACK)
    t_small, came, e_gg, e_ug, e_hidden, s_act = lax.optimization_barrier(
        (t_small, came, e_gg, e_ug, e_hidden, s_act)
    )
    ffn_sums = list(weight_grads(0, e_gg, e_ug, e_hidden, s_act))
    for one in came:
        ffn_sums = [a + b.astype(F32) for a, b in zip(ffn_sums, one)]
    e_sums = ffn_sums[:3]
    s_sums = [ffn_sums[3][:, :fs], ffn_sums[3][:, fp : fp + fs], ffn_sums[4][:, :fs]]
    return (
        output,
        input_grad,
        t_small[cuts[0] : cuts[1]],
        t_query,
        t_latent,
        t_small[cuts[2] : cuts[3]],
        t_expand,
        out_total,
        t_small[cuts[1] : cuts[2]],
        t_small[cuts[3] : cuts[4]].reshape(-1, experts),
        *e_sums,
        *s_sums,
    )


def solution(mesh):
    placed = (
        P("fsdp", "ctx", None),
        P("fsdp", "ctx", None),
        P("fsdp", None),
        P("fsdp", None, None),
        P("fsdp", "ctx", None),
        P(("fsdp", "ctx")),
        P(("fsdp", "ctx"), None),
        P(("fsdp", "ctx"), None),
        P(("fsdp", "ctx")),
        P(("fsdp", "ctx"), None),
        P(("fsdp", "ctx"), None),
        P(("fsdp", "ctx")),
        P(("fsdp", "ctx"), None),
        P("fsdp", "ctx"),
        P("fsdp", "ctx"),
        P("fsdp", "ctx"),
        P("fsdp", "ctx"),
        P("fsdp", "ctx"),
        P("fsdp", "ctx"),
    )
    return jax.shard_map(
        body,
        mesh=mesh,
        in_specs=placed,
        out_specs=(
            P("fsdp", "ctx", None),
            P("fsdp", "ctx", None),
            P(("fsdp", "ctx")),
            P(("fsdp", "ctx"), None),
            P(("fsdp", "ctx"), None),
            P(("fsdp", "ctx")),
            P(("fsdp", "ctx"), None),
            P(("fsdp", "ctx"), None),
            P(("fsdp", "ctx")),
            P(("fsdp", "ctx"), None),
            P("fsdp", "ctx"),
            P("fsdp", "ctx"),
            P("fsdp", "ctx"),
            P("fsdp", "ctx"),
            P("fsdp", "ctx"),
            P("fsdp", "ctx"),
        ),
        check_vma=False,
    )
```

```python
import functools
import math

import jax
import jax.numpy as jnp
from jax import lax
from jax.experimental import pallas as pl
from jax.experimental.pallas import tpu as pltpu
from jax.sharding import PartitionSpec as P

D = 2048
H = 16
DN = 128
DR = 64
DV = 128
LAT = 512
TOP = 6
SEGS = 13
PACK = 2048

MESH = pl.DeviceIdType.MESH
BF = jnp.bfloat16
F32 = jnp.float32

epsilon = 1e-06
rope_base = 10000.0


def multiply(left, right):
    return jnp.dot(left, right, preferred_element_type=F32)


def multiply_transposed(left, right):
    return lax.dot_general(left, right, (((1,), (1,)), ((), ())), preferred_element_type=F32)


def transposed_multiply(left, right):
    return lax.dot_general(left, right, (((0,), (0,)), ((), ())), preferred_element_type=F32)


def normalize(tensor_in, gain_vec):
    inverse = lax.rsqrt(jnp.mean(tensor_in * tensor_in, axis=-1, keepdims=True) + epsilon)
    normed = tensor_in * inverse
    return (normed, inverse, normed * gain_vec)


def normalize_back(grad_out, normed, inverse, gain_vec):
    weighted = grad_out * gain_vec
    centre = jnp.mean(weighted * normed, axis=-1, keepdims=True)
    return (inverse * (weighted - normed * centre), jnp.sum(grad_out * normed, axis=0))


def rotate(tensor_in, cosine, sine):
    half_width = tensor_in.shape[-1] // 2
    former = tensor_in[..., :half_width]
    latter = tensor_in[..., half_width:]
    return jnp.concatenate(
        [former * cosine - latter * sine, latter * cosine + former * sine], axis=-1
    )


def tree_mask(segment_ids, path_table, first_row, row_count):
    labels = jnp.arange(SEGS, dtype=jnp.int32)
    own_ids = lax.dynamic_slice_in_dim(segment_ids, first_row, row_count)
    own_hot = (own_ids[:, None] == labels[None, :]).astype(BF)
    all_hot = (segment_ids[:, None] == labels[None, :]).astype(BF)
    ancestry = multiply(own_hot, path_table.astype(BF)).astype(BF)
    related = multiply_transposed(ancestry, all_hot)
    places = jnp.arange(segment_ids.shape[0], dtype=jnp.int32)
    queries = first_row + jnp.arange(row_count, dtype=jnp.int32)
    allowed = (related > 0) & (places[None, :] <= queries[:, None])
    positions = jnp.sum(allowed.astype(jnp.int32), axis=1) - 1
    return (allowed, positions)


def three_parts(value):
    first = lax.reduce_precision(value, 8, 7)
    second = lax.reduce_precision(value - first, 8, 7)
    third = value - first - second
    return (first.astype(BF), second.astype(BF), third.astype(BF))


class Ring:
    def __init__(self, nf, nc):
        self.nf, self.chips = nf, nc // 2
        half = self.chips // 2
        if nf == 2:
            self.place = lambda p: (1 - p // half) * 2 * p + (p // half) * (4 * half - 1 - 2 * p)
            self.where = lambda j: (1 - j % 2) * (j // 2) + (j % 2) * (2 * half - 1 - j // 2)
        else:
            self.place = lambda p: (1 - p // half) * p + (p // half) * (3 * half - 1 - p)
            self.where = self.place

    def here(self):
        f, c = lax.axis_index("fsdp"), lax.axis_index("ctx")
        core = c % 2
        return f, c, core, self.where(c // 2), 1 - 2 * core

    def device(self, position, core):
        return self.place((position + 2 * self.chips) % self.chips) * 2 + core


def greet(ring, f, c, core, p, way, over_fsdp):
    barrier = pltpu.get_barrier_semaphore()
    targets = [(f, ring.device(p - way, core)), (f, c + 1 - 2 * core)]
    if over_fsdp:
        targets += [((f + k) % ring.nf, c) for k in range(1, ring.nf)]
    for target in targets:
        pl.semaphore_signal(barrier, inc=1, device_id=target, device_id_type=MESH)
    pl.semaphore_wait(barrier, len(targets))


def gather_kernel(ring, wide, leads, count, swaps, *refs):
    swap_ins, swap_outs = refs[count : count + swaps], refs[2 * count + swaps : 2 * (count + swaps)]
    ins, outs = refs[:count], refs[count + swaps : 2 * count + swaps]
    own_sem, yss, yrs, rss, rrs, sss, srs, wss, wrs = refs[2 * (count + swaps) :]
    f, c, core, p, way = ring.here()
    n, nf = ring.chips, ring.nf
    greet(ring, f, c, core, p, way, any(wide))
    to_next = (f, ring.device(p + way, core))
    to_twin = (f, c + 1 - 2 * core)
    started, own = [], []

    def remote(src, dst, ss, rs, dev):
        return pltpu.make_async_remote_copy(
            src_ref=src, dst_ref=dst, send_sem=ss, recv_sem=rs, device_id=dev, device_id_type=MESH
        )

    streams, late = [], []
    number = 0
    for i in range(count):
        if wide[i]:
            streams.append((number, i, f, ins[i]))
            number += 1
        else:
            for a in range(leads[i]):
                streams.append((number, i, a, ins[i].at[a]))
                number += 1
    first = len(streams)
    yn = 0
    for i in range(count):
        if wide[i]:
            for k in range(1, nf):
                late.append((number, i, (f - k + nf) % nf, k, yn))
                number += 1
                yn += 1

    def send_ring(s, number, i, lead, owner, src):
        cp = remote(src, outs[i].at[lead, owner], rss.at[s, number], rrs.at[s, number], to_next)
        cp.start()
        started.append(cp)

    def send_twin(s, number, i, lead, owner, src):
        cp = remote(src, outs[i].at[lead, owner], sss.at[s, number], srs.at[s, number], to_twin)
        cp.start()
        started.append(cp)

    for number, i, lead, k, y in late:
        cp = remote(ins[i], outs[i].at[f, c], yss.at[y], yrs.at[y], ((f + k) % nf, c))
        cp.start()
        started.append(cp)
    for number, i, lead, src in streams:
        send_ring(0, number, i, lead, c, src)
    for number, i, lead, src in streams:
        send_twin(0, number, i, lead, c, src)
        cp = pltpu.make_async_copy(src, outs[i].at[lead, c], own_sem.at[number])
        cp.start()
        own.append(cp)
    everything = [(number, i, lead) for number, i, lead, _ in streams]
    everything += [(number, i, lead) for number, i, lead, _, _ in late]
    for number, i, lead, k, y in late:
        here = outs[i].at[lead, c]
        remote(here, here, yss.at[y], yrs.at[y], to_next).wait_recv()
        send_ring(0, number, i, lead, c, here)
        send_twin(0, number, i, lead, c, here)
    swapped = []
    for i in range(swaps):
        cp = remote(swap_ins[i], swap_outs[i], wss.at[i], wrs.at[i], ((f + 1) % nf, c))
        cp.start()
        swapped.append(cp)
    for s in range(1, n):
        owner = ring.device(p - way * s, core)
        for number, i, lead in everything:
            here = outs[i].at[lead, owner]
            remote(here, here, rss.at[s - 1, number], rrs.at[s - 1, number], to_next).wait_recv()
            if s < n - 1:
                send_ring(s, number, i, lead, owner, here)
            send_twin(s, number, i, lead, owner, here)
    for s in range(n):
        owner = ring.device(p + way * s, 1 - core)
        for number, i, lead in everything:
            here = outs[i].at[lead, owner]
            remote(here, here, sss.at[s, number], srs.at[s, number], to_twin).wait_recv()
    for cp in own:
        cp.wait()
    for cp in started:
        cp.wait_send()
    for cp in swapped:
        cp.wait()


def ring_gather(ring, number, arrays, wide, swaps=()):
    n, nf = ring.chips, ring.nf
    leads = [1 if w else a.shape[0] for a, w in zip(arrays, wide)]
    shapes, streams, late, size = [], 0, 0, 0
    for a, w in zip(arrays, wide):
        if w:
            shapes.append(jax.ShapeDtypeStruct((nf, 2 * n) + a.shape, a.dtype))
            streams += nf
            late += nf - 1
        else:
            shapes.append(jax.ShapeDtypeStruct((a.shape[0], 2 * n) + a.shape[1:], a.dtype))
            streams += a.shape[0]
        size += shapes[-1].size * 2
    dma = pltpu.SemaphoreType.DMA
    shapes += [jax.ShapeDtypeStruct(a.shape, a.dtype) for a in swaps]
    return pl.pallas_call(
        functools.partial(
            gather_kernel, ring, tuple(wide), tuple(leads), len(arrays), len(swaps)
        ),
        out_shape=shapes,
        in_specs=[pl.BlockSpec(memory_space=pl.ANY)] * len(shapes),
        out_specs=[pl.BlockSpec(memory_space=pl.ANY)] * len(shapes),
        scratch_shapes=[
            dma((streams,)),
            dma((max(1, late),)),
            dma((max(1, late),)),
            dma((n - 1, streams)),
            dma((n - 1, streams)),
            dma((n, streams)),
            dma((n, streams)),
            dma((max(1, len(swaps)),)),
            dma((max(1, len(swaps)),)),
        ],
        compiler_params=pltpu.CompilerParams(collective_id=number, has_side_effects=True),
        cost_estimate=pl.CostEstimate(flops=0, bytes_accessed=2 * size, transcendentals=0),
        name="ring_gather_%d" % number,
    )(*arrays, *swaps)


def add_rows(shape, work):
    rows = shape[0]
    step = 16 if rows % 16 == 0 else rows

    def one(r, carry):
        work(pl.ds(pl.multiple_of(r * step, step), step))
        return carry

    lax.fori_loop(0, rows // step, one, 0)


class Products:
    tile = 256

    def __init__(self, cuts, pairs, lefts, rights, outs, held, *rest):
        self.cuts, self.pairs, self.lefts, self.rights, self.outs = cuts, pairs, lefts, rights, outs
        self.held = held
        self.tiles, self.stage, self.load_sem, self.tile_sem, self.store_sem = rest
        self.units = [
            (j, m) for j in range(len(pairs)) for m in range(0, cuts[pairs[j][0]][1], self.tile)
        ]
        self.done, self.loaded, self.stores = 0, set(), [None, None]
        self.ship, self.shipped = {}, []

    def deliver(self):
        for j in sorted(self.ship):
            last = max(i for i, unit in enumerate(self.units) if unit[0] == j)
            if self.done > last + 2 or (self.done == len(self.units) and self.stores == []):
                cp = self.ship.pop(j)()
                cp.start()
                self.shipped.append(cp)

    def fetch(self, number):
        j, m = self.units[number]
        left = self.pairs[j][0]
        source, slot = self.lefts[left], number % 2
        return pltpu.make_async_copy(
            source.at[:, pl.ds(self.cuts[left][0] + m, self.tile)],
            self.tiles.at[slot, pl.ds(0, source.shape[0]), :],
            self.tile_sem.at[slot],
        )

    def start(self):
        self.fetch(0).start()
        self.loads = []
        for i, source in enumerate(self.rights):
            cp = pltpu.make_async_copy(source, self.held[i], self.load_sem.at[i])
            cp.start()
            self.loads.append(cp)

    def run(self, upto):
        while self.done < min(upto, len(self.units)):
            j, m = self.units[self.done]
            left, right, first, width = self.pairs[j]
            if right not in self.loaded:
                self.loads[right].wait()
                self.loaded.add(right)
            self.fetch(self.done).wait()
            if self.done + 1 < len(self.units):
                self.fetch(self.done + 1).start()
            slot = self.done % 2
            value = lax.dot_general(
                self.tiles[slot, pl.ds(0, self.lefts[left].shape[0]), :],
                self.held[right][:, pl.ds(first, width)],
                (((0,), (0,)), ((), ())),
                preferred_element_type=F32,
            )
            if self.stores[slot] is not None:
                self.stores[slot].wait()
            self.stage[slot, :, pl.ds(0, width)] = value.astype(BF)
            cp = pltpu.make_async_copy(
                self.stage.at[slot, :, pl.ds(0, width)],
                self.outs[j].at[pl.ds(m, self.tile), :],
                self.store_sem.at[slot],
            )
            cp.start()
            self.stores[slot] = cp
            self.done += 1
            self.deliver()

    def finish(self):
        self.run(len(self.units))
        for cp in self.stores:
            if cp is not None:
                cp.wait()
        self.stores = []
        self.deliver()
        for cp in self.shipped:
            cp.wait()


def reduce_kernel(ring, wide, leads, count, cuts, pairs, ships, *refs):
    njobs = len(pairs)
    nleft = len(cuts)
    nright = 1 + max([p[1] for p in pairs], default=-1)
    nops = nleft + nright
    ins, sources, refs = refs[:count], refs[count : count + nops], refs[count + nops :]
    outs, job_outs, refs = refs[:count], refs[count : count + njobs], refs[count + njobs :]
    ship_outs, refs = refs[: len(ships)], refs[len(ships) :]
    own, twin, got = (refs[k * count : (1 + k) * count] for k in range(3))
    refs = refs[3 * count :]
    wides = sum(wide)
    finals, ygots = refs[:wides], refs[wides : 2 * wides]
    own_sem, tss, trs, rss, rrs, yss, yrs = refs[2 * wides : 2 * wides + 7]
    refs = refs[2 * wides + 7 :]
    jobs = None
    if njobs:
        jobs = Products(
            cuts, pairs, sources[:nleft], sources[nleft:], job_outs, refs[:nright], *refs[nright : nright + 5]
        )
    f, c, core, p, way = ring.here()
    n, nf = ring.chips, ring.nf
    greet(ring, f, c, core, p, way, any(wide) or len(ships) > 0)
    to_next = (f, ring.device(p + way, core))
    to_twin = (f, c + 1 - 2 * core)

    def remote(src, dst, ss, rs, dev):
        return pltpu.make_async_remote_copy(
            src_ref=src, dst_ref=dst, send_sem=ss, recv_sem=rs, device_id=dev, device_id_type=MESH
        )

    streams = []
    for k in range(max(leads)):
        for i in range(count):
            if k < leads[i]:
                lead = (f + 1 + k) % nf if wide[i] else k
                streams.append((len(streams), i, k, lead))
    started, loads = [], {}
    for s in range(n):
        theirs = ring.device(p + way * (1 + s), 1 - core)
        mine = ring.device(p - way * (1 + s), core)
        for number, i, k, lead in streams:
            cp = remote(
                ins[i].at[lead, theirs], twin[i].at[s, k], tss.at[s, number], trs.at[s, number], to_twin
            )
            cp.start()
            started.append(cp)
            cp = pltpu.make_async_copy(
                ins[i].at[lead, mine], own[i].at[s, k], own_sem.at[s, number]
            )
            cp.start()
            loads[s, number] = cp

    if jobs:
        for w, j in enumerate(ships):
            jobs.ship[j] = functools.partial(
                remote, job_outs[j], ship_outs[w], refs[-2].at[w], refs[-1].at[w], ((f + 1) % nf, c)
            )
        jobs.start()

    def wait_parts(s, number, i, k):
        loads[s, number].wait()
        here = twin[i].at[s, k]
        remote(here, here, tss.at[s, number], trs.at[s, number], to_twin).wait_recv()

    def pass_on(s, number, i, k, src):
        cp = remote(src, got[i].at[s, k], rss.at[s, number], rrs.at[s, number], to_next)
        cp.start()
        started.append(cp)

    turn, turns = 0, (n - 1) * len(streams)
    for s in range(n):
        for number, i, k, lead in streams:
            if jobs and s > 0:
                jobs.run(-(-len(jobs.units) * turn // turns))
                turn += 1
            wait_parts(s, number, i, k)
            mine, other = own[i].at[s, k], twin[i].at[s, k]
            if s == 0:

                def start(rows, mine=mine, other=other):
                    mine[rows, :] = (mine[rows, :].astype(F32) + other[rows, :].astype(F32)).astype(BF)

                add_rows(mine.shape, start)
                pass_on(0, number, i, k, mine)
                continue
            came = got[i].at[s - 1, k]
            remote(came, came, rss.at[s - 1, number], rrs.at[s - 1, number], to_next).wait_recv()
            if s < n - 1:

                def middle(rows, mine=mine, other=other, came=came):
                    total = mine[rows, :].astype(F32) + other[rows, :].astype(F32)
                    came[rows, :] = (came[rows, :].astype(F32) + total).astype(BF)

                add_rows(mine.shape, middle)
                pass_on(s, number, i, k, came)
                continue
            if not wide[i]:
                target = outs[i].at[k]
            elif k == nf - 1:
                target = outs[i]
            else:
                target = finals[sum(wide[:i])].at[k]

            def last(rows, mine=mine, other=other, came=came, target=target):
                total = mine[rows, :].astype(F32) + other[rows, :].astype(F32)
                target[rows, :] = (came[rows, :].astype(F32) + total).astype(target.dtype)

            add_rows(mine.shape, last)
            if wide[i] and k < nf - 1:
                w = sum(wide[:i])
                cp = remote(target, ygots[w].at[k], yss.at[w, k], yrs.at[w, k], ((f + 1 + k) % nf, c))
                cp.start()
                started.append(cp)
    for i in range(count):
        if wide[i]:
            w = sum(wide[:i])
            for k in range(nf - 1):
                here = ygots[w].at[k]
                remote(here, here, yss.at[w, k], yrs.at[w, k], to_next).wait_recv()

                def finish(rows, here=here, target=outs[i]):
                    target[rows, :] = target[rows, :] + here[rows, :].astype(F32)

                add_rows(here.shape, finish)
    if jobs:
        jobs.finish()
    for cp in started:
        cp.wait_send()


def ring_reduce(ring, number, arrays, wide, lefts=(), rights=(), cuts=(), pairs=(), ships=()):
    n, nf = ring.chips, ring.nf
    leads = [a.shape[0] for a in arrays]
    more = [jax.ShapeDtypeStruct((cuts[l][1], width), BF) for l, _, _, width in pairs]
    streams = sum(leads)
    block = [a.shape[2:] for a in arrays]
    shapes = [
        jax.ShapeDtypeStruct(b if w else (l,) + b, F32) for b, w, l in zip(block, wide, leads)
    ]
    dma = pltpu.SemaphoreType.DMA
    scratch = [pltpu.VMEM((n, l) + b, BF) for b, l in zip(block, leads)] * 2
    scratch += [pltpu.VMEM((n - 1, l) + b, BF) for b, l in zip(block, leads)]
    scratch += [pltpu.VMEM((nf - 1,) + b, BF) for b, w in zip(block, wide) if w] * 2
    more += [more[j] for j in ships]
    wides = max(1, sum(wide))
    extra = []
    if pairs:
        extra = [pltpu.VMEM(a.shape, BF) for a in rights]
        extra += [
            pltpu.VMEM((2, max(a.shape[0] for a in lefts), Products.tile), BF),
            pltpu.VMEM((2, Products.tile, max(p[3] for p in pairs)), BF),
            dma((len(rights),)),
            dma((2,)),
            dma((2,)),
        ]
    if ships:
        extra += [dma((len(ships),)), dma((len(ships),))]
    return pl.pallas_call(
        functools.partial(
            reduce_kernel, ring, tuple(wide), tuple(leads), len(arrays), tuple(cuts), tuple(pairs), tuple(ships)
        ),
        out_shape=shapes + more,
        in_specs=[pl.BlockSpec(memory_space=pl.ANY)] * (len(arrays) + len(lefts) + len(rights)),
        out_specs=[pl.BlockSpec(memory_space=pltpu.VMEM)] * len(arrays)
        + [pl.BlockSpec(memory_space=pl.ANY)] * len(more),
        scratch_shapes=scratch
        + [
            dma((n, streams)),
            dma((n, streams)),
            dma((n, streams)),
            dma((n - 1, streams)),
            dma((n - 1, streams)),
            dma((wides, max(1, nf - 1))),
            dma((wides, max(1, nf - 1))),
        ]
        + extra,
        compiler_params=pltpu.CompilerParams(
            collective_id=number, has_side_effects=True, vmem_limit_bytes=60 << 20
        ),
        cost_estimate=pl.CostEstimate(flops=0, bytes_accessed=1 << 20, transcendentals=0),
        name="ring_reduce_%d" % number,
    )(*arrays, *lefts, *rights)


def expert_kernel(nf, experts, fp, bundle_slots, *refs):
    x_ref, g_ref, probs_ref, slot_ref, column_ref = refs[:5]
    weights, refs = refs[5 : 5 + 4 * nf], refs[5 + 4 * nf :]
    back_ref, out_ref, delta_ref, rows_ref, grads_ref, hid_ref, gg_ref, ug_ref, act_ref = refs[:9]
    w_gate, w_up, w_down, w_shared, pre_gate, pre_up, pre_in, pre_s, raw, sems = refs[9:]
    mine = lax.axis_index("ctx")
    held = (w_gate, w_up, w_down, w_shared)
    part = w_gate.shape[0] // nf
    wide = w_gate.shape[0]
    copies = [
        [
            pltpu.make_async_copy(
                weights[4 * k + i], held[i].at[pl.ds(k * part, part)], sems.at[i, k]
            )
            for k in range(nf)
        ]
        for i in range(4)
    ]
    first = pl.program_id(0) == 0

    def ready(i):
        @pl.when(first)
        def _():
            for cp in copies[i]:
                cp.wait()

    @pl.when(first)
    def _():
        for i in (3, 0, 1, 2):
            for cp in copies[i]:
                cp.start()

    def nt(left, right):
        return lax.dot_general(left, right, (((1,), (1,)), ((), ())), preferred_element_type=F32)

    bundles, _, rows = slot_ref.shape
    lane = lax.broadcasted_iota(jnp.int32, (rows, 128), 1)
    own_lane = (lane % experts == mine) & (lane < 3 * experts)
    puts, row_gates = [], []
    for b in range(bundles):
        cut, spot = pl.ds(b * rows, rows), pl.ds(b * bundle_slots, bundle_slots)
        takes = (
            slot_ref[b] == lax.broadcasted_iota(jnp.int32, (bundle_slots, rows), 0)
        ).astype(F32).astype(BF)
        puts.append(
            (
                column_ref[cut, :] == lax.broadcasted_iota(jnp.int32, (rows, bundle_slots), 1)
            ).astype(F32).astype(BF)
        )
        own = jnp.where(own_lane, probs_ref[cut, :].astype(F32), 0.0)
        row_gates.append(jnp.sum(own, axis=1, keepdims=True))
        gate = jnp.sum(multiply(takes, own.astype(BF)), axis=1, keepdims=True)
        for start in range(0, wide, 512):
            piece = pl.ds(start, 512)
            rows_ref[spot, piece] = multiply(takes, x_ref[cut, piece]).astype(BF)
            taken = multiply(takes, g_ref[cut, piece])
            raw[spot, piece] = taken.astype(BF)
            grads_ref[spot, piece] = (gate * taken).astype(BF)

    ready(3)
    pre_s[:, : 2 * fp] = multiply(x_ref[...], w_shared[:, : 2 * fp])
    pre_s[:, 2 * fp :] = multiply(g_ref[...], w_shared[:, 2 * fp :])

    def activate(gate_pre, up_pre, inner):
        sig = jax.nn.sigmoid(gate_pre)
        activated = gate_pre * sig
        hidden = activated * up_pre
        gate_grad = inner * up_pre * sig * (1.0 + gate_pre * (1.0 - sig))
        return hidden.astype(BF), gate_grad.astype(BF), (inner * activated).astype(BF)

    step = 32

    def shared_rows(r, carry):
        at = pl.ds(pl.multiple_of(r * step, step), step)
        for start in range(0, fp, 128):
            cuts = [pl.ds(i * fp + start, 128) for i in range(3)]
            hidden, gate_grad, up_grad = activate(*(pre_s[at, c] for c in cuts))
            act_ref[at, cuts[0]] = gate_grad
            act_ref[at, cuts[1]] = up_grad
            act_ref[at, cuts[2]] = hidden
        return carry

    lax.fori_loop(0, pre_s.shape[0] // step, shared_rows, 0)

    ready(0)
    pre_gate[...] = multiply(rows_ref[...], w_gate[...])
    ready(1)
    pre_up[...] = multiply(rows_ref[...], w_up[...])
    ready(2)
    pre_in[...] = multiply(grads_ref[...], w_down[...])

    def expert_rows(r, carry):
        at = pl.ds(pl.multiple_of(r * step, step), step)
        for start in range(0, hid_ref.shape[1], 128):
            c = pl.ds(start, 128)
            hidden, gate_grad, up_grad = activate(pre_gate[at, c], pre_up[at, c], pre_in[at, c])
            hid_ref[at, c] = hidden
            gg_ref[at, c] = gate_grad
            ug_ref[at, c] = up_grad
        return carry

    lax.fori_loop(0, hid_ref.shape[0] // step, expert_rows, 0)

    delta = 0.0
    for start in range(0, wide, 512):
        piece = pl.ds(start, 512)
        e_back = nt(gg_ref[...], w_gate[piece, :]) + nt(ug_ref[...], w_up[piece, :])
        e_back = e_back.astype(BF)
        e_out = nt(hid_ref[...], w_down[piece, :]).astype(BF)
        delta = delta + jnp.sum(
            raw[:, piece].astype(F32) * e_out.astype(F32), axis=1, keepdims=True
        )
        for b in range(bundles):
            cut = pl.ds(b * rows, rows)
            spot = slice(b * bundle_slots, (b + 1) * bundle_slots)
            s_back = nt(act_ref[cut, : 2 * fp], w_shared[piece, : 2 * fp])
            back_ref[cut, piece] = (multiply(puts[b], e_back[spot]) + s_back).astype(BF)
            s_out = nt(act_ref[cut, 2 * fp :], w_shared[piece, 2 * fp :])
            out_ref[cut, piece] = (row_gates[b] * multiply(puts[b], e_out[spot]) + s_out).astype(BF)
    for b in range(bundles):
        own = delta[b * bundle_slots : (b + 1) * bundle_slots]
        high = own.astype(BF).astype(F32)
        middle = (own - high).astype(BF).astype(F32)
        low = own - high - middle
        spread = jnp.where(lane[:bundle_slots] < experts, high, jnp.where(lane[:bundle_slots] < 2 * experts, middle, low))
        spread = jnp.where(own_lane[:bundle_slots], spread, 0.0).astype(BF)
        delta_ref[pl.ds(b * rows, rows), :] = multiply(puts[b], spread).astype(BF)


def run_experts(nf, experts, capacity, tok_loc, tree_rows, tree_grads, tree_probs, slot, weights):
    rows, wide = tree_rows.shape
    bundles, per = slot.shape
    bundle_slots = capacity * (per // tok_loc)
    hidden, fp = weights[0][0].shape[1], weights[0][3].shape[1] // 3
    group = 2 if bundles % 2 == 0 else 1
    steps = bundles // group
    block, slots = rows // steps, group * bundle_slots
    flat = [w for piece in weights for w in piece]
    by_row = lambda width: pl.BlockSpec((block, width), lambda i: (i, 0))
    by_slot = lambda width: pl.BlockSpec((slots, width), lambda i: (i, 0))
    any_spec = pl.BlockSpec(memory_space=pl.ANY)
    shape = lambda n, width: jax.ShapeDtypeStruct((n, width), BF)
    total = steps * slots
    flops = 2 * (6 * total * wide * hidden + 6 * rows * wide * fp + 4 * rows * bundle_slots * wide)
    return pl.pallas_call(
        functools.partial(expert_kernel, nf, experts, fp, bundle_slots),
        grid=(steps,),
        out_shape=[shape(rows, wide), shape(rows, wide), shape(rows, 128)]
        + [shape(total, wide)] * 2
        + [shape(total, hidden)] * 3
        + [shape(rows, 3 * fp)],
        in_specs=[
            by_row(wide),
            by_row(wide),
            by_row(128),
            pl.BlockSpec((group, 1, per), lambda i: (i, 0, 0)),
            pl.BlockSpec((block, 1), lambda i: (i, 0)),
        ]
        + [any_spec] * len(flat),
        out_specs=[by_row(wide), by_row(wide), by_row(128)]
        + [by_slot(wide)] * 2
        + [by_slot(hidden)] * 3
        + [by_row(3 * fp)],
        scratch_shapes=[pltpu.VMEM((wide, hidden), BF)] * 3
        + [pltpu.VMEM((wide, 3 * fp), BF)]
        + [pltpu.VMEM((slots, hidden), F32)] * 3
        + [pltpu.VMEM((block, 3 * fp), F32), pltpu.VMEM((slots, wide), BF)]
        + [pltpu.SemaphoreType.DMA((4, nf))],
        compiler_params=pltpu.CompilerParams(vmem_limit_bytes=61 << 20),
        cost_estimate=pl.CostEstimate(
            flops=flops, bytes_accessed=10 * rows * wide, transcendentals=total * hidden
        ),
        name="experts",
    )(tree_rows, tree_grads, tree_probs, slot[:, None, :], slot.reshape(rows, 1), *flat)


def nt(left, right):
    return lax.dot_general(left, right, (((1,), (1,)), ((), ())), preferred_element_type=F32)


def tn(left, right):
    return lax.dot_general(left, right, (((0,), (0,)), ((), ())), preferred_element_type=F32)


HEADS = 4


def attend_kernel(scale, nope, rope, keys, allowed, expand, tokens, w_hbm, cat, lse, mixed, heads, residual, w_out, sem):
    trees, tok = cat.shape[0], cat.shape[2]
    copy = pltpu.make_async_copy(w_hbm, w_out, sem)
    copy.start()
    for h in range(H):
        low = nt(nope[:, h * DN : (h + 1) * DN], expand[:, h * (DN + DV) : h * (DN + DV) + DN])
        low = low.astype(BF)
        for b in range(trees):
            rows = slice(b * tok, (b + 1) * tok)
            cat[b, h, :, :LAT] = low[rows]
            cat[b, h, :, LAT:] = rope[rows, h * 128 : (h + 1) * 128]

    def group(i, carry):
        b, g = i // (H // HEADS), i % (H // HEADS) * HEADS
        query = cat[b, pl.ds(g, HEADS)].reshape(HEADS * tok, -1)
        scores = nt(query, keys[b]) * scale
        scores = scores.reshape(HEADS, tok, -1)
        scores = jnp.where(allowed[b][None] > 0, scores, -1e30)
        highest = jnp.max(scores, axis=-1, keepdims=True)
        raised = jnp.exp(scores - highest)
        total = jnp.sum(raised, axis=-1, keepdims=True)
        lse[b, pl.ds(g, HEADS)] = highest + jnp.log(total)
        probs = (raised * (1.0 / total)).astype(BF).reshape(HEADS * tok, -1)
        mix = multiply(probs, keys[b, :, :LAT]).astype(BF)
        mixed[b, pl.ds(g, HEADS)] = mix.reshape(HEADS, tok, LAT)
        return carry

    lax.fori_loop(0, trees * (H // HEADS), group, 0)
    for h in range(H):
        mix = jnp.concatenate([mixed[b, h] for b in range(trees)], axis=0)
        value = expand[:, h * (DN + DV) + DN : (h + 1) * (DN + DV)]
        heads[:, h * DV : (h + 1) * DV] = multiply(mix, value).astype(BF)
    copy.wait()
    for start in range(0, D, 512):
        cut = slice(start, start + 512)
        residual[:, cut] = tokens[:, cut].astype(F32) + multiply(heads[...], w_out[:, cut])


def attend(nope, rope, keys, allowed, expand, tokens, w_output, tok, scale):
    rows = tokens.shape[0]
    trees = rows // tok
    vmem = pl.BlockSpec(memory_space=pltpu.VMEM)
    length, width = keys.shape[1:]
    return pl.pallas_call(
        functools.partial(attend_kernel, scale),
        out_shape=[
            jax.ShapeDtypeStruct((trees, H, tok, width), BF),
            jax.ShapeDtypeStruct((trees, H, tok, 1), F32),
            jax.ShapeDtypeStruct((trees, H, tok, LAT), BF),
            jax.ShapeDtypeStruct((rows, H * DV), BF),
            jax.ShapeDtypeStruct((rows, D), F32),
        ],
        in_specs=[vmem] * 6 + [pl.BlockSpec(memory_space=pl.ANY)],
        out_specs=[vmem] * 5,
        scratch_shapes=[pltpu.VMEM(w_output.shape, BF), pltpu.SemaphoreType.DMA],
        compiler_params=pltpu.CompilerParams(vmem_limit_bytes=56 << 20),
        cost_estimate=pl.CostEstimate(
            flops=2 * rows * H * length * 1152, bytes_accessed=30 << 20, transcendentals=rows * H * length
        ),
        name="attend",
    )(nope, rope, keys, allowed, expand, tokens, w_output)


def attend_back_kernel(
    scale, grad, w_out, expand, cat, keys, lse, allowed, mixed, nope, keys_grad, nope_grad, rope_grad,
    expand_grad, heads_grad, mix_grad, low_probs, score_grad, cat_grad,
):
    trees, tok = cat.shape[0], cat.shape[2]
    for start in range(0, H * DV, 512):
        heads_grad[:, start : start + 512] = nt(grad[...], w_out[start : start + 512, :]).astype(BF)
    for h in range(H):
        value = expand[:, h * (DN + DV) + DN : (h + 1) * (DN + DV)]
        own = heads_grad[:, h * DV : (h + 1) * DV]
        back = nt(own, value).astype(BF)
        for b in range(trees):
            mix_grad[b, h] = back[b * tok : (b + 1) * tok]
        mix = jnp.concatenate([mixed[b, h] for b in range(trees)], axis=0)
        expand_grad[:, h * (DN + DV) + DN : (h + 1) * (DN + DV)] = tn(mix, own).astype(BF)
    for b in range(trees):

        def group(i, carry, b=b):
            g = i * HEADS
            rows = pl.ds(pl.multiple_of(g * tok, HEADS * tok), HEADS * tok)
            query = cat[b, pl.ds(g, HEADS)].reshape(HEADS * tok, -1)
            mix = mix_grad[b, pl.ds(g, HEADS)].reshape(HEADS * tok, -1)
            scores = (nt(query, keys[b]) * scale).reshape(HEADS, tok, -1)
            probs = jnp.where(
                allowed[b][None] > 0, jnp.exp(scores - lse[b, pl.ds(g, HEADS)]), 0.0
            ).reshape(HEADS * tok, -1)
            prob_grad = nt(mix, keys[b, :, :LAT])
            centre = jnp.sum(probs * prob_grad, axis=-1, keepdims=True)
            low_probs[rows, :] = probs.astype(BF)
            own = (probs * (prob_grad - centre)).astype(BF)
            score_grad[rows, :] = own
            back = (multiply(own, keys[b]) * scale).reshape(HEADS, tok, -1)
            cat_grad[b, pl.ds(g, HEADS)] = back[..., :LAT].astype(BF)
            for k in range(HEADS):
                rope_grad[b, g + k] = back[k, :, LAT:]
            return carry

        lax.fori_loop(0, H // HEADS, group, 0)
        query = cat[b].reshape(H * tok, -1)
        mix = mix_grad[b].reshape(H * tok, -1)
        length = keys.shape[1]
        for start in range(0, length, 256):
            cut = slice(start, start + 256)
            total = tn(score_grad[:, cut], query) * scale
            keys_grad[b, cut, :LAT] = (total[:, :LAT] + tn(low_probs[:, cut], mix)).astype(BF)
            keys_grad[b, cut, LAT:] = total[:, LAT:].astype(BF)
    for h in range(H):
        low = jnp.concatenate([cat_grad[b, h] for b in range(trees)], axis=0)
        key = expand[:, h * (DN + DV) : h * (DN + DV) + DN]
        nope_grad[:, h * DN : (h + 1) * DN] = multiply(low, key)
        expand_grad[:, h * (DN + DV) : h * (DN + DV) + DN] = tn(
            low, nope[:, h * DN : (h + 1) * DN]
        ).astype(BF)


def attend_back(grad, w_output, expand, cat, keys, lse, allowed, mixed, nope, scale):
    trees, _, tok, width = cat.shape
    length, rows = keys.shape[1], grad.shape[0]
    vmem = pl.BlockSpec(memory_space=pltpu.VMEM)
    return pl.pallas_call(
        functools.partial(attend_back_kernel, scale),
        out_shape=[
            jax.ShapeDtypeStruct(keys.shape, BF),
            jax.ShapeDtypeStruct((rows, H * DN), F32),
            jax.ShapeDtypeStruct((trees, H, tok, width - LAT), F32),
            jax.ShapeDtypeStruct(expand.shape, BF),
        ],
        in_specs=[vmem] * 9,
        out_specs=[vmem] * 4,
        scratch_shapes=[
            pltpu.VMEM((rows, H * DV), BF),
            pltpu.VMEM((trees, H, tok, LAT), BF),
            pltpu.VMEM((H * tok, length), BF),
            pltpu.VMEM((H * tok, length), BF),
            pltpu.VMEM((trees, H, tok, LAT), BF),
        ],
        compiler_params=pltpu.CompilerParams(vmem_limit_bytes=60 << 20),
        cost_estimate=pl.CostEstimate(
            flops=0, bytes_accessed=1 << 20, transcendentals=0
        ),
        name="attend_back",
    )(grad, w_output, expand, cat, keys, lse, allowed, mixed, nope)


def body(
    tokens,
    out_grad,
    segments,
    path_mask,
    expert_ids,
    norm_attn,
    attn_q,
    attn_kva,
    norm_latent,
    attn_kvb,
    attn_out,
    norm_ffn,
    router,
    expert_gate,
    expert_up,
    expert_down,
    shared_gate,
    shared_up,
    shared_down,
):
    trees, tok_loc = tokens.shape[:2]
    row_total = trees * tok_loc
    nc, nf = lax.axis_size("ctx"), lax.axis_size("fsdp")
    mine, group = lax.axis_index("ctx"), lax.axis_index("fsdp")
    experts = nc
    ring = Ring(nf, nc)
    tree_len = tok_loc * nc
    group_rows = trees * tree_len
    first_row = mine * tok_loc
    capacity = min(tok_loc, tok_loc * TOP * 4 // (3 * experts))
    slot_total = nc * trees * capacity
    score_scale = 1.0 / math.sqrt(DN + DR)
    frequency = rope_base ** (-(jnp.arange(DR // 2, dtype=F32) * 2.0 / DR))
    labels = jnp.arange(experts, dtype=jnp.int32)
    both = ("fsdp", "ctx")
    part = D // nf

    def roll_in(x):
        return lax.dynamic_slice_in_dim(jnp.concatenate([x, x], axis=-1), group * part, D, x.ndim - 1)

    def roll_out(x):
        return lax.dynamic_slice_in_dim(
            jnp.concatenate([x, x], axis=-1), (nf - group) % nf * part, D, x.ndim - 1
        )

    def fetch(w):
        pieces = [w]
        for k in range(1, nf):
            pieces.append(lax.ppermute(w, "fsdp", [(i, (i - k) % nf) for i in range(nf)]))
        return pieces

    fs = shared_gate.shape[1]
    fp = -(-fs // 128) * 128
    shared_w = jnp.concatenate(
        [jnp.pad(w, ((0, 0), (0, fp - fs))) for w in (shared_gate, shared_up, shared_down)], axis=1
    )
    small = jnp.concatenate(
        [
            norm_attn,
            norm_ffn,
            norm_latent,
            router.reshape(-1),
            expert_ids.astype(BF).reshape(-1),
        ]
    )
    small = jnp.pad(small, (0, PACK - small.shape[0])).reshape(16, PACK // 16)
    if nf == 2:
        w_latent, w_query, w_expand, small_all, w_output, other_gate, other_shared = ring_gather(
            ring, 0, [attn_kva, attn_q, attn_kvb, small, attn_out], [True] * 5, [expert_gate, shared_w]
        )
        e_gate, s_all = [expert_gate, other_gate], [shared_w, other_shared]
        later_up, later_down, later_grads, small_all = lax.optimization_barrier(
            (expert_up, expert_down, out_grad, small_all)
        )
    else:
        w_latent, w_query, w_expand, small_all, w_output = (
            lax.all_gather(w, both, axis=0) for w in (attn_kva, attn_q, attn_kvb, small, attn_out)
        )
        e_gate, s_all = fetch(expert_gate), fetch(shared_w)
        later_up, later_down, later_grads = expert_up, expert_down, out_grad
    e_up, e_down = fetch(later_up), fetch(later_down)
    w_output = w_output.reshape(H * DV, D)
    w_latent, w_query = w_latent.reshape(D, -1), w_query.reshape(D, -1)
    w_expand = w_expand.reshape(LAT, -1)
    small_all = small_all.reshape(nf * nc, PACK)
    r_one, r_lat, r_router = norm_attn.shape[0], norm_latent.shape[0], router.size
    cuts = [0, r_one, 2 * r_one, 2 * r_one + r_lat, 2 * r_one + r_lat + r_router]
    gain_attn = small_all[:, cuts[0] : cuts[1]].reshape(-1).astype(F32)
    gain_ffn = small_all[:, cuts[1] : cuts[2]].reshape(-1).astype(F32)
    gain_latent = small_all[:, cuts[2] : cuts[3]].reshape(-1).astype(F32)
    w_router = small_all[:, cuts[3] : cuts[4]].reshape(D, experts)
    ids_all = lax.dynamic_slice_in_dim(small_all.reshape(nf, nc, PACK), group, 1, 0)[0]
    ids_all = ids_all[:, cuts[4] : cuts[4] + expert_ids.size].reshape(nc, trees, tok_loc, TOP)
    ids_all = ids_all.transpose(1, 0, 2, 3).reshape(group_rows, TOP)

    upstream_low = out_grad.reshape(row_total, D)
    upstream = upstream_low.astype(F32)
    tree_grads = lax.all_gather(roll_in(later_grads), "ctx", axis=1, tiled=True).reshape(group_rows, D)

    def one_mask(segment_ids, path_table):
        return tree_mask(segment_ids, path_table, first_row, tok_loc)

    allowed, positions = jax.vmap(one_mask)(segments, path_mask)
    rotation = positions.astype(F32)[:, :, None] * frequency[None, None, :]
    cosine, sine = jnp.cos(rotation), jnp.sin(rotation)
    inputs = tokens.astype(F32).reshape(row_total, D)
    normed_in, inverse_in, gained_in = normalize(inputs, gain_attn)
    hidden_in = gained_in.astype(BF)
    latent_all = multiply(hidden_in, w_latent)
    latent_normed, latent_inverse, latent_gained = normalize(latent_all[:, :LAT], gain_latent)
    key_latent = latent_gained.astype(BF).reshape(trees, tok_loc, LAT)
    key_rope = rotate(latent_all[:, LAT:].reshape(trees, tok_loc, DR), cosine, sine).astype(BF)
    key_pad = jnp.zeros((trees, tok_loc, 128 - DR), BF)
    (keys,) = ring_gather(
        ring, 1, [jnp.concatenate([key_latent, key_rope, key_pad], axis=-1)], [False]
    )
    keys = keys.reshape(trees, tree_len, LAT + 128)
    query_all = lax.optimization_barrier(multiply(hidden_in, w_query))
    query_all = query_all.reshape(trees, tok_loc, H, DN + DR)
    query_nope = query_all[..., :DN].astype(BF).reshape(row_total, H * DN)
    query_rope = rotate(
        query_all[..., DN:], cosine[:, :, None, :], sine[:, :, None, :]
    ).astype(BF)
    query_rope = jnp.pad(query_rope, ((0, 0), (0, 0), (0, 0), (0, 128 - DR)))
    allowed = allowed.astype(F32)
    query_cat, log_total, mixed, heads, residual = attend(
        query_nope,
        query_rope.reshape(row_total, H * 128),
        keys,
        allowed,
        w_expand,
        tokens.reshape(row_total, D),
        w_output,
        tok_loc,
        score_scale,
    )
    normed_mid, inverse_mid, gained_mid = normalize(residual, gain_ffn)
    hidden_mid = gained_mid.astype(BF)
    expert_probs = jax.nn.softmax(multiply(hidden_mid, w_router), axis=-1)

    probs_parts = jnp.concatenate(three_parts(expert_probs), axis=-1)
    probs_parts = jnp.pad(probs_parts, ((0, 0), (0, 128 - 3 * experts)))
    tree_rows, tree_probs = ring_gather(
        ring,
        2,
        [roll_in(hidden_mid).reshape(trees, tok_loc, D), probs_parts.reshape(trees, tok_loc, 128)],
        [False, False],
    )
    tree_rows = tree_rows.reshape(group_rows, D)
    tree_probs = tree_probs.reshape(group_rows, 128)

    member = jnp.any(ids_all == mine.astype(BF), axis=1)
    blocks = trees * nc
    bundle = 4 if blocks % 4 == 0 else 1
    bundles = blocks // bundle
    grid = member.astype(BF).reshape(blocks, tok_loc)
    upper = (jnp.arange(tok_loc)[:, None] <= jnp.arange(tok_loc)[None, :]).astype(BF)
    slot = multiply(grid, upper).astype(jnp.int32) - 1
    slot = slot + (jnp.arange(blocks, dtype=jnp.int32) % bundle * capacity)[:, None]
    slot = jnp.where(grid > 0, slot, -1).reshape(bundles, bundle * tok_loc)
    back, out_part, delta_out, e_rows, e_grads, e_hidden, e_gg, e_ug, s_act = run_experts(
        nf,
        experts,
        capacity,
        tok_loc,
        tree_rows,
        tree_grads,
        tree_probs,
        slot,
        list(zip(e_gate, e_up, e_down, s_all)),
    )

    def weight_grads(k, e_gg, e_ug, e_hidden, s_act):
        cut = slice(k * part, (k + 1) * part)
        return (
            transposed_multiply(tree_rows[:, cut], s_act[:, : 2 * fp]),
            transposed_multiply(tree_grads[:, cut], s_act[:, 2 * fp :]),
            transposed_multiply(e_rows[:, cut], e_gg),
            transposed_multiply(e_rows[:, cut], e_ug),
            transposed_multiply(e_grads[:, cut], e_hidden),
        )

    job_arrays = [e_rows, e_grads, tree_rows, tree_grads], [e_gg, e_ug, e_hidden, s_act]
    job_pairs = [
        (2, 3, 0, 2 * fp),
        (3, 3, 2 * fp, fp),
        (0, 0, 0, e_gg.shape[1]),
        (0, 1, 0, e_gg.shape[1]),
        (1, 2, 0, e_gg.shape[1]),
    ]

    def job_cuts(k):
        return [(k * part, part)] * 4

    def by_owner(x):
        return x.reshape(trees, nc, tok_loc, x.shape[-1])

    if nf == 2:
        back_sum, delta_sum, *sent = ring_reduce(
            ring,
            3,
            [by_owner(back), by_owner(delta_out)],
            [False] * 2,
            *job_arrays,
            job_cuts(1),
            job_pairs,
            (0, 1),
        )
        there, sent = sent[5:], sent[2:5]
    else:
        back_sum, delta_sum = ring_reduce(
            ring, 3, [by_owner(back), by_owner(delta_out)], [False] * 2
        )
    back_sum, out_part = lax.optimization_barrier((back_sum, out_part))
    back_sum = roll_out(back_sum.reshape(row_total, D))
    prob_delta = jnp.sum(
        delta_sum.reshape(row_total, 128)[:, : 3 * experts].reshape(row_total, 3, experts), axis=1
    )
    out_sum = lax.psum_scatter(
        out_part.reshape(trees, tree_len, D), "ctx", scatter_dimension=1, tiled=True
    )

    came = []
    for k in range(1, nf):
        perm = [(i, (i + k) % nf) for i in range(nf)]
        grads = sent if nf == 2 else weight_grads(k, e_gg, e_ug, e_hidden, s_act)
        came.append([lax.ppermute(g.astype(BF), "fsdp", perm) for g in grads])
    if nf == 2:
        came[0] = list(there) + came[0]

    logit_grad = (
        expert_probs * (prob_delta - jnp.sum(expert_probs * prob_delta, axis=-1, keepdims=True))
    ).astype(BF)
    grad_router = transposed_multiply(hidden_mid, logit_grad)
    mid_grad = back_sum + multiply_transposed(logit_grad, w_router)
    mid_input, grad_gain_ffn = normalize_back(mid_grad, normed_mid, inverse_mid, gain_ffn)
    residual_grad = upstream + mid_input
    residual_low = residual_grad.astype(BF)
    keys_grad, qnope_grad, qrope_grad, grad_expand = attend_back(
        residual_low,
        w_output,
        w_expand,
        query_cat,
        keys,
        log_total,
        allowed,
        mixed,
        query_nope,
        score_scale,
    )
    qrope_grad = qrope_grad[..., :DR].transpose(0, 2, 1, 3)
    query_grad = jnp.concatenate(
        [
            qnope_grad.reshape(trees, tok_loc, H, DN),
            rotate(qrope_grad, cosine[:, :, None, :], -sine[:, :, None, :]),
        ],
        axis=-1,
    )
    query_grad = query_grad.astype(BF).reshape(row_total, H * (DN + DR))
    own_keys_grad, grad_query, grad_output = ring_reduce(
        ring,
        4,
        [keys_grad.reshape(trees, nc, tok_loc, LAT + 128)],
        [False],
        [hidden_in, heads],
        [query_grad, residual_low],
        [(0, D), (0, H * DV)],
        [(0, 0, 0, query_grad.shape[1]), (1, 1, 0, D)],
    )
    own_keys_grad, out_sum = lax.optimization_barrier((own_keys_grad, out_sum))
    out_sum = roll_out(out_sum.reshape(row_total, D).astype(F32))
    output = (residual + out_sum).astype(BF).reshape(trees, tok_loc, D)
    hidden_grad = multiply_transposed(query_grad, w_query)
    latent_in_grad, grad_gain_latent = normalize_back(
        own_keys_grad[..., :LAT].reshape(row_total, LAT), latent_normed, latent_inverse, gain_latent
    )
    rope_back = rotate(own_keys_grad[..., LAT : LAT + DR], cosine, -sine).reshape(row_total, DR)
    latent_grad = jnp.concatenate([latent_in_grad, rope_back], axis=-1).astype(BF)
    grad_latent = transposed_multiply(hidden_in, latent_grad)
    hidden_grad = hidden_grad + multiply_transposed(latent_grad, w_latent)
    input_part, grad_gain_attn = normalize_back(hidden_grad, normed_in, inverse_in, gain_attn)
    input_grad = (input_part + residual_grad).reshape(trees, tok_loc, D)

    grad_small = jnp.concatenate(
        [
            grad_gain_attn.reshape(nf * nc, r_one),
            grad_gain_ffn.reshape(nf * nc, r_one),
            grad_gain_latent.reshape(nf * nc, r_lat),
            grad_router.reshape(nf * nc, r_router),
        ],
        axis=1,
    ).astype(BF)
    grad_small = jnp.pad(grad_small, ((0, 0), (0, PACK - grad_small.shape[1])))
    parts = [
        grad_query.reshape(nf, nc, -1, w_query.shape[1]),
        grad_expand.reshape(nf, nc, -1, w_expand.shape[1]),
        grad_latent.astype(BF).reshape(nf, nc, -1, w_latent.shape[1]),
        grad_small.reshape(nf, nc, 16, PACK // 16),
        grad_output.reshape(nf, nc, -1, D),
    ]
    if nf == 2:
        t_query, t_expand, t_latent, t_small, out_total, *ffn_sums = ring_reduce(
            ring, 5, parts, [True] * 5, *job_arrays, job_cuts(0), job_pairs
        )
        came, ffn_sums = lax.optimization_barrier((came, ffn_sums))
    else:
        t_query, t_expand, t_latent, t_small, out_total = (
            lax.psum_scatter(
                x.reshape((nf * nc,) + x.shape[2:]), both, scatter_dimension=0, tiled=True
            )[0].astype(F32)
            for x in parts
        )
        ffn_sums = weight_grads(0, e_gg, e_ug, e_hidden, s_act)
    t_small = t_small.reshape(PACK)
    for one in came:
        ffn_sums = [a.astype(F32) + b.astype(F32) for a, b in zip(ffn_sums, one)]
    e_sums = ffn_sums[2:]
    s_sums = [ffn_sums[0][:, :fs], ffn_sums[0][:, fp : fp + fs], ffn_sums[1][:, :fs]]
    return (
        output,
        input_grad,
        t_small[cuts[0] : cuts[1]],
        t_query,
        t_latent,
        t_small[cuts[2] : cuts[3]],
        t_expand,
        out_total,
        t_small[cuts[1] : cuts[2]],
        t_small[cuts[3] : cuts[4]].reshape(-1, experts),
        *e_sums,
        *s_sums,
    )


def solution(mesh):
    placed = (
        P("fsdp", "ctx", None),
        P("fsdp", "ctx", None),
        P("fsdp", None),
        P("fsdp", None, None),
        P("fsdp", "ctx", None),
        P(("fsdp", "ctx")),
        P(("fsdp", "ctx"), None),
        P(("fsdp", "ctx"), None),
        P(("fsdp", "ctx")),
        P(("fsdp", "ctx"), None),
        P(("fsdp", "ctx"), None),
        P(("fsdp", "ctx")),
        P(("fsdp", "ctx"), None),
        P("fsdp", "ctx"),
        P("fsdp", "ctx"),
        P("fsdp", "ctx"),
        P("fsdp", "ctx"),
        P("fsdp", "ctx"),
        P("fsdp", "ctx"),
    )
    return jax.shard_map(
        body,
        mesh=mesh,
        in_specs=placed,
        out_specs=(
            P("fsdp", "ctx", None),
            P("fsdp", "ctx", None),
            P(("fsdp", "ctx")),
            P(("fsdp", "ctx"), None),
            P(("fsdp", "ctx"), None),
            P(("fsdp", "ctx")),
            P(("fsdp", "ctx"), None),
            P(("fsdp", "ctx"), None),
            P(("fsdp", "ctx")),
            P(("fsdp", "ctx"), None),
            P("fsdp", "ctx"),
            P("fsdp", "ctx"),
            P("fsdp", "ctx"),
            P("fsdp", "ctx"),
            P("fsdp", "ctx"),
            P("fsdp", "ctx"),
        ),
        check_vma=False,
    )
```

```python
import functools
import math

import jax
import jax.numpy as jnp
from jax import lax
from jax.experimental import pallas as pl
from jax.experimental.pallas import tpu as pltpu
from jax.sharding import PartitionSpec as P

D = 2048
H = 16
DN = 128
DR = 64
DV = 128
LAT = 512
TOP = 6
SEGS = 13
PACK = 2048

MESH = pl.DeviceIdType.MESH
BF = jnp.bfloat16
F32 = jnp.float32

epsilon = 1e-06
rope_base = 10000.0


def multiply(left, right):
    return jnp.dot(left, right, preferred_element_type=F32)


def multiply_transposed(left, right):
    return lax.dot_general(left, right, (((1,), (1,)), ((), ())), preferred_element_type=F32)


def transposed_multiply(left, right):
    return lax.dot_general(left, right, (((0,), (0,)), ((), ())), preferred_element_type=F32)


def normalize(tensor_in, gain_vec):
    inverse = lax.rsqrt(jnp.mean(tensor_in * tensor_in, axis=-1, keepdims=True) + epsilon)
    normed = tensor_in * inverse
    return (normed, inverse, normed * gain_vec)


def normalize_back(grad_out, normed, inverse, gain_vec):
    weighted = grad_out * gain_vec
    centre = jnp.mean(weighted * normed, axis=-1, keepdims=True)
    return (inverse * (weighted - normed * centre), jnp.sum(grad_out * normed, axis=0))


def rotate(tensor_in, cosine, sine):
    half_width = tensor_in.shape[-1] // 2
    former = tensor_in[..., :half_width]
    latter = tensor_in[..., half_width:]
    return jnp.concatenate(
        [former * cosine - latter * sine, latter * cosine + former * sine], axis=-1
    )


def tree_mask(segment_ids, path_table, first_row, row_count):
    labels = jnp.arange(SEGS, dtype=jnp.int32)
    own_ids = lax.dynamic_slice_in_dim(segment_ids, first_row, row_count)
    own_hot = (own_ids[:, None] == labels[None, :]).astype(BF)
    all_hot = (segment_ids[:, None] == labels[None, :]).astype(BF)
    ancestry = multiply(own_hot, path_table.astype(BF)).astype(BF)
    related = multiply_transposed(ancestry, all_hot)
    places = jnp.arange(segment_ids.shape[0], dtype=jnp.int32)
    queries = first_row + jnp.arange(row_count, dtype=jnp.int32)
    allowed = (related > 0) & (places[None, :] <= queries[:, None])
    positions = jnp.sum(allowed.astype(jnp.int32), axis=1) - 1
    return (allowed, positions)


def three_parts(value):
    first = lax.reduce_precision(value, 8, 7)
    second = lax.reduce_precision(value - first, 8, 7)
    third = value - first - second
    return (first.astype(BF), second.astype(BF), third.astype(BF))


class Ring:
    def __init__(self, nf, nc):
        self.nf, self.chips = nf, nc // 2
        half = self.chips // 2
        if nf == 2:
            self.place = lambda p: (1 - p // half) * 2 * p + (p // half) * (4 * half - 1 - 2 * p)
            self.where = lambda j: (1 - j % 2) * (j // 2) + (j % 2) * (2 * half - 1 - j // 2)
        else:
            self.place = lambda p: (1 - p // half) * p + (p // half) * (3 * half - 1 - p)
            self.where = self.place

    def here(self):
        f, c = lax.axis_index("fsdp"), lax.axis_index("ctx")
        core = c % 2
        return f, c, core, self.where(c // 2), 1 - 2 * core

    def device(self, position, core):
        return self.place((position + 2 * self.chips) % self.chips) * 2 + core


def greet(ring, f, c, core, p, way, over_fsdp):
    barrier = pltpu.get_barrier_semaphore()
    targets = [(f, ring.device(p - way, core)), (f, c + 1 - 2 * core)]
    if over_fsdp:
        targets += [((f + k) % ring.nf, c) for k in range(1, ring.nf)]
    for target in targets:
        pl.semaphore_signal(barrier, inc=1, device_id=target, device_id_type=MESH)
    pl.semaphore_wait(barrier, len(targets))


def gather_kernel(ring, wide, leads, count, swaps, *refs):
    swap_ins, swap_outs = refs[count : count + swaps], refs[2 * count + swaps : 2 * (count + swaps)]
    ins, outs = refs[:count], refs[count + swaps : 2 * count + swaps]
    own_sem, yss, yrs, rss, rrs, sss, srs, wss, wrs = refs[2 * (count + swaps) :]
    f, c, core, p, way = ring.here()
    n, nf = ring.chips, ring.nf
    greet(ring, f, c, core, p, way, any(wide))
    to_next = (f, ring.device(p + way, core))
    to_twin = (f, c + 1 - 2 * core)
    started, own = [], []

    def remote(src, dst, ss, rs, dev):
        return pltpu.make_async_remote_copy(
            src_ref=src, dst_ref=dst, send_sem=ss, recv_sem=rs, device_id=dev, device_id_type=MESH
        )

    streams, late = [], []
    number = 0
    for i in range(count):
        if wide[i]:
            streams.append((number, i, f, ins[i]))
            number += 1
        else:
            for a in range(leads[i]):
                streams.append((number, i, a, ins[i].at[a]))
                number += 1
    first = len(streams)
    yn = 0
    for i in range(count):
        if wide[i]:
            for k in range(1, nf):
                late.append((number, i, (f - k + nf) % nf, k, yn))
                number += 1
                yn += 1

    def send_ring(s, number, i, lead, owner, src):
        cp = remote(src, outs[i].at[lead, owner], rss.at[s, number], rrs.at[s, number], to_next)
        cp.start()
        started.append(cp)

    def send_twin(s, number, i, lead, owner, src):
        cp = remote(src, outs[i].at[lead, owner], sss.at[s, number], srs.at[s, number], to_twin)
        cp.start()
        started.append(cp)

    for number, i, lead, k, y in late:
        cp = remote(ins[i], outs[i].at[f, c], yss.at[y], yrs.at[y], ((f + k) % nf, c))
        cp.start()
        started.append(cp)
    for number, i, lead, src in streams:
        send_ring(0, number, i, lead, c, src)
    for number, i, lead, src in streams:
        send_twin(0, number, i, lead, c, src)
        cp = pltpu.make_async_copy(src, outs[i].at[lead, c], own_sem.at[number])
        cp.start()
        own.append(cp)
    everything = [(number, i, lead) for number, i, lead, _ in streams]
    everything += [(number, i, lead) for number, i, lead, _, _ in late]
    for number, i, lead, k, y in late:
        here = outs[i].at[lead, c]
        remote(here, here, yss.at[y], yrs.at[y], to_next).wait_recv()
        send_ring(0, number, i, lead, c, here)
        send_twin(0, number, i, lead, c, here)
    swapped = []
    for i in range(swaps):
        cp = remote(swap_ins[i], swap_outs[i], wss.at[i], wrs.at[i], ((f + 1) % nf, c))
        cp.start()
        swapped.append(cp)
    for s in range(1, n):
        owner = ring.device(p - way * s, core)
        for number, i, lead in everything:
            here = outs[i].at[lead, owner]
            remote(here, here, rss.at[s - 1, number], rrs.at[s - 1, number], to_next).wait_recv()
            if s < n - 1:
                send_ring(s, number, i, lead, owner, here)
            send_twin(s, number, i, lead, owner, here)
    for s in range(n):
        owner = ring.device(p + way * s, 1 - core)
        for number, i, lead in everything:
            here = outs[i].at[lead, owner]
            remote(here, here, sss.at[s, number], srs.at[s, number], to_twin).wait_recv()
    for cp in own:
        cp.wait()
    for cp in started:
        cp.wait_send()
    for cp in swapped:
        cp.wait()


def ring_gather(ring, number, arrays, wide, swaps=()):
    n, nf = ring.chips, ring.nf
    leads = [1 if w else a.shape[0] for a, w in zip(arrays, wide)]
    shapes, streams, late, size = [], 0, 0, 0
    for a, w in zip(arrays, wide):
        if w:
            shapes.append(jax.ShapeDtypeStruct((nf, 2 * n) + a.shape, a.dtype))
            streams += nf
            late += nf - 1
        else:
            shapes.append(jax.ShapeDtypeStruct((a.shape[0], 2 * n) + a.shape[1:], a.dtype))
            streams += a.shape[0]
        size += shapes[-1].size * 2
    dma = pltpu.SemaphoreType.DMA
    shapes += [jax.ShapeDtypeStruct(a.shape, a.dtype) for a in swaps]
    return pl.pallas_call(
        functools.partial(
            gather_kernel, ring, tuple(wide), tuple(leads), len(arrays), len(swaps)
        ),
        out_shape=shapes,
        in_specs=[pl.BlockSpec(memory_space=pl.ANY)] * len(shapes),
        out_specs=[pl.BlockSpec(memory_space=pl.ANY)] * len(shapes),
        scratch_shapes=[
            dma((streams,)),
            dma((max(1, late),)),
            dma((max(1, late),)),
            dma((n - 1, streams)),
            dma((n - 1, streams)),
            dma((n, streams)),
            dma((n, streams)),
            dma((max(1, len(swaps)),)),
            dma((max(1, len(swaps)),)),
        ],
        compiler_params=pltpu.CompilerParams(collective_id=number, has_side_effects=True),
        cost_estimate=pl.CostEstimate(flops=0, bytes_accessed=2 * size, transcendentals=0),
        name="ring_gather_%d" % number,
    )(*arrays, *swaps)


def front_kernel(ring, latent_part, *refs):
    ins, swap_ins, (normed, cosine, sine) = refs[:5], refs[5:7], refs[7:10]
    outs, swap_outs, (keys, hidden, latent) = refs[10:15], refs[15:17], refs[17:20]
    small_held, kva_held, own_keys = refs[20:23]
    own_sem, yss, yrs, rss, rrs, sss, srs, wss, wrs, load_sem = refs[23:]
    f, c, core, p, way = ring.here()
    n, nf = ring.chips, ring.nf
    nc = 2 * n
    greet(ring, f, c, core, p, way, True)
    to_next, to_twin = (f, ring.device(p + way, core)), (f, c + 1 - 2 * core)
    to_other, other = ((f + 1) % nf, c), (f + 1) % nf
    started, own = [], {}

    def remote(src, dst, ss, rs, dev):
        return pltpu.make_async_remote_copy(
            src_ref=src, dst_ref=dst, send_sem=ss, recv_sem=rs, device_id=dev, device_id_type=MESH
        )

    def place(number, owner):
        if number < 10:
            return outs[number // 2].at[(f + number % 2) % nf, owner]
        return keys.at[number - 10, owner]

    def send(s, number, owner, src, ring_too=True):
        dst = place(number, owner)
        if ring_too:
            cp = remote(src, dst, rss.at[s, number], rrs.at[s, number], to_next)
            cp.start()
            started.append(cp)
        cp = remote(src, dst, sss.at[s, number], srs.at[s, number], to_twin)
        cp.start()
        started.append(cp)

    def keep(number, src):
        own[number] = pltpu.make_async_copy(src, place(number, c), own_sem.at[number])
        own[number].start()

    def pass_on(s, number):
        owner = ring.device(p - way * s, core)
        here = place(number, owner)
        remote(here, here, rss.at[s - 1, number], rrs.at[s - 1, number], to_next).wait_recv()
        send(s, number, owner, here, s < n - 1)

    def late(i):
        here = outs[i].at[other, c]
        remote(here, here, yss.at[i], yrs.at[i], to_next).wait_recv()
        send(0, 2 * i + 1, c, here)

    def from_twin(s, number):
        here = place(number, ring.device(p + way * s, 1 - core))
        remote(here, here, sss.at[s, number], srs.at[s, number], to_twin).wait_recv()

    for i in range(5):
        cp = remote(ins[i], outs[i].at[f, c], yss.at[i], yrs.at[i], to_other)
        cp.start()
        started.append(cp)
        send(0, 2 * i, c, ins[i])
        keep(2 * i, ins[i])
    swapped = []

    def swap():
        for i in range(2):
            cp = remote(swap_ins[i], swap_outs[i], wss.at[i], wrs.at[i], to_other)
            cp.start()
            swapped.append(cp)

    bulk = [functools.partial(late, i) for i in (2, 3, 4)] + [swap]
    bulk += [functools.partial(pass_on, s, number) for s in range(1, n) for number in range(4, 10)]

    def some(count):
        for work in bulk[:count]:
            work()
        del bulk[:count]

    late(0)
    late(1)
    for s in range(1, n):
        for number in range(4):
            pass_on(s, number)
        some(3)
    for number in range(4):
        for s in range(n):
            from_twin(s, number)
    for number in (0, 2):
        own[number].wait()
    loads = [
        pltpu.make_async_copy(outs[i], held, load_sem.at[i])
        for i, held in enumerate((small_held, kva_held))
    ]
    for cp in loads:
        cp.start()
    for cp in loads:
        cp.wait()
    lane = lax.broadcasted_iota(jnp.int32, (1, 128), 1)

    def gain(row, first, each):
        total = jnp.zeros((1, 128), F32)
        for k in range(128 // each):
            d = first // each + k
            own_row = small_held[d // nc, d % nc, row : row + 1, :].astype(F32)
            total = jnp.where(lane // each == k, own_row, total)
        return total

    for start in range(0, D, 128):
        cut = slice(start, start + 128)
        hidden[:, cut] = (normed[:, cut] * gain(0, start, D // (nf * nc))).astype(BF)
    latent[:, LAT:] = jnp.zeros((latent.shape[0], 128), F32)
    latent[:, : LAT + DR] = multiply(hidden[...], kva_held[...].reshape(D, LAT + DR))
    trees, tok = own_keys.shape[:2]
    low = latent[:, :LAT]
    inverse = lax.rsqrt(jnp.mean(low * low, axis=-1, keepdims=True) + epsilon)
    for start in range(0, LAT, 128):
        cut = slice(start, start + 128)
        key = (latent[:, cut] * inverse * gain(1, start, latent_part)).astype(BF)
        for a in range(trees):
            own_keys[a, :, cut] = key[a * tok : (a + 1) * tok]
    half = DR // 2
    former, latter = latent[:, LAT : LAT + half], latent[:, LAT + half : LAT + DR]
    turned = (
        (former * cosine[...] - latter * sine[...]).astype(BF),
        (latter * cosine[...] + former * sine[...]).astype(BF),
    )
    own_keys[:, :, LAT:] = jnp.zeros((trees, tok, 128), BF)
    for a in range(trees):
        for k in range(2):
            own_keys[a, :, LAT + k * half : LAT + (k + 1) * half] = turned[k][a * tok : (a + 1) * tok]
    for a in range(trees):
        send(0, 10 + a, c, own_keys.at[a])
        keep(10 + a, own_keys.at[a])
    for s in range(1, n):
        some(3)
        for a in range(trees):
            pass_on(s, 10 + a)
    some(len(bulk))
    for number in range(4, 10 + trees):
        for s in range(n):
            from_twin(s, number)
    for number in own:
        if number not in (0, 2):
            own[number].wait()
    for cp in started:
        cp.wait_send()
    for cp in swapped:
        cp.wait()


def front(ring, number, arrays, swaps, normed, cosine, sine, latent_part, trees, tok):
    n, nf = ring.chips, ring.nf
    rows = normed.shape[0]
    shapes = [jax.ShapeDtypeStruct((nf, 2 * n) + a.shape, a.dtype) for a in arrays]
    size = sum(a.size * 2 for a in shapes)
    shapes += [jax.ShapeDtypeStruct(a.shape, a.dtype) for a in swaps]
    shapes += [
        jax.ShapeDtypeStruct((trees, 2 * n, tok, LAT + 128), BF),
        jax.ShapeDtypeStruct((rows, D), BF),
        jax.ShapeDtypeStruct((rows, LAT + 128), F32),
    ]
    dma = pltpu.SemaphoreType.DMA
    streams = 10 + trees
    vmem, far = pl.BlockSpec(memory_space=pltpu.VMEM), pl.BlockSpec(memory_space=pl.ANY)
    return pl.pallas_call(
        functools.partial(front_kernel, ring, latent_part),
        out_shape=shapes,
        in_specs=[far] * 7 + [vmem] * 3,
        out_specs=[far] * 8 + [vmem] * 2,
        scratch_shapes=[
            pltpu.VMEM(shapes[0].shape, BF),
            pltpu.VMEM(shapes[1].shape, BF),
            pltpu.VMEM((trees, tok, LAT + 128), BF),
            dma((streams,)),
            dma((5,)),
            dma((5,)),
            dma((n - 1, streams)),
            dma((n - 1, streams)),
            dma((n, streams)),
            dma((n, streams)),
            dma((2,)),
            dma((2,)),
            dma((2,)),
        ],
        compiler_params=pltpu.CompilerParams(
            collective_id=number, has_side_effects=True, vmem_limit_bytes=32 << 20
        ),
        cost_estimate=pl.CostEstimate(flops=0, bytes_accessed=2 * size, transcendentals=0),
        name="front",
    )(*arrays, *swaps, normed, cosine, sine)


def add_rows(shape, work):
    rows = shape[0]
    step = 16 if rows % 16 == 0 else rows

    def one(r, carry):
        work(pl.ds(pl.multiple_of(r * step, step), step))
        return carry

    lax.fori_loop(0, rows // step, one, 0)


class Products:
    tile = 256

    def __init__(self, cuts, pairs, lefts, rights, outs, held, *rest):
        self.cuts, self.pairs, self.lefts, self.rights, self.outs = cuts, pairs, lefts, rights, outs
        self.held = held
        self.tiles, self.stage, self.load_sem, self.tile_sem, self.store_sem = rest
        self.units = [
            (j, m) for j in range(len(pairs)) for m in range(0, cuts[pairs[j][0]][1], self.tile)
        ]
        self.done, self.loaded, self.stores = 0, set(), [None, None]
        self.ship, self.shipped = {}, []

    def deliver(self):
        for j in sorted(self.ship):
            last = max(i for i, unit in enumerate(self.units) if unit[0] == j)
            if self.done > last + 2 or (self.done == len(self.units) and self.stores == []):
                cp = self.ship.pop(j)()
                cp.start()
                self.shipped.append(cp)

    def fetch(self, number):
        j, m = self.units[number]
        left = self.pairs[j][0]
        source, slot = self.lefts[left], number % 2
        return pltpu.make_async_copy(
            source.at[:, pl.ds(self.cuts[left][0] + m, self.tile)],
            self.tiles.at[slot, pl.ds(0, source.shape[0]), :],
            self.tile_sem.at[slot],
        )

    def start(self):
        self.fetch(0).start()
        self.loads = []
        for i, source in enumerate(self.rights):
            cp = pltpu.make_async_copy(source, self.held[i], self.load_sem.at[i])
            cp.start()
            self.loads.append(cp)

    def run(self, upto):
        while self.done < min(upto, len(self.units)):
            j, m = self.units[self.done]
            left, right, first, width = self.pairs[j]
            if right not in self.loaded:
                self.loads[right].wait()
                self.loaded.add(right)
            self.fetch(self.done).wait()
            if self.done + 1 < len(self.units):
                self.fetch(self.done + 1).start()
            slot = self.done % 2
            value = lax.dot_general(
                self.tiles[slot, pl.ds(0, self.lefts[left].shape[0]), :],
                self.held[right][:, pl.ds(first, width)],
                (((0,), (0,)), ((), ())),
                preferred_element_type=F32,
            )
            if self.stores[slot] is not None:
                self.stores[slot].wait()
            self.stage[slot, :, pl.ds(0, width)] = value.astype(BF)
            cp = pltpu.make_async_copy(
                self.stage.at[slot, :, pl.ds(0, width)],
                self.outs[j].at[pl.ds(m, self.tile), :],
                self.store_sem.at[slot],
            )
            cp.start()
            self.stores[slot] = cp
            self.done += 1
            self.deliver()

    def finish(self):
        self.run(len(self.units))
        for cp in self.stores:
            if cp is not None:
                cp.wait()
        self.stores = []
        self.deliver()
        for cp in self.shipped:
            cp.wait()


def reduce_kernel(ring, wide, leads, count, cuts, pairs, ships, *refs):
    njobs = len(pairs)
    nleft = len(cuts)
    nright = 1 + max([p[1] for p in pairs], default=-1)
    nops = nleft + nright
    ins, sources, refs = refs[:count], refs[count : count + nops], refs[count + nops :]
    outs, job_outs, refs = refs[:count], refs[count : count + njobs], refs[count + njobs :]
    ship_outs, refs = refs[: len(ships)], refs[len(ships) :]
    own, twin, got = (refs[k * count : (1 + k) * count] for k in range(3))
    refs = refs[3 * count :]
    wides = sum(wide)
    finals, ygots = refs[:wides], refs[wides : 2 * wides]
    own_sem, tss, trs, rss, rrs, yss, yrs = refs[2 * wides : 2 * wides + 7]
    refs = refs[2 * wides + 7 :]
    jobs = None
    if njobs:
        jobs = Products(
            cuts, pairs, sources[:nleft], sources[nleft:], job_outs, refs[:nright], *refs[nright : nright + 5]
        )
    f, c, core, p, way = ring.here()
    n, nf = ring.chips, ring.nf
    greet(ring, f, c, core, p, way, any(wide) or len(ships) > 0)
    to_next = (f, ring.device(p + way, core))
    to_twin = (f, c + 1 - 2 * core)

    def remote(src, dst, ss, rs, dev):
        return pltpu.make_async_remote_copy(
            src_ref=src, dst_ref=dst, send_sem=ss, recv_sem=rs, device_id=dev, device_id_type=MESH
        )

    streams = []
    for k in range(max(leads)):
        for i in range(count):
            if k < leads[i]:
                lead = (f + 1 + k) % nf if wide[i] else k
                streams.append((len(streams), i, k, lead))
    started, loads = [], {}
    for s in range(n):
        theirs = ring.device(p + way * (1 + s), 1 - core)
        mine = ring.device(p - way * (1 + s), core)
        for number, i, k, lead in streams:
            cp = remote(
                ins[i].at[lead, theirs], twin[i].at[s, k], tss.at[s, number], trs.at[s, number], to_twin
            )
            cp.start()
            started.append(cp)
            cp = pltpu.make_async_copy(
                ins[i].at[lead, mine], own[i].at[s, k], own_sem.at[s, number]
            )
            cp.start()
            loads[s, number] = cp

    if jobs:
        for w, j in enumerate(ships):
            jobs.ship[j] = functools.partial(
                remote, job_outs[j], ship_outs[w], refs[-2].at[w], refs[-1].at[w], ((f + 1) % nf, c)
            )
        jobs.start()

    def wait_parts(s, number, i, k):
        loads[s, number].wait()
        here = twin[i].at[s, k]
        remote(here, here, tss.at[s, number], trs.at[s, number], to_twin).wait_recv()

    def pass_on(s, number, i, k, src):
        cp = remote(src, got[i].at[s, k], rss.at[s, number], rrs.at[s, number], to_next)
        cp.start()
        started.append(cp)

    turn, turns = 0, (n - 1) * len(streams)
    for s in range(n):
        for number, i, k, lead in streams:
            if jobs and s > 0:
                jobs.run(-(-len(jobs.units) * turn // turns))
                turn += 1
            wait_parts(s, number, i, k)
            mine, other = own[i].at[s, k], twin[i].at[s, k]
            if s == 0:

                def start(rows, mine=mine, other=other):
                    mine[rows, :] = (mine[rows, :].astype(F32) + other[rows, :].astype(F32)).astype(BF)

                add_rows(mine.shape, start)
                pass_on(0, number, i, k, mine)
                continue
            came = got[i].at[s - 1, k]
            remote(came, came, rss.at[s - 1, number], rrs.at[s - 1, number], to_next).wait_recv()
            if s < n - 1:

                def middle(rows, mine=mine, other=other, came=came):
                    total = mine[rows, :].astype(F32) + other[rows, :].astype(F32)
                    came[rows, :] = (came[rows, :].astype(F32) + total).astype(BF)

                add_rows(mine.shape, middle)
                pass_on(s, number, i, k, came)
                continue
            if not wide[i]:
                target = outs[i].at[k]
            elif k == nf - 1:
                target = outs[i]
            else:
                target = finals[sum(wide[:i])].at[k]

            def last(rows, mine=mine, other=other, came=came, target=target):
                total = mine[rows, :].astype(F32) + other[rows, :].astype(F32)
                target[rows, :] = (came[rows, :].astype(F32) + total).astype(target.dtype)

            add_rows(mine.shape, last)
            if wide[i] and k < nf - 1:
                w = sum(wide[:i])
                cp = remote(target, ygots[w].at[k], yss.at[w, k], yrs.at[w, k], ((f + 1 + k) % nf, c))
                cp.start()
                started.append(cp)
    for i in range(count):
        if wide[i]:
            w = sum(wide[:i])
            for k in range(nf - 1):
                here = ygots[w].at[k]
                remote(here, here, yss.at[w, k], yrs.at[w, k], to_next).wait_recv()

                def finish(rows, here=here, target=outs[i]):
                    target[rows, :] = target[rows, :] + here[rows, :].astype(F32)

                add_rows(here.shape, finish)
    if jobs:
        jobs.finish()
    for cp in started:
        cp.wait_send()


def ring_reduce(ring, number, arrays, wide, lefts=(), rights=(), cuts=(), pairs=(), ships=()):
    n, nf = ring.chips, ring.nf
    leads = [a.shape[0] for a in arrays]
    more = [jax.ShapeDtypeStruct((cuts[l][1], width), BF) for l, _, _, width in pairs]
    streams = sum(leads)
    block = [a.shape[2:] for a in arrays]
    shapes = [
        jax.ShapeDtypeStruct(b if w else (l,) + b, F32) for b, w, l in zip(block, wide, leads)
    ]
    dma = pltpu.SemaphoreType.DMA
    scratch = [pltpu.VMEM((n, l) + b, BF) for b, l in zip(block, leads)] * 2
    scratch += [pltpu.VMEM((n - 1, l) + b, BF) for b, l in zip(block, leads)]
    scratch += [pltpu.VMEM((nf - 1,) + b, BF) for b, w in zip(block, wide) if w] * 2
    more += [more[j] for j in ships]
    wides = max(1, sum(wide))
    extra = []
    if pairs:
        extra = [pltpu.VMEM(a.shape, BF) for a in rights]
        extra += [
            pltpu.VMEM((2, max(a.shape[0] for a in lefts), Products.tile), BF),
            pltpu.VMEM((2, Products.tile, max(p[3] for p in pairs)), BF),
            dma((len(rights),)),
            dma((2,)),
            dma((2,)),
        ]
    if ships:
        extra += [dma((len(ships),)), dma((len(ships),))]
    return pl.pallas_call(
        functools.partial(
            reduce_kernel, ring, tuple(wide), tuple(leads), len(arrays), tuple(cuts), tuple(pairs), tuple(ships)
        ),
        out_shape=shapes + more,
        in_specs=[pl.BlockSpec(memory_space=pl.ANY)] * (len(arrays) + len(lefts) + len(rights)),
        out_specs=[pl.BlockSpec(memory_space=pltpu.VMEM)] * len(arrays)
        + [pl.BlockSpec(memory_space=pl.ANY)] * len(more),
        scratch_shapes=scratch
        + [
            dma((n, streams)),
            dma((n, streams)),
            dma((n, streams)),
            dma((n - 1, streams)),
            dma((n - 1, streams)),
            dma((wides, max(1, nf - 1))),
            dma((wides, max(1, nf - 1))),
        ]
        + extra,
        compiler_params=pltpu.CompilerParams(
            collective_id=number, has_side_effects=True, vmem_limit_bytes=60 << 20
        ),
        cost_estimate=pl.CostEstimate(flops=0, bytes_accessed=1 << 20, transcendentals=0),
        name="ring_reduce_%d" % number,
    )(*arrays, *lefts, *rights)


def expert_kernel(nf, experts, fp, bundle_slots, *refs):
    x_ref, g_ref, probs_ref, slot_ref, column_ref = refs[:5]
    weights, refs = refs[5 : 5 + 4 * nf], refs[5 + 4 * nf :]
    back_ref, out_ref, delta_ref, rows_ref, grads_ref, hid_ref, gg_ref, ug_ref, act_ref = refs[:9]
    w_gate, w_up, w_down, w_shared, pre_gate, pre_up, pre_in, pre_s, raw, sems = refs[9:]
    mine = lax.axis_index("ctx")
    held = (w_gate, w_up, w_down, w_shared)
    part = w_gate.shape[0] // nf
    wide = w_gate.shape[0]
    copies = [
        [
            pltpu.make_async_copy(
                weights[4 * k + i], held[i].at[pl.ds(k * part, part)], sems.at[i, k]
            )
            for k in range(nf)
        ]
        for i in range(4)
    ]
    first = pl.program_id(0) == 0

    def ready(i):
        @pl.when(first)
        def _():
            for cp in copies[i]:
                cp.wait()

    @pl.when(first)
    def _():
        for i in (3, 0, 1, 2):
            for cp in copies[i]:
                cp.start()

    def nt(left, right):
        return lax.dot_general(left, right, (((1,), (1,)), ((), ())), preferred_element_type=F32)

    bundles, _, rows = slot_ref.shape
    lane = lax.broadcasted_iota(jnp.int32, (rows, 128), 1)
    own_lane = (lane % experts == mine) & (lane < 3 * experts)
    puts, row_gates = [], []
    for b in range(bundles):
        cut, spot = pl.ds(b * rows, rows), pl.ds(b * bundle_slots, bundle_slots)
        takes = (
            slot_ref[b] == lax.broadcasted_iota(jnp.int32, (bundle_slots, rows), 0)
        ).astype(F32).astype(BF)
        puts.append(
            (
                column_ref[cut, :] == lax.broadcasted_iota(jnp.int32, (rows, bundle_slots), 1)
            ).astype(F32).astype(BF)
        )
        own = jnp.where(own_lane, probs_ref[cut, :].astype(F32), 0.0)
        row_gates.append(jnp.sum(own, axis=1, keepdims=True))
        gate = jnp.sum(multiply(takes, own.astype(BF)), axis=1, keepdims=True)
        for start in range(0, wide, 512):
            piece = pl.ds(start, 512)
            rows_ref[spot, piece] = multiply(takes, x_ref[cut, piece]).astype(BF)
            taken = multiply(takes, g_ref[cut, piece])
            raw[spot, piece] = taken.astype(BF)
            grads_ref[spot, piece] = (gate * taken).astype(BF)

    ready(3)
    pre_s[:, : 2 * fp] = multiply(x_ref[...], w_shared[:, : 2 * fp])
    pre_s[:, 2 * fp :] = multiply(g_ref[...], w_shared[:, 2 * fp :])

    def activate(gate_pre, up_pre, inner):
        sig = jax.nn.sigmoid(gate_pre)
        activated = gate_pre * sig
        hidden = activated * up_pre
        gate_grad = inner * up_pre * sig * (1.0 + gate_pre * (1.0 - sig))
        return hidden.astype(BF), gate_grad.astype(BF), (inner * activated).astype(BF)

    step = 32

    def shared_rows(r, carry):
        at = pl.ds(pl.multiple_of(r * step, step), step)
        for start in range(0, fp, 128):
            cuts = [pl.ds(i * fp + start, 128) for i in range(3)]
            hidden, gate_grad, up_grad = activate(*(pre_s[at, c] for c in cuts))
            act_ref[at, cuts[0]] = gate_grad
            act_ref[at, cuts[1]] = up_grad
            act_ref[at, cuts[2]] = hidden
        return carry

    lax.fori_loop(0, pre_s.shape[0] // step, shared_rows, 0)

    ready(0)
    pre_gate[...] = multiply(rows_ref[...], w_gate[...])
    ready(1)
    pre_up[...] = multiply(rows_ref[...], w_up[...])
    ready(2)
    pre_in[...] = multiply(grads_ref[...], w_down[...])

    def expert_rows(r, carry):
        at = pl.ds(pl.multiple_of(r * step, step), step)
        for start in range(0, hid_ref.shape[1], 128):
            c = pl.ds(start, 128)
            hidden, gate_grad, up_grad = activate(pre_gate[at, c], pre_up[at, c], pre_in[at, c])
            hid_ref[at, c] = hidden
            gg_ref[at, c] = gate_grad
            ug_ref[at, c] = up_grad
        return carry

    lax.fori_loop(0, hid_ref.shape[0] // step, expert_rows, 0)

    delta = 0.0
    for start in range(0, wide, 512):
        piece = pl.ds(start, 512)
        e_back = nt(gg_ref[...], w_gate[piece, :]) + nt(ug_ref[...], w_up[piece, :])
        e_back = e_back.astype(BF)
        e_out = nt(hid_ref[...], w_down[piece, :]).astype(BF)
        delta = delta + jnp.sum(
            raw[:, piece].astype(F32) * e_out.astype(F32), axis=1, keepdims=True
        )
        for b in range(bundles):
            cut = pl.ds(b * rows, rows)
            spot = slice(b * bundle_slots, (b + 1) * bundle_slots)
            s_back = nt(act_ref[cut, : 2 * fp], w_shared[piece, : 2 * fp])
            back_ref[cut, piece] = (multiply(puts[b], e_back[spot]) + s_back).astype(BF)
            s_out = nt(act_ref[cut, 2 * fp :], w_shared[piece, 2 * fp :])
            out_ref[cut, piece] = (row_gates[b] * multiply(puts[b], e_out[spot]) + s_out).astype(BF)
    for b in range(bundles):
        own = delta[b * bundle_slots : (b + 1) * bundle_slots]
        high = own.astype(BF).astype(F32)
        middle = (own - high).astype(BF).astype(F32)
        low = own - high - middle
        spread = jnp.where(lane[:bundle_slots] < experts, high, jnp.where(lane[:bundle_slots] < 2 * experts, middle, low))
        spread = jnp.where(own_lane[:bundle_slots], spread, 0.0).astype(BF)
        delta_ref[pl.ds(b * rows, rows), :] = multiply(puts[b], spread).astype(BF)


def run_experts(nf, experts, capacity, tok_loc, tree_rows, tree_grads, tree_probs, slot, weights):
    rows, wide = tree_rows.shape
    bundles, per = slot.shape
    bundle_slots = capacity * (per // tok_loc)
    hidden, fp = weights[0][0].shape[1], weights[0][3].shape[1] // 3
    group = 2 if bundles % 2 == 0 else 1
    steps = bundles // group
    block, slots = rows // steps, group * bundle_slots
    flat = [w for piece in weights for w in piece]
    by_row = lambda width: pl.BlockSpec((block, width), lambda i: (i, 0))
    by_slot = lambda width: pl.BlockSpec((slots, width), lambda i: (i, 0))
    any_spec = pl.BlockSpec(memory_space=pl.ANY)
    shape = lambda n, width: jax.ShapeDtypeStruct((n, width), BF)
    total = steps * slots
    flops = 2 * (6 * total * wide * hidden + 6 * rows * wide * fp + 4 * rows * bundle_slots * wide)
    return pl.pallas_call(
        functools.partial(expert_kernel, nf, experts, fp, bundle_slots),
        grid=(steps,),
        out_shape=[shape(rows, wide), shape(rows, wide), shape(rows, 128)]
        + [shape(total, wide)] * 2
        + [shape(total, hidden)] * 3
        + [shape(rows, 3 * fp)],
        in_specs=[
            by_row(wide),
            by_row(wide),
            by_row(128),
            pl.BlockSpec((group, 1, per), lambda i: (i, 0, 0)),
            pl.BlockSpec((block, 1), lambda i: (i, 0)),
        ]
        + [any_spec] * len(flat),
        out_specs=[by_row(wide), by_row(wide), by_row(128)]
        + [by_slot(wide)] * 2
        + [by_slot(hidden)] * 3
        + [by_row(3 * fp)],
        scratch_shapes=[pltpu.VMEM((wide, hidden), BF)] * 3
        + [pltpu.VMEM((wide, 3 * fp), BF)]
        + [pltpu.VMEM((slots, hidden), F32)] * 3
        + [pltpu.VMEM((block, 3 * fp), F32), pltpu.VMEM((slots, wide), BF)]
        + [pltpu.SemaphoreType.DMA((4, nf))],
        compiler_params=pltpu.CompilerParams(vmem_limit_bytes=61 << 20),
        cost_estimate=pl.CostEstimate(
            flops=flops, bytes_accessed=10 * rows * wide, transcendentals=total * hidden
        ),
        name="experts",
    )(tree_rows, tree_grads, tree_probs, slot[:, None, :], slot.reshape(rows, 1), *flat)


def nt(left, right):
    return lax.dot_general(left, right, (((1,), (1,)), ((), ())), preferred_element_type=F32)


def tn(left, right):
    return lax.dot_general(left, right, (((0,), (0,)), ((), ())), preferred_element_type=F32)


HEADS = 4


def attend_kernel(
    scale, hidden, cosine, sine, keys, allowed, expand, tokens, wq_hbm, wo_hbm,
    cat, lse, mixed, heads, residual, nope, w_out, w_part, query, sem, part_sem,
):
    trees, tok = cat.shape[0], cat.shape[2]
    copy = pltpu.make_async_copy(wo_hbm, w_out, sem)
    pair = 2 * (DN + DR)

    def part(i):
        return pltpu.make_async_copy(
            wq_hbm.at[:, pl.ds(i * pair, pair)], w_part.at[i % 2], part_sem.at[i % 2]
        )

    part(0).start()
    cat[:, :, :, LAT + DR :] = jnp.zeros((trees, H, tok, 128 - DR), BF)
    half = DR // 2
    for i in range(H // 2):
        part(i).wait()
        if i + 1 < H // 2:
            part(i + 1).start()
        else:
            copy.start()
        query[...] = multiply(hidden[...], w_part[i % 2])
        for h in (2 * i, 2 * i + 1):
            first = h % 2 * (DN + DR)
            nope[:, h * DN : (h + 1) * DN] = query[:, first : first + DN].astype(BF)
            former = query[:, first + DN : first + DN + half]
            latter = query[:, first + DN + half : first + DN + DR]
            turned = (
                (former * cosine[...] - latter * sine[...]).astype(BF),
                (latter * cosine[...] + former * sine[...]).astype(BF),
            )
            low = nt(nope[:, h * DN : (h + 1) * DN], expand[:, h * (DN + DV) : h * (DN + DV) + DN])
            low = low.astype(BF)
            for b in range(trees):
                rows = slice(b * tok, (b + 1) * tok)
                cat[b, h, :, :LAT] = low[rows]
                cat[b, h, :, LAT : LAT + half] = turned[0][rows]
                cat[b, h, :, LAT + half : LAT + DR] = turned[1][rows]

    def group(i, carry):
        b, g = i // (H // HEADS), i % (H // HEADS) * HEADS
        query = cat[b, pl.ds(g, HEADS)].reshape(HEADS * tok, -1)
        scores = nt(query, keys[b]) * scale
        scores = scores.reshape(HEADS, tok, -1)
        scores = jnp.where(allowed[b][None] > 0, scores, -1e30)
        highest = jnp.max(scores, axis=-1, keepdims=True)
        raised = jnp.exp(scores - highest)
        total = jnp.sum(raised, axis=-1, keepdims=True)
        lse[b, pl.ds(g, HEADS)] = highest + jnp.log(total)
        probs = (raised * (1.0 / total)).astype(BF).reshape(HEADS * tok, -1)
        mix = multiply(probs, keys[b, :, :LAT]).astype(BF)
        mixed[b, pl.ds(g, HEADS)] = mix.reshape(HEADS, tok, LAT)
        return carry

    lax.fori_loop(0, trees * (H // HEADS), group, 0)
    for h in range(H):
        mix = jnp.concatenate([mixed[b, h] for b in range(trees)], axis=0)
        value = expand[:, h * (DN + DV) + DN : (h + 1) * (DN + DV)]
        heads[:, h * DV : (h + 1) * DV] = multiply(mix, value).astype(BF)
    copy.wait()
    for start in range(0, D, 512):
        cut = slice(start, start + 512)
        residual[:, cut] = tokens[:, cut].astype(F32) + multiply(heads[...], w_out[:, cut])


def attend(hidden, cosine, sine, keys, allowed, expand, tokens, w_query, w_output, tok, scale):
    rows = tokens.shape[0]
    trees = rows // tok
    vmem, far = pl.BlockSpec(memory_space=pltpu.VMEM), pl.BlockSpec(memory_space=pl.ANY)
    length, width = keys.shape[1:]
    return pl.pallas_call(
        functools.partial(attend_kernel, scale),
        out_shape=[
            jax.ShapeDtypeStruct((trees, H, tok, width), BF),
            jax.ShapeDtypeStruct((trees, H, tok, 1), F32),
            jax.ShapeDtypeStruct((trees, H, tok, LAT), BF),
            jax.ShapeDtypeStruct((rows, H * DV), BF),
            jax.ShapeDtypeStruct((rows, D), F32),
            jax.ShapeDtypeStruct((rows, H * DN), BF),
        ],
        in_specs=[vmem] * 7 + [far] * 2,
        out_specs=[vmem] * 6,
        scratch_shapes=[
            pltpu.VMEM(w_output.shape, BF),
            pltpu.VMEM((2, D, 2 * (DN + DR)), BF),
            pltpu.VMEM((rows, 2 * (DN + DR)), F32),
            pltpu.SemaphoreType.DMA,
            pltpu.SemaphoreType.DMA((2,)),
        ],
        compiler_params=pltpu.CompilerParams(vmem_limit_bytes=56 << 20),
        cost_estimate=pl.CostEstimate(
            flops=2 * rows * H * length * 1152, bytes_accessed=30 << 20, transcendentals=rows * H * length
        ),
        name="attend",
    )(hidden, cosine, sine, keys, allowed, expand, tokens, w_query, w_output)


def attend_back_kernel(
    scale, grad, w_out, expand, cat, keys, lse, allowed, mixed, nope, keys_grad, nope_grad, rope_grad,
    expand_grad, heads_grad, mix_grad, low_probs, score_grad, cat_grad,
):
    trees, tok = cat.shape[0], cat.shape[2]
    for start in range(0, H * DV, 512):
        heads_grad[:, start : start + 512] = nt(grad[...], w_out[start : start + 512, :]).astype(BF)
    for h in range(H):
        value = expand[:, h * (DN + DV) + DN : (h + 1) * (DN + DV)]
        own = heads_grad[:, h * DV : (h + 1) * DV]
        back = nt(own, value).astype(BF)
        for b in range(trees):
            mix_grad[b, h] = back[b * tok : (b + 1) * tok]
        mix = jnp.concatenate([mixed[b, h] for b in range(trees)], axis=0)
        expand_grad[:, h * (DN + DV) + DN : (h + 1) * (DN + DV)] = tn(mix, own).astype(BF)
    for b in range(trees):

        def group(i, carry, b=b):
            g = i * HEADS
            rows = pl.ds(pl.multiple_of(g * tok, HEADS * tok), HEADS * tok)
            query = cat[b, pl.ds(g, HEADS)].reshape(HEADS * tok, -1)
            mix = mix_grad[b, pl.ds(g, HEADS)].reshape(HEADS * tok, -1)
            scores = (nt(query, keys[b]) * scale).reshape(HEADS, tok, -1)
            probs = jnp.where(
                allowed[b][None] > 0, jnp.exp(scores - lse[b, pl.ds(g, HEADS)]), 0.0
            ).reshape(HEADS * tok, -1)
            prob_grad = nt(mix, keys[b, :, :LAT])
            centre = jnp.sum(probs * prob_grad, axis=-1, keepdims=True)
            low_probs[rows, :] = probs.astype(BF)
            own = (probs * (prob_grad - centre)).astype(BF)
            score_grad[rows, :] = own
            back = (multiply(own, keys[b]) * scale).reshape(HEADS, tok, -1)
            cat_grad[b, pl.ds(g, HEADS)] = back[..., :LAT].astype(BF)
            for k in range(HEADS):
                rope_grad[b, g + k] = back[k, :, LAT:]
            return carry

        lax.fori_loop(0, H // HEADS, group, 0)
        query = cat[b].reshape(H * tok, -1)
        mix = mix_grad[b].reshape(H * tok, -1)
        length = keys.shape[1]
        for start in range(0, length, 256):
            cut = slice(start, start + 256)
            total = tn(score_grad[:, cut], query) * scale
            keys_grad[b, cut, :LAT] = (total[:, :LAT] + tn(low_probs[:, cut], mix)).astype(BF)
            keys_grad[b, cut, LAT:] = total[:, LAT:].astype(BF)
    for h in range(H):
        low = jnp.concatenate([cat_grad[b, h] for b in range(trees)], axis=0)
        key = expand[:, h * (DN + DV) : h * (DN + DV) + DN]
        nope_grad[:, h * DN : (h + 1) * DN] = multiply(low, key)
        expand_grad[:, h * (DN + DV) : h * (DN + DV) + DN] = tn(
            low, nope[:, h * DN : (h + 1) * DN]
        ).astype(BF)


def attend_back(grad, w_output, expand, cat, keys, lse, allowed, mixed, nope, scale):
    trees, _, tok, width = cat.shape
    length, rows = keys.shape[1], grad.shape[0]
    vmem = pl.BlockSpec(memory_space=pltpu.VMEM)
    return pl.pallas_call(
        functools.partial(attend_back_kernel, scale),
        out_shape=[
            jax.ShapeDtypeStruct(keys.shape, BF),
            jax.ShapeDtypeStruct((rows, H * DN), F32),
            jax.ShapeDtypeStruct((trees, H, tok, width - LAT), F32),
            jax.ShapeDtypeStruct(expand.shape, BF),
        ],
        in_specs=[vmem] * 9,
        out_specs=[vmem] * 4,
        scratch_shapes=[
            pltpu.VMEM((rows, H * DV), BF),
            pltpu.VMEM((trees, H, tok, LAT), BF),
            pltpu.VMEM((H * tok, length), BF),
            pltpu.VMEM((H * tok, length), BF),
            pltpu.VMEM((trees, H, tok, LAT), BF),
        ],
        compiler_params=pltpu.CompilerParams(vmem_limit_bytes=60 << 20),
        cost_estimate=pl.CostEstimate(
            flops=0, bytes_accessed=1 << 20, transcendentals=0
        ),
        name="attend_back",
    )(grad, w_output, expand, cat, keys, lse, allowed, mixed, nope)


def body(
    tokens,
    out_grad,
    segments,
    path_mask,
    expert_ids,
    norm_attn,
    attn_q,
    attn_kva,
    norm_latent,
    attn_kvb,
    attn_out,
    norm_ffn,
    router,
    expert_gate,
    expert_up,
    expert_down,
    shared_gate,
    shared_up,
    shared_down,
):
    trees, tok_loc = tokens.shape[:2]
    row_total = trees * tok_loc
    nc, nf = lax.axis_size("ctx"), lax.axis_size("fsdp")
    mine, group = lax.axis_index("ctx"), lax.axis_index("fsdp")
    experts = nc
    ring = Ring(nf, nc)
    tree_len = tok_loc * nc
    group_rows = trees * tree_len
    first_row = mine * tok_loc
    capacity = min(tok_loc, tok_loc * TOP * 4 // (3 * experts))
    slot_total = nc * trees * capacity
    score_scale = 1.0 / math.sqrt(DN + DR)
    frequency = rope_base ** (-(jnp.arange(DR // 2, dtype=F32) * 2.0 / DR))
    labels = jnp.arange(experts, dtype=jnp.int32)
    both = ("fsdp", "ctx")
    part = D // nf

    def roll_in(x):
        return lax.dynamic_slice_in_dim(jnp.concatenate([x, x], axis=-1), group * part, D, x.ndim - 1)

    def roll_out(x):
        return lax.dynamic_slice_in_dim(
            jnp.concatenate([x, x], axis=-1), (nf - group) % nf * part, D, x.ndim - 1
        )

    def fetch(w):
        pieces = [w]
        for k in range(1, nf):
            pieces.append(lax.ppermute(w, "fsdp", [(i, (i - k) % nf) for i in range(nf)]))
        return pieces

    fs = shared_gate.shape[1]
    fp = -(-fs // 128) * 128
    shared_w = jnp.concatenate(
        [jnp.pad(w, ((0, 0), (0, fp - fs))) for w in (shared_gate, shared_up, shared_down)], axis=1
    )
    def one_mask(segment_ids, path_table):
        return tree_mask(segment_ids, path_table, first_row, tok_loc)

    allowed, positions = jax.vmap(one_mask)(segments, path_mask)
    rotation = positions.astype(F32)[:, :, None] * frequency[None, None, :]
    cosine, sine = jnp.cos(rotation), jnp.sin(rotation)
    inputs = tokens.astype(F32).reshape(row_total, D)
    inverse_in = lax.rsqrt(jnp.mean(inputs * inputs, axis=-1, keepdims=True) + epsilon)
    normed_in = inputs * inverse_in

    r_one, r_lat, r_router = norm_attn.shape[0], norm_latent.shape[0], router.size
    small = jnp.concatenate(
        [
            jnp.tile(norm_attn, 128 // r_one),
            jnp.tile(norm_latent, 128 // r_lat),
            norm_attn,
            norm_ffn,
            norm_latent,
            router.reshape(-1),
            expert_ids.astype(BF).reshape(-1),
        ]
    )
    small = jnp.pad(small, (0, 2 * PACK - small.shape[0])).reshape(2 * PACK // 128, 128)
    if nf == 2:
        small_all, w_latent, w_query, w_expand, w_output, other_gate, other_up, keys, hidden_in, latent_all = front(
            ring,
            0,
            [small, attn_kva, attn_q, attn_kvb, attn_out],
            [expert_gate, expert_up],
            normed_in,
            cosine.reshape(row_total, -1),
            sine.reshape(row_total, -1),
            r_lat,
            trees,
            tok_loc,
        )
        e_gate, e_up = [expert_gate, other_gate], [expert_up, other_up]
        later_shared, later_down, later_grads, small_all = lax.optimization_barrier(
            (shared_w, expert_down, out_grad, small_all)
        )
    else:
        w_latent, w_query, w_expand, small_all, w_output = (
            lax.all_gather(w, both, axis=0) for w in (attn_kva, attn_q, attn_kvb, small, attn_out)
        )
        e_gate, e_up = fetch(expert_gate), fetch(expert_up)
        later_shared, later_down, later_grads = shared_w, expert_down, out_grad
    s_all, e_down = fetch(later_shared), fetch(later_down)
    w_output = w_output.reshape(H * DV, D)
    w_latent, w_query = w_latent.reshape(D, -1), w_query.reshape(D, -1)
    w_expand = w_expand.reshape(LAT, -1)
    small_all = small_all.reshape(nf * nc, 2 * PACK)[:, 256:]
    cuts = [0, r_one, 2 * r_one, 2 * r_one + r_lat, 2 * r_one + r_lat + r_router]
    gain_attn = small_all[:, cuts[0] : cuts[1]].reshape(-1).astype(F32)
    gain_ffn = small_all[:, cuts[1] : cuts[2]].reshape(-1).astype(F32)
    gain_latent = small_all[:, cuts[2] : cuts[3]].reshape(-1).astype(F32)
    w_router = small_all[:, cuts[3] : cuts[4]].reshape(D, experts)
    ids_all = lax.dynamic_slice_in_dim(small_all.reshape(nf, nc, -1), group, 1, 0)[0]
    ids_all = ids_all[:, cuts[4] : cuts[4] + expert_ids.size].reshape(nc, trees, tok_loc, TOP)
    ids_all = ids_all.transpose(1, 0, 2, 3).reshape(group_rows, TOP)

    upstream_low = out_grad.reshape(row_total, D)
    upstream = upstream_low.astype(F32)
    tree_grads = lax.all_gather(roll_in(later_grads), "ctx", axis=1, tiled=True).reshape(group_rows, D)

    if nf != 2:
        hidden_in = (normed_in * gain_attn).astype(BF)
        latent_all = multiply(hidden_in, w_latent)
    latent_normed, latent_inverse, latent_gained = normalize(latent_all[:, :LAT], gain_latent)
    if nf != 2:
        key_latent = latent_gained.astype(BF).reshape(trees, tok_loc, LAT)
        key_rope = rotate(latent_all[:, LAT:].reshape(trees, tok_loc, DR), cosine, sine).astype(BF)
        key_pad = jnp.zeros((trees, tok_loc, 128 - DR), BF)
        (keys,) = ring_gather(
            ring, 1, [jnp.concatenate([key_latent, key_rope, key_pad], axis=-1)], [False]
        )
    keys = keys.reshape(trees, tree_len, LAT + 128)
    allowed = allowed.astype(F32)
    query_cat, log_total, mixed, heads, residual, query_nope = attend(
        hidden_in,
        cosine.reshape(row_total, -1),
        sine.reshape(row_total, -1),
        keys,
        allowed,
        w_expand,
        tokens.reshape(row_total, D),
        w_query,
        w_output,
        tok_loc,
        score_scale,
    )
    normed_mid, inverse_mid, gained_mid = normalize(residual, gain_ffn)
    hidden_mid = gained_mid.astype(BF)
    expert_probs = jax.nn.softmax(multiply(hidden_mid, w_router), axis=-1)

    probs_parts = jnp.concatenate(three_parts(expert_probs), axis=-1)
    probs_parts = jnp.pad(probs_parts, ((0, 0), (0, 128 - 3 * experts)))
    tree_rows, tree_probs = ring_gather(
        ring,
        2,
        [roll_in(hidden_mid).reshape(trees, tok_loc, D), probs_parts.reshape(trees, tok_loc, 128)],
        [False, False],
    )
    tree_rows = tree_rows.reshape(group_rows, D)
    tree_probs = tree_probs.reshape(group_rows, 128)

    member = jnp.any(ids_all == mine.astype(BF), axis=1)
    blocks = trees * nc
    bundle = 4 if blocks % 4 == 0 else 1
    bundles = blocks // bundle
    grid = member.astype(BF).reshape(blocks, tok_loc)
    upper = (jnp.arange(tok_loc)[:, None] <= jnp.arange(tok_loc)[None, :]).astype(BF)
    slot = multiply(grid, upper).astype(jnp.int32) - 1
    slot = slot + (jnp.arange(blocks, dtype=jnp.int32) % bundle * capacity)[:, None]
    slot = jnp.where(grid > 0, slot, -1).reshape(bundles, bundle * tok_loc)
    back, out_part, delta_out, e_rows, e_grads, e_hidden, e_gg, e_ug, s_act = run_experts(
        nf,
        experts,
        capacity,
        tok_loc,
        tree_rows,
        tree_grads,
        tree_probs,
        slot,
        list(zip(e_gate, e_up, e_down, s_all)),
    )

    def weight_grads(k, e_gg, e_ug, e_hidden, s_act):
        cut = slice(k * part, (k + 1) * part)
        return (
            transposed_multiply(tree_rows[:, cut], s_act[:, : 2 * fp]),
            transposed_multiply(tree_grads[:, cut], s_act[:, 2 * fp :]),
            transposed_multiply(e_rows[:, cut], e_gg),
            transposed_multiply(e_rows[:, cut], e_ug),
            transposed_multiply(e_grads[:, cut], e_hidden),
        )

    job_arrays = [e_rows, e_grads, tree_rows, tree_grads], [e_gg, e_ug, e_hidden, s_act]
    job_pairs = [
        (2, 3, 0, 2 * fp),
        (3, 3, 2 * fp, fp),
        (0, 0, 0, e_gg.shape[1]),
        (0, 1, 0, e_gg.shape[1]),
        (1, 2, 0, e_gg.shape[1]),
    ]

    def job_cuts(k):
        return [(k * part, part)] * 4

    def by_owner(x):
        return x.reshape(trees, nc, tok_loc, x.shape[-1])

    if nf == 2:
        back_sum, delta_sum, *sent = ring_reduce(
            ring,
            3,
            [by_owner(back), by_owner(delta_out)],
            [False] * 2,
            *job_arrays,
            job_cuts(1),
            job_pairs,
            (0, 1),
        )
        there, sent = sent[5:], sent[2:5]
    else:
        back_sum, delta_sum = ring_reduce(
            ring, 3, [by_owner(back), by_owner(delta_out)], [False] * 2
        )
    back_sum, out_part = lax.optimization_barrier((back_sum, out_part))
    back_sum = roll_out(back_sum.reshape(row_total, D))
    prob_delta = jnp.sum(
        delta_sum.reshape(row_total, 128)[:, : 3 * experts].reshape(row_total, 3, experts), axis=1
    )
    out_sum = lax.psum_scatter(
        out_part.reshape(trees, tree_len, D), "ctx", scatter_dimension=1, tiled=True
    )

    came = []
    for k in range(1, nf):
        perm = [(i, (i + k) % nf) for i in range(nf)]
        grads = sent if nf == 2 else weight_grads(k, e_gg, e_ug, e_hidden, s_act)
        came.append([lax.ppermute(g.astype(BF), "fsdp", perm) for g in grads])
    if nf == 2:
        came[0] = list(there) + came[0]

    logit_grad = (
        expert_probs * (prob_delta - jnp.sum(expert_probs * prob_delta, axis=-1, keepdims=True))
    ).astype(BF)
    grad_router = transposed_multiply(hidden_mid, logit_grad)
    mid_grad = back_sum + multiply_transposed(logit_grad, w_router)
    mid_input, grad_gain_ffn = normalize_back(mid_grad, normed_mid, inverse_mid, gain_ffn)
    residual_grad = upstream + mid_input
    residual_low = residual_grad.astype(BF)
    keys_grad, qnope_grad, qrope_grad, grad_expand = attend_back(
        residual_low,
        w_output,
        w_expand,
        query_cat,
        keys,
        log_total,
        allowed,
        mixed,
        query_nope,
        score_scale,
    )
    qrope_grad = qrope_grad[..., :DR].transpose(0, 2, 1, 3)
    query_grad = jnp.concatenate(
        [
            qnope_grad.reshape(trees, tok_loc, H, DN),
            rotate(qrope_grad, cosine[:, :, None, :], -sine[:, :, None, :]),
        ],
        axis=-1,
    )
    query_grad = query_grad.astype(BF).reshape(row_total, H * (DN + DR))
    own_keys_grad, grad_query, grad_output = ring_reduce(
        ring,
        4,
        [keys_grad.reshape(trees, nc, tok_loc, LAT + 128)],
        [False],
        [hidden_in, heads],
        [query_grad, residual_low],
        [(0, D), (0, H * DV)],
        [(0, 0, 0, query_grad.shape[1]), (1, 1, 0, D)],
    )
    own_keys_grad, out_sum = lax.optimization_barrier((own_keys_grad, out_sum))
    out_sum = roll_out(out_sum.reshape(row_total, D).astype(F32))
    output = (residual + out_sum).astype(BF).reshape(trees, tok_loc, D)
    hidden_grad = multiply_transposed(query_grad, w_query)
    latent_in_grad, grad_gain_latent = normalize_back(
        own_keys_grad[..., :LAT].reshape(row_total, LAT), latent_normed, latent_inverse, gain_latent
    )
    rope_back = rotate(own_keys_grad[..., LAT : LAT + DR], cosine, -sine).reshape(row_total, DR)
    latent_grad = jnp.concatenate([latent_in_grad, rope_back], axis=-1).astype(BF)
    grad_latent = transposed_multiply(hidden_in, latent_grad)
    hidden_grad = hidden_grad + multiply_transposed(latent_grad, w_latent)
    input_part, grad_gain_attn = normalize_back(hidden_grad, normed_in, inverse_in, gain_attn)
    input_grad = (input_part + residual_grad).reshape(trees, tok_loc, D)

    grad_small = jnp.concatenate(
        [
            grad_gain_attn.reshape(nf * nc, r_one),
            grad_gain_ffn.reshape(nf * nc, r_one),
            grad_gain_latent.reshape(nf * nc, r_lat),
            grad_router.reshape(nf * nc, r_router),
        ],
        axis=1,
    ).astype(BF)
    grad_small = jnp.pad(grad_small, ((0, 0), (0, PACK - grad_small.shape[1])))
    parts = [
        grad_query.reshape(nf, nc, -1, w_query.shape[1]),
        grad_expand.reshape(nf, nc, -1, w_expand.shape[1]),
        grad_latent.astype(BF).reshape(nf, nc, -1, w_latent.shape[1]),
        grad_small.reshape(nf, nc, 16, PACK // 16),
        grad_output.reshape(nf, nc, -1, D),
    ]
    if nf == 2:
        t_query, t_expand, t_latent, t_small, out_total, *ffn_sums = ring_reduce(
            ring, 5, parts, [True] * 5, *job_arrays, job_cuts(0), job_pairs
        )
        came, ffn_sums = lax.optimization_barrier((came, ffn_sums))
    else:
        t_query, t_expand, t_latent, t_small, out_total = (
            lax.psum_scatter(
                x.reshape((nf * nc,) + x.shape[2:]), both, scatter_dimension=0, tiled=True
            )[0].astype(F32)
            for x in parts
        )
        ffn_sums = weight_grads(0, e_gg, e_ug, e_hidden, s_act)
    t_small = t_small.reshape(PACK)
    for one in came:
        ffn_sums = [a.astype(F32) + b.astype(F32) for a, b in zip(ffn_sums, one)]
    e_sums = ffn_sums[2:]
    s_sums = [ffn_sums[0][:, :fs], ffn_sums[0][:, fp : fp + fs], ffn_sums[1][:, :fs]]
    return (
        output,
        input_grad,
        t_small[cuts[0] : cuts[1]],
        t_query,
        t_latent,
        t_small[cuts[2] : cuts[3]],
        t_expand,
        out_total,
        t_small[cuts[1] : cuts[2]],
        t_small[cuts[3] : cuts[4]].reshape(-1, experts),
        *e_sums,
        *s_sums,
    )


def solution(mesh):
    placed = (
        P("fsdp", "ctx", None),
        P("fsdp", "ctx", None),
        P("fsdp", None),
        P("fsdp", None, None),
        P("fsdp", "ctx", None),
        P(("fsdp", "ctx")),
        P(("fsdp", "ctx"), None),
        P(("fsdp", "ctx"), None),
        P(("fsdp", "ctx")),
        P(("fsdp", "ctx"), None),
        P(("fsdp", "ctx"), None),
        P(("fsdp", "ctx")),
        P(("fsdp", "ctx"), None),
        P("fsdp", "ctx"),
        P("fsdp", "ctx"),
        P("fsdp", "ctx"),
        P("fsdp", "ctx"),
        P("fsdp", "ctx"),
        P("fsdp", "ctx"),
    )
    return jax.shard_map(
        body,
        mesh=mesh,
        in_specs=placed,
        out_specs=(
            P("fsdp", "ctx", None),
            P("fsdp", "ctx", None),
            P(("fsdp", "ctx")),
            P(("fsdp", "ctx"), None),
            P(("fsdp", "ctx"), None),
            P(("fsdp", "ctx")),
            P(("fsdp", "ctx"), None),
            P(("fsdp", "ctx"), None),
            P(("fsdp", "ctx")),
            P(("fsdp", "ctx"), None),
            P("fsdp", "ctx"),
            P("fsdp", "ctx"),
            P("fsdp", "ctx"),
            P("fsdp", "ctx"),
            P("fsdp", "ctx"),
            P("fsdp", "ctx"),
        ),
        check_vma=False,
    )
```

```python
import functools
import math

import jax
import jax.numpy as jnp
from jax import lax
from jax.experimental import pallas as pl
from jax.experimental.pallas import tpu as pltpu
from jax.sharding import PartitionSpec as P

D = 2048
H = 16
DN = 128
DR = 64
DV = 128
LAT = 512
TOP = 6
SEGS = 13
PACK = 2048

MESH = pl.DeviceIdType.MESH
BF = jnp.bfloat16
F32 = jnp.float32

epsilon = 1e-06
rope_base = 10000.0


def multiply(left, right):
    return jnp.dot(left, right, preferred_element_type=F32)


def multiply_transposed(left, right):
    return lax.dot_general(left, right, (((1,), (1,)), ((), ())), preferred_element_type=F32)


def transposed_multiply(left, right):
    return lax.dot_general(left, right, (((0,), (0,)), ((), ())), preferred_element_type=F32)


def normalize(tensor_in, gain_vec):
    inverse = lax.rsqrt(jnp.mean(tensor_in * tensor_in, axis=-1, keepdims=True) + epsilon)
    normed = tensor_in * inverse
    return (normed, inverse, normed * gain_vec)


def normalize_back(grad_out, normed, inverse, gain_vec):
    weighted = grad_out * gain_vec
    centre = jnp.mean(weighted * normed, axis=-1, keepdims=True)
    return (inverse * (weighted - normed * centre), jnp.sum(grad_out * normed, axis=0))


def rotate(tensor_in, cosine, sine):
    half_width = tensor_in.shape[-1] // 2
    former = tensor_in[..., :half_width]
    latter = tensor_in[..., half_width:]
    return jnp.concatenate(
        [former * cosine - latter * sine, latter * cosine + former * sine], axis=-1
    )


def tree_mask(segment_ids, path_table, first_row, row_count):
    labels = jnp.arange(SEGS, dtype=jnp.int32)
    own_ids = lax.dynamic_slice_in_dim(segment_ids, first_row, row_count)
    own_hot = (own_ids[:, None] == labels[None, :]).astype(BF)
    all_hot = (segment_ids[:, None] == labels[None, :]).astype(BF)
    ancestry = multiply(own_hot, path_table.astype(BF)).astype(BF)
    related = multiply_transposed(ancestry, all_hot)
    places = jnp.arange(segment_ids.shape[0], dtype=jnp.int32)
    queries = first_row + jnp.arange(row_count, dtype=jnp.int32)
    allowed = (related > 0) & (places[None, :] <= queries[:, None])
    positions = jnp.sum(allowed.astype(jnp.int32), axis=1) - 1
    return (allowed, positions)


def three_parts(value):
    first = lax.reduce_precision(value, 8, 7)
    second = lax.reduce_precision(value - first, 8, 7)
    third = value - first - second
    return (first.astype(BF), second.astype(BF), third.astype(BF))


class Ring:
    def __init__(self, nf, nc):
        self.nf, self.chips = nf, nc // 2
        half = self.chips // 2
        if nf == 2:
            self.place = lambda p: (1 - p // half) * 2 * p + (p // half) * (4 * half - 1 - 2 * p)
            self.where = lambda j: (1 - j % 2) * (j // 2) + (j % 2) * (2 * half - 1 - j // 2)
        else:
            self.place = lambda p: (1 - p // half) * p + (p // half) * (3 * half - 1 - p)
            self.where = self.place

    def here(self):
        f, c = lax.axis_index("fsdp"), lax.axis_index("ctx")
        core = c % 2
        return f, c, core, self.where(c // 2), 1 - 2 * core

    def device(self, position, core):
        return self.place((position + 2 * self.chips) % self.chips) * 2 + core


def greet(ring, f, c, core, p, way, over_fsdp):
    barrier = pltpu.get_barrier_semaphore()
    targets = [(f, ring.device(p - way, core)), (f, c + 1 - 2 * core)]
    if over_fsdp:
        targets += [((f + k) % ring.nf, c) for k in range(1, ring.nf)]
    for target in targets:
        pl.semaphore_signal(barrier, inc=1, device_id=target, device_id_type=MESH)
    pl.semaphore_wait(barrier, len(targets))


def gather_kernel(ring, wide, leads, count, swaps, *refs):
    swap_ins, swap_outs = refs[count : count + swaps], refs[2 * count + swaps : 2 * (count + swaps)]
    ins, outs = refs[:count], refs[count + swaps : 2 * count + swaps]
    own_sem, yss, yrs, rss, rrs, sss, srs, wss, wrs = refs[2 * (count + swaps) :]
    f, c, core, p, way = ring.here()
    n, nf = ring.chips, ring.nf
    greet(ring, f, c, core, p, way, any(wide))
    to_next = (f, ring.device(p + way, core))
    to_twin = (f, c + 1 - 2 * core)
    started, own = [], []

    def remote(src, dst, ss, rs, dev):
        return pltpu.make_async_remote_copy(
            src_ref=src, dst_ref=dst, send_sem=ss, recv_sem=rs, device_id=dev, device_id_type=MESH
        )

    streams, late = [], []
    number = 0
    for i in range(count):
        if wide[i]:
            streams.append((number, i, f, ins[i]))
            number += 1
        else:
            for a in range(leads[i]):
                streams.append((number, i, a, ins[i].at[a]))
                number += 1
    first = len(streams)
    yn = 0
    for i in range(count):
        if wide[i]:
            for k in range(1, nf):
                late.append((number, i, (f - k + nf) % nf, k, yn))
                number += 1
                yn += 1

    def send_ring(s, number, i, lead, owner, src):
        cp = remote(src, outs[i].at[lead, owner], rss.at[s, number], rrs.at[s, number], to_next)
        cp.start()
        started.append(cp)

    def send_twin(s, number, i, lead, owner, src):
        cp = remote(src, outs[i].at[lead, owner], sss.at[s, number], srs.at[s, number], to_twin)
        cp.start()
        started.append(cp)

    for number, i, lead, k, y in late:
        cp = remote(ins[i], outs[i].at[f, c], yss.at[y], yrs.at[y], ((f + k) % nf, c))
        cp.start()
        started.append(cp)
    for number, i, lead, src in streams:
        send_ring(0, number, i, lead, c, src)
    for number, i, lead, src in streams:
        send_twin(0, number, i, lead, c, src)
        cp = pltpu.make_async_copy(src, outs[i].at[lead, c], own_sem.at[number])
        cp.start()
        own.append(cp)
    everything = [(number, i, lead) for number, i, lead, _ in streams]
    everything += [(number, i, lead) for number, i, lead, _, _ in late]
    for number, i, lead, k, y in late:
        here = outs[i].at[lead, c]
        remote(here, here, yss.at[y], yrs.at[y], to_next).wait_recv()
        send_ring(0, number, i, lead, c, here)
        send_twin(0, number, i, lead, c, here)
    swapped = []
    for i in range(swaps):
        cp = remote(swap_ins[i], swap_outs[i], wss.at[i], wrs.at[i], ((f + 1) % nf, c))
        cp.start()
        swapped.append(cp)
    for s in range(1, n):
        owner = ring.device(p - way * s, core)
        for number, i, lead in everything:
            here = outs[i].at[lead, owner]
            remote(here, here, rss.at[s - 1, number], rrs.at[s - 1, number], to_next).wait_recv()
            if s < n - 1:
                send_ring(s, number, i, lead, owner, here)
            send_twin(s, number, i, lead, owner, here)
    for s in range(n):
        owner = ring.device(p + way * s, 1 - core)
        for number, i, lead in everything:
            here = outs[i].at[lead, owner]
            remote(here, here, sss.at[s, number], srs.at[s, number], to_twin).wait_recv()
    for cp in own:
        cp.wait()
    for cp in started:
        cp.wait_send()
    for cp in swapped:
        cp.wait()


def ring_gather(ring, number, arrays, wide, swaps=()):
    n, nf = ring.chips, ring.nf
    leads = [1 if w else a.shape[0] for a, w in zip(arrays, wide)]
    shapes, streams, late, size = [], 0, 0, 0
    for a, w in zip(arrays, wide):
        if w:
            shapes.append(jax.ShapeDtypeStruct((nf, 2 * n) + a.shape, a.dtype))
            streams += nf
            late += nf - 1
        else:
            shapes.append(jax.ShapeDtypeStruct((a.shape[0], 2 * n) + a.shape[1:], a.dtype))
            streams += a.shape[0]
        size += shapes[-1].size * 2
    dma = pltpu.SemaphoreType.DMA
    shapes += [jax.ShapeDtypeStruct(a.shape, a.dtype) for a in swaps]
    return pl.pallas_call(
        functools.partial(
            gather_kernel, ring, tuple(wide), tuple(leads), len(arrays), len(swaps)
        ),
        out_shape=shapes,
        in_specs=[pl.BlockSpec(memory_space=pl.ANY)] * len(shapes),
        out_specs=[pl.BlockSpec(memory_space=pl.ANY)] * len(shapes),
        scratch_shapes=[
            dma((streams,)),
            dma((max(1, late),)),
            dma((max(1, late),)),
            dma((n - 1, streams)),
            dma((n - 1, streams)),
            dma((n, streams)),
            dma((n, streams)),
            dma((max(1, len(swaps)),)),
            dma((max(1, len(swaps)),)),
        ],
        compiler_params=pltpu.CompilerParams(collective_id=number, has_side_effects=True),
        cost_estimate=pl.CostEstimate(flops=0, bytes_accessed=2 * size, transcendentals=0),
        name="ring_gather_%d" % number,
    )(*arrays, *swaps)


def front_kernel(ring, latent_part, *refs):
    ins, swap_ins, (normed, cosine, sine) = refs[:5], refs[5:7], refs[7:10]
    outs, swap_outs, (keys, hidden, latent) = refs[10:15], refs[15:17], refs[17:20]
    small_held, kva_held, own_keys = refs[20:23]
    own_sem, yss, yrs, rss, rrs, sss, srs, wss, wrs, load_sem = refs[23:]
    f, c, core, p, way = ring.here()
    n, nf = ring.chips, ring.nf
    nc = 2 * n
    greet(ring, f, c, core, p, way, True)
    to_next, to_twin = (f, ring.device(p + way, core)), (f, c + 1 - 2 * core)
    to_other, other = ((f + 1) % nf, c), (f + 1) % nf
    started, own = [], {}

    def remote(src, dst, ss, rs, dev):
        return pltpu.make_async_remote_copy(
            src_ref=src, dst_ref=dst, send_sem=ss, recv_sem=rs, device_id=dev, device_id_type=MESH
        )

    def place(number, owner):
        if number < 10:
            return outs[number // 2].at[(f + number % 2) % nf, owner]
        return keys.at[number - 10, owner]

    def send(s, number, owner, src, ring_too=True):
        dst = place(number, owner)
        if ring_too:
            cp = remote(src, dst, rss.at[s, number], rrs.at[s, number], to_next)
            cp.start()
            started.append(cp)
        cp = remote(src, dst, sss.at[s, number], srs.at[s, number], to_twin)
        cp.start()
        started.append(cp)

    def keep(number, src):
        own[number] = pltpu.make_async_copy(src, place(number, c), own_sem.at[number])
        own[number].start()

    def pass_on(s, number):
        owner = ring.device(p - way * s, core)
        here = place(number, owner)
        remote(here, here, rss.at[s - 1, number], rrs.at[s - 1, number], to_next).wait_recv()
        send(s, number, owner, here, s < n - 1)

    def late(i):
        here = outs[i].at[other, c]
        remote(here, here, yss.at[i], yrs.at[i], to_next).wait_recv()
        send(0, 2 * i + 1, c, here)

    def from_twin(s, number):
        here = place(number, ring.device(p + way * s, 1 - core))
        remote(here, here, sss.at[s, number], srs.at[s, number], to_twin).wait_recv()

    for i in range(5):
        cp = remote(ins[i], outs[i].at[f, c], yss.at[i], yrs.at[i], to_other)
        cp.start()
        started.append(cp)
        send(0, 2 * i, c, ins[i])
        keep(2 * i, ins[i])
    swapped = []

    def swap():
        for i in range(2):
            cp = remote(swap_ins[i], swap_outs[i], wss.at[i], wrs.at[i], to_other)
            cp.start()
            swapped.append(cp)

    bulk = [functools.partial(late, i) for i in (2, 3, 4)] + [swap]
    bulk += [functools.partial(pass_on, s, number) for s in range(1, n) for number in range(4, 10)]

    def some(count):
        for work in bulk[:count]:
            work()
        del bulk[:count]

    late(0)
    late(1)
    for s in range(1, n):
        for number in range(4):
            pass_on(s, number)
        some(3)
    for number in range(4):
        for s in range(n):
            from_twin(s, number)
    for number in (0, 2):
        own[number].wait()
    loads = [
        pltpu.make_async_copy(outs[i], held, load_sem.at[i])
        for i, held in enumerate((small_held, kva_held))
    ]
    for cp in loads:
        cp.start()
    for cp in loads:
        cp.wait()
    lane = lax.broadcasted_iota(jnp.int32, (1, 128), 1)

    def gain(row, first, each):
        total = jnp.zeros((1, 128), F32)
        for k in range(128 // each):
            d = first // each + k
            own_row = small_held[d // nc, d % nc, row : row + 1, :].astype(F32)
            total = jnp.where(lane // each == k, own_row, total)
        return total

    for start in range(0, D, 128):
        cut = slice(start, start + 128)
        hidden[:, cut] = (normed[:, cut] * gain(0, start, D // (nf * nc))).astype(BF)
    latent[:, LAT:] = jnp.zeros((latent.shape[0], 128), F32)
    latent[:, : LAT + DR] = multiply(hidden[...], kva_held[...].reshape(D, LAT + DR))
    trees, tok = own_keys.shape[:2]
    low = latent[:, :LAT]
    inverse = lax.rsqrt(jnp.mean(low * low, axis=-1, keepdims=True) + epsilon)
    for start in range(0, LAT, 128):
        cut = slice(start, start + 128)
        key = (latent[:, cut] * inverse * gain(1, start, latent_part)).astype(BF)
        for a in range(trees):
            own_keys[a, :, cut] = key[a * tok : (a + 1) * tok]
    half = DR // 2
    former, latter = latent[:, LAT : LAT + half], latent[:, LAT + half : LAT + DR]
    turned = (
        (former * cosine[...] - latter * sine[...]).astype(BF),
        (latter * cosine[...] + former * sine[...]).astype(BF),
    )
    own_keys[:, :, LAT:] = jnp.zeros((trees, tok, 128), BF)
    for a in range(trees):
        for k in range(2):
            own_keys[a, :, LAT + k * half : LAT + (k + 1) * half] = turned[k][a * tok : (a + 1) * tok]
    for a in range(trees):
        send(0, 10 + a, c, own_keys.at[a])
        keep(10 + a, own_keys.at[a])
    for s in range(1, n):
        some(3)
        for a in range(trees):
            pass_on(s, 10 + a)
    some(len(bulk))
    for number in range(4, 10 + trees):
        for s in range(n):
            from_twin(s, number)
    for number in own:
        if number not in (0, 2):
            own[number].wait()
    for cp in started:
        cp.wait_send()
    for cp in swapped:
        cp.wait()


def front(ring, number, arrays, swaps, normed, cosine, sine, latent_part, trees, tok):
    n, nf = ring.chips, ring.nf
    rows = normed.shape[0]
    shapes = [jax.ShapeDtypeStruct((nf, 2 * n) + a.shape, a.dtype) for a in arrays]
    size = sum(a.size * 2 for a in shapes)
    shapes += [jax.ShapeDtypeStruct(a.shape, a.dtype) for a in swaps]
    shapes += [
        jax.ShapeDtypeStruct((trees, 2 * n, tok, LAT + 128), BF),
        jax.ShapeDtypeStruct((rows, D), BF),
        jax.ShapeDtypeStruct((rows, LAT + 128), F32),
    ]
    dma = pltpu.SemaphoreType.DMA
    streams = 10 + trees
    vmem, far = pl.BlockSpec(memory_space=pltpu.VMEM), pl.BlockSpec(memory_space=pl.ANY)
    return pl.pallas_call(
        functools.partial(front_kernel, ring, latent_part),
        out_shape=shapes,
        in_specs=[far] * 7 + [vmem] * 3,
        out_specs=[far] * 8 + [vmem] * 2,
        scratch_shapes=[
            pltpu.VMEM(shapes[0].shape, BF),
            pltpu.VMEM(shapes[1].shape, BF),
            pltpu.VMEM((trees, tok, LAT + 128), BF),
            dma((streams,)),
            dma((5,)),
            dma((5,)),
            dma((n - 1, streams)),
            dma((n - 1, streams)),
            dma((n, streams)),
            dma((n, streams)),
            dma((2,)),
            dma((2,)),
            dma((2,)),
        ],
        compiler_params=pltpu.CompilerParams(
            collective_id=number, has_side_effects=True, vmem_limit_bytes=60 << 20
        ),
        cost_estimate=pl.CostEstimate(flops=0, bytes_accessed=2 * size, transcendentals=0),
        name="front",
    )(*arrays, *swaps, normed, cosine, sine)


def add_rows(shape, work):
    rows = shape[0]
    step = 16 if rows % 16 == 0 else rows

    def one(r, carry):
        work(pl.ds(pl.multiple_of(r * step, step), step))
        return carry

    lax.fori_loop(0, rows // step, one, 0)


class Products:
    tile = 256

    def __init__(self, cuts, pairs, lefts, rights, outs, held, *rest):
        self.cuts, self.pairs, self.lefts, self.rights, self.outs = cuts, pairs, lefts, rights, outs
        self.held = held
        self.tiles, self.stage, self.load_sem, self.tile_sem, self.store_sem = rest
        self.units = [
            (j, m) for j in range(len(pairs)) for m in range(0, cuts[pairs[j][0]][1], self.tile)
        ]
        self.done, self.loaded, self.stores = 0, set(), [None, None]
        self.ship, self.shipped = {}, []

    def deliver(self):
        for j in sorted(self.ship):
            last = max(i for i, unit in enumerate(self.units) if unit[0] == j)
            if self.done > last + 2 or (self.done == len(self.units) and self.stores == []):
                cp = self.ship.pop(j)()
                cp.start()
                self.shipped.append(cp)

    def fetch(self, number):
        j, m = self.units[number]
        left = self.pairs[j][0]
        source, slot = self.lefts[left], number % 2
        return pltpu.make_async_copy(
            source.at[:, pl.ds(self.cuts[left][0] + m, self.tile)],
            self.tiles.at[slot, pl.ds(0, source.shape[0]), :],
            self.tile_sem.at[slot],
        )

    def start(self):
        self.fetch(0).start()
        self.loads = []
        for i, source in enumerate(self.rights):
            cp = pltpu.make_async_copy(source, self.held[i], self.load_sem.at[i])
            cp.start()
            self.loads.append(cp)

    def run(self, upto):
        while self.done < min(upto, len(self.units)):
            j, m = self.units[self.done]
            left, right, first, width = self.pairs[j]
            if right not in self.loaded:
                self.loads[right].wait()
                self.loaded.add(right)
            self.fetch(self.done).wait()
            if self.done + 1 < len(self.units):
                self.fetch(self.done + 1).start()
            slot = self.done % 2
            value = lax.dot_general(
                self.tiles[slot, pl.ds(0, self.lefts[left].shape[0]), :],
                self.held[right][:, pl.ds(first, width)],
                (((0,), (0,)), ((), ())),
                preferred_element_type=F32,
            )
            if self.stores[slot] is not None:
                self.stores[slot].wait()
            self.stage[slot, :, pl.ds(0, width)] = value.astype(BF)
            cp = pltpu.make_async_copy(
                self.stage.at[slot, :, pl.ds(0, width)],
                self.outs[j].at[pl.ds(m, self.tile), :],
                self.store_sem.at[slot],
            )
            cp.start()
            self.stores[slot] = cp
            self.done += 1
            self.deliver()

    def finish(self):
        self.run(len(self.units))
        for cp in self.stores:
            if cp is not None:
                cp.wait()
        self.stores = []
        self.deliver()
        for cp in self.shipped:
            cp.wait()


def reduce_kernel(ring, wide, leads, count, cuts, pairs, ships, *refs):
    njobs = len(pairs)
    nleft = len(cuts)
    nright = 1 + max([p[1] for p in pairs], default=-1)
    nops = nleft + nright
    ins, sources, refs = refs[:count], refs[count : count + nops], refs[count + nops :]
    outs, job_outs, refs = refs[:count], refs[count : count + njobs], refs[count + njobs :]
    ship_outs, refs = refs[: len(ships)], refs[len(ships) :]
    own, twin, got = (refs[k * count : (1 + k) * count] for k in range(3))
    refs = refs[3 * count :]
    wides = sum(wide)
    finals, ygots = refs[:wides], refs[wides : 2 * wides]
    own_sem, tss, trs, rss, rrs, yss, yrs = refs[2 * wides : 2 * wides + 7]
    refs = refs[2 * wides + 7 :]
    jobs = None
    if njobs:
        jobs = Products(
            cuts, pairs, sources[:nleft], sources[nleft:], job_outs, refs[:nright], *refs[nright : nright + 5]
        )
    f, c, core, p, way = ring.here()
    n, nf = ring.chips, ring.nf
    greet(ring, f, c, core, p, way, any(wide) or len(ships) > 0)
    to_next = (f, ring.device(p + way, core))
    to_twin = (f, c + 1 - 2 * core)

    def remote(src, dst, ss, rs, dev):
        return pltpu.make_async_remote_copy(
            src_ref=src, dst_ref=dst, send_sem=ss, recv_sem=rs, device_id=dev, device_id_type=MESH
        )

    streams = []
    for k in range(max(leads)):
        for i in range(count):
            if k < leads[i]:
                lead = (f + 1 + k) % nf if wide[i] else k
                streams.append((len(streams), i, k, lead))
    started, loads = [], {}
    for s in range(n):
        theirs = ring.device(p + way * (1 + s), 1 - core)
        mine = ring.device(p - way * (1 + s), core)
        for number, i, k, lead in streams:
            cp = remote(
                ins[i].at[lead, theirs], twin[i].at[s, k], tss.at[s, number], trs.at[s, number], to_twin
            )
            cp.start()
            started.append(cp)
            cp = pltpu.make_async_copy(
                ins[i].at[lead, mine], own[i].at[s, k], own_sem.at[s, number]
            )
            cp.start()
            loads[s, number] = cp

    if jobs:
        for w, j in enumerate(ships):
            jobs.ship[j] = functools.partial(
                remote, job_outs[j], ship_outs[w], refs[-2].at[w], refs[-1].at[w], ((f + 1) % nf, c)
            )
        jobs.start()

    def wait_parts(s, number, i, k):
        loads[s, number].wait()
        here = twin[i].at[s, k]
        remote(here, here, tss.at[s, number], trs.at[s, number], to_twin).wait_recv()

    def pass_on(s, number, i, k, src):
        cp = remote(src, got[i].at[s, k], rss.at[s, number], rrs.at[s, number], to_next)
        cp.start()
        started.append(cp)

    turn, turns = 0, (n - 1) * len(streams)
    for s in range(n):
        for number, i, k, lead in streams:
            if jobs and s > 0:
                jobs.run(-(-len(jobs.units) * turn // turns))
                turn += 1
            wait_parts(s, number, i, k)
            mine, other = own[i].at[s, k], twin[i].at[s, k]
            if s == 0:

                def start(rows, mine=mine, other=other):
                    mine[rows, :] = (mine[rows, :].astype(F32) + other[rows, :].astype(F32)).astype(BF)

                add_rows(mine.shape, start)
                pass_on(0, number, i, k, mine)
                continue
            came = got[i].at[s - 1, k]
            remote(came, came, rss.at[s - 1, number], rrs.at[s - 1, number], to_next).wait_recv()
            if s < n - 1:

                def middle(rows, mine=mine, other=other, came=came):
                    total = mine[rows, :].astype(F32) + other[rows, :].astype(F32)
                    came[rows, :] = (came[rows, :].astype(F32) + total).astype(BF)

                add_rows(mine.shape, middle)
                pass_on(s, number, i, k, came)
                continue
            if not wide[i]:
                target = outs[i].at[k]
            elif k == nf - 1:
                target = outs[i]
            else:
                target = finals[sum(wide[:i])].at[k]

            def last(rows, mine=mine, other=other, came=came, target=target):
                total = mine[rows, :].astype(F32) + other[rows, :].astype(F32)
                target[rows, :] = (came[rows, :].astype(F32) + total).astype(target.dtype)

            add_rows(mine.shape, last)
            if wide[i] and k < nf - 1:
                w = sum(wide[:i])
                cp = remote(target, ygots[w].at[k], yss.at[w, k], yrs.at[w, k], ((f + 1 + k) % nf, c))
                cp.start()
                started.append(cp)
    for i in range(count):
        if wide[i]:
            w = sum(wide[:i])
            for k in range(nf - 1):
                here = ygots[w].at[k]
                remote(here, here, yss.at[w, k], yrs.at[w, k], to_next).wait_recv()

                def finish(rows, here=here, target=outs[i]):
                    target[rows, :] = target[rows, :] + here[rows, :].astype(F32)

                add_rows(here.shape, finish)
    if jobs:
        jobs.finish()
    for cp in started:
        cp.wait_send()


def ring_reduce(ring, number, arrays, wide, lefts=(), rights=(), cuts=(), pairs=(), ships=()):
    n, nf = ring.chips, ring.nf
    leads = [a.shape[0] for a in arrays]
    more = [jax.ShapeDtypeStruct((cuts[l][1], width), BF) for l, _, _, width in pairs]
    streams = sum(leads)
    block = [a.shape[2:] for a in arrays]
    shapes = [
        jax.ShapeDtypeStruct(b if w else (l,) + b, F32) for b, w, l in zip(block, wide, leads)
    ]
    dma = pltpu.SemaphoreType.DMA
    scratch = [pltpu.VMEM((n, l) + b, BF) for b, l in zip(block, leads)] * 2
    scratch += [pltpu.VMEM((n - 1, l) + b, BF) for b, l in zip(block, leads)]
    scratch += [pltpu.VMEM((nf - 1,) + b, BF) for b, w in zip(block, wide) if w] * 2
    more += [more[j] for j in ships]
    wides = max(1, sum(wide))
    extra = []
    if pairs:
        extra = [pltpu.VMEM(a.shape, BF) for a in rights]
        extra += [
            pltpu.VMEM((2, max(a.shape[0] for a in lefts), Products.tile), BF),
            pltpu.VMEM((2, Products.tile, max(p[3] for p in pairs)), BF),
            dma((len(rights),)),
            dma((2,)),
            dma((2,)),
        ]
    if ships:
        extra += [dma((len(ships),)), dma((len(ships),))]
    return pl.pallas_call(
        functools.partial(
            reduce_kernel, ring, tuple(wide), tuple(leads), len(arrays), tuple(cuts), tuple(pairs), tuple(ships)
        ),
        out_shape=shapes + more,
        in_specs=[pl.BlockSpec(memory_space=pl.ANY)] * (len(arrays) + len(lefts) + len(rights)),
        out_specs=[pl.BlockSpec(memory_space=pltpu.VMEM)] * len(arrays)
        + [pl.BlockSpec(memory_space=pl.ANY)] * len(more),
        scratch_shapes=scratch
        + [
            dma((n, streams)),
            dma((n, streams)),
            dma((n, streams)),
            dma((n - 1, streams)),
            dma((n - 1, streams)),
            dma((wides, max(1, nf - 1))),
            dma((wides, max(1, nf - 1))),
        ]
        + extra,
        compiler_params=pltpu.CompilerParams(
            collective_id=number, has_side_effects=True, vmem_limit_bytes=60 << 20
        ),
        cost_estimate=pl.CostEstimate(flops=0, bytes_accessed=1 << 20, transcendentals=0),
        name="ring_reduce_%d" % number,
    )(*arrays, *lefts, *rights)


def expert_kernel(nf, experts, fp, bundle_slots, *refs):
    x_ref, g_ref, probs_ref, slot_ref, column_ref = refs[:5]
    weights, refs = refs[5 : 5 + 4 * nf], refs[5 + 4 * nf :]
    back_ref, out_ref, delta_ref, rows_ref, grads_ref, hid_ref, gg_ref, ug_ref, act_ref = refs[:9]
    w_gate, w_up, w_down, w_shared, pre_gate, pre_up, pre_in, pre_s, raw, sems = refs[9:]
    mine = lax.axis_index("ctx")
    held = (w_gate, w_up, w_down, w_shared)
    part = w_gate.shape[0] // nf
    wide = w_gate.shape[0]
    copies = [
        [
            pltpu.make_async_copy(
                weights[4 * k + i], held[i].at[pl.ds(k * part, part)], sems.at[i, k]
            )
            for k in range(nf)
        ]
        for i in range(4)
    ]
    first = pl.program_id(0) == 0

    def ready(i):
        @pl.when(first)
        def _():
            for cp in copies[i]:
                cp.wait()

    @pl.when(first)
    def _():
        for i in (3, 0, 1, 2):
            for cp in copies[i]:
                cp.start()

    def nt(left, right):
        return lax.dot_general(left, right, (((1,), (1,)), ((), ())), preferred_element_type=F32)

    bundles, _, rows = slot_ref.shape
    lane = lax.broadcasted_iota(jnp.int32, (rows, 128), 1)
    own_lane = (lane % experts == mine) & (lane < 3 * experts)
    puts, row_gates = [], []
    for b in range(bundles):
        cut, spot = pl.ds(b * rows, rows), pl.ds(b * bundle_slots, bundle_slots)
        takes = (
            slot_ref[b] == lax.broadcasted_iota(jnp.int32, (bundle_slots, rows), 0)
        ).astype(F32).astype(BF)
        puts.append(
            (
                column_ref[cut, :] == lax.broadcasted_iota(jnp.int32, (rows, bundle_slots), 1)
            ).astype(F32).astype(BF)
        )
        own = jnp.where(own_lane, probs_ref[cut, :].astype(F32), 0.0)
        row_gates.append(jnp.sum(own, axis=1, keepdims=True))
        gate = jnp.sum(multiply(takes, own.astype(BF)), axis=1, keepdims=True)
        for start in range(0, wide, 512):
            piece = pl.ds(start, 512)
            rows_ref[spot, piece] = multiply(takes, x_ref[cut, piece]).astype(BF)
            taken = multiply(takes, g_ref[cut, piece])
            raw[spot, piece] = taken.astype(BF)
            grads_ref[spot, piece] = (gate * taken).astype(BF)

    ready(3)
    pre_s[:, : 2 * fp] = multiply(x_ref[...], w_shared[:, : 2 * fp])
    pre_s[:, 2 * fp :] = multiply(g_ref[...], w_shared[:, 2 * fp :])

    def activate(gate_pre, up_pre, inner):
        sig = jax.nn.sigmoid(gate_pre)
        activated = gate_pre * sig
        hidden = activated * up_pre
        gate_grad = inner * up_pre * sig * (1.0 + gate_pre * (1.0 - sig))
        return hidden.astype(BF), gate_grad.astype(BF), (inner * activated).astype(BF)

    step = 32

    def shared_rows(r, carry):
        at = pl.ds(pl.multiple_of(r * step, step), step)
        for start in range(0, fp, 128):
            cuts = [pl.ds(i * fp + start, 128) for i in range(3)]
            hidden, gate_grad, up_grad = activate(*(pre_s[at, c] for c in cuts))
            act_ref[at, cuts[0]] = gate_grad
            act_ref[at, cuts[1]] = up_grad
            act_ref[at, cuts[2]] = hidden
        return carry

    lax.fori_loop(0, pre_s.shape[0] // step, shared_rows, 0)

    ready(0)
    pre_gate[...] = multiply(rows_ref[...], w_gate[...])
    ready(1)
    pre_up[...] = multiply(rows_ref[...], w_up[...])
    ready(2)
    pre_in[...] = multiply(grads_ref[...], w_down[...])

    def expert_rows(r, carry):
        at = pl.ds(pl.multiple_of(r * step, step), step)
        for start in range(0, hid_ref.shape[1], 128):
            c = pl.ds(start, 128)
            hidden, gate_grad, up_grad = activate(pre_gate[at, c], pre_up[at, c], pre_in[at, c])
            hid_ref[at, c] = hidden
            gg_ref[at, c] = gate_grad
            ug_ref[at, c] = up_grad
        return carry

    lax.fori_loop(0, hid_ref.shape[0] // step, expert_rows, 0)

    delta = 0.0
    for start in range(0, wide, 512):
        piece = pl.ds(start, 512)
        e_back = nt(gg_ref[...], w_gate[piece, :]) + nt(ug_ref[...], w_up[piece, :])
        e_back = e_back.astype(BF)
        e_out = nt(hid_ref[...], w_down[piece, :]).astype(BF)
        delta = delta + jnp.sum(
            raw[:, piece].astype(F32) * e_out.astype(F32), axis=1, keepdims=True
        )
        for b in range(bundles):
            cut = pl.ds(b * rows, rows)
            spot = slice(b * bundle_slots, (b + 1) * bundle_slots)
            s_back = nt(act_ref[cut, : 2 * fp], w_shared[piece, : 2 * fp])
            back_ref[cut, piece] = (multiply(puts[b], e_back[spot]) + s_back).astype(BF)
            s_out = nt(act_ref[cut, 2 * fp :], w_shared[piece, 2 * fp :])
            out_ref[cut, piece] = (row_gates[b] * multiply(puts[b], e_out[spot]) + s_out).astype(BF)
    for b in range(bundles):
        own = delta[b * bundle_slots : (b + 1) * bundle_slots]
        high = own.astype(BF).astype(F32)
        middle = (own - high).astype(BF).astype(F32)
        low = own - high - middle
        spread = jnp.where(lane[:bundle_slots] < experts, high, jnp.where(lane[:bundle_slots] < 2 * experts, middle, low))
        spread = jnp.where(own_lane[:bundle_slots], spread, 0.0).astype(BF)
        delta_ref[pl.ds(b * rows, rows), :] = multiply(puts[b], spread).astype(BF)


def run_experts(nf, experts, capacity, tok_loc, tree_rows, tree_grads, tree_probs, slot, weights):
    rows, wide = tree_rows.shape
    bundles, per = slot.shape
    bundle_slots = capacity * (per // tok_loc)
    hidden, fp = weights[0][0].shape[1], weights[0][3].shape[1] // 3
    group = 2 if bundles % 2 == 0 else 1
    steps = bundles // group
    block, slots = rows // steps, group * bundle_slots
    flat = [w for piece in weights for w in piece]
    by_row = lambda width: pl.BlockSpec((block, width), lambda i: (i, 0))
    by_slot = lambda width: pl.BlockSpec((slots, width), lambda i: (i, 0))
    any_spec = pl.BlockSpec(memory_space=pl.ANY)
    shape = lambda n, width: jax.ShapeDtypeStruct((n, width), BF)
    total = steps * slots
    flops = 2 * (6 * total * wide * hidden + 6 * rows * wide * fp + 4 * rows * bundle_slots * wide)
    return pl.pallas_call(
        functools.partial(expert_kernel, nf, experts, fp, bundle_slots),
        grid=(steps,),
        out_shape=[shape(rows, wide), shape(rows, wide), shape(rows, 128)]
        + [shape(total, wide)] * 2
        + [shape(total, hidden)] * 3
        + [shape(rows, 3 * fp)],
        in_specs=[
            by_row(wide),
            by_row(wide),
            by_row(128),
            pl.BlockSpec((group, 1, per), lambda i: (i, 0, 0)),
            pl.BlockSpec((block, 1), lambda i: (i, 0)),
        ]
        + [any_spec] * len(flat),
        out_specs=[by_row(wide), by_row(wide), by_row(128)]
        + [by_slot(wide)] * 2
        + [by_slot(hidden)] * 3
        + [by_row(3 * fp)],
        scratch_shapes=[pltpu.VMEM((wide, hidden), BF)] * 3
        + [pltpu.VMEM((wide, 3 * fp), BF)]
        + [pltpu.VMEM((slots, hidden), F32)] * 3
        + [pltpu.VMEM((block, 3 * fp), F32), pltpu.VMEM((slots, wide), BF)]
        + [pltpu.SemaphoreType.DMA((4, nf))],
        compiler_params=pltpu.CompilerParams(vmem_limit_bytes=61 << 20),
        cost_estimate=pl.CostEstimate(
            flops=flops, bytes_accessed=10 * rows * wide, transcendentals=total * hidden
        ),
        name="experts",
    )(tree_rows, tree_grads, tree_probs, slot[:, None, :], slot.reshape(rows, 1), *flat)


def nt(left, right):
    return lax.dot_general(left, right, (((1,), (1,)), ((), ())), preferred_element_type=F32)


def tn(left, right):
    return lax.dot_general(left, right, (((0,), (0,)), ((), ())), preferred_element_type=F32)


HEADS = 4


def attend_kernel(
    scale, hidden, cosine, sine, keys, allowed, expand, tokens, wq_hbm, wo_hbm,
    cat, lse, mixed, heads, residual, nope, w_out, w_part, query, sem, part_sem,
):
    trees, tok = cat.shape[0], cat.shape[2]
    copy = pltpu.make_async_copy(wo_hbm, w_out, sem)
    pair = 2 * (DN + DR)

    def part(i):
        return pltpu.make_async_copy(
            wq_hbm.at[:, pl.ds(i * pair, pair)], w_part.at[i % 2], part_sem.at[i % 2]
        )

    part(0).start()
    cat[:, :, :, LAT + DR :] = jnp.zeros((trees, H, tok, 128 - DR), BF)
    half = DR // 2
    for i in range(H // 2):
        part(i).wait()
        if i + 1 < H // 2:
            part(i + 1).start()
        else:
            copy.start()
        query[...] = multiply(hidden[...], w_part[i % 2])
        for h in (2 * i, 2 * i + 1):
            first = h % 2 * (DN + DR)
            nope[:, h * DN : (h + 1) * DN] = query[:, first : first + DN].astype(BF)
            former = query[:, first + DN : first + DN + half]
            latter = query[:, first + DN + half : first + DN + DR]
            turned = (
                (former * cosine[...] - latter * sine[...]).astype(BF),
                (latter * cosine[...] + former * sine[...]).astype(BF),
            )
            low = nt(nope[:, h * DN : (h + 1) * DN], expand[:, h * (DN + DV) : h * (DN + DV) + DN])
            low = low.astype(BF)
            for b in range(trees):
                rows = slice(b * tok, (b + 1) * tok)
                cat[b, h, :, :LAT] = low[rows]
                cat[b, h, :, LAT : LAT + half] = turned[0][rows]
                cat[b, h, :, LAT + half : LAT + DR] = turned[1][rows]

    def group(i, carry):
        b, g = i // (H // HEADS), i % (H // HEADS) * HEADS
        query = cat[b, pl.ds(g, HEADS)].reshape(HEADS * tok, -1)
        scores = nt(query, keys[b]) * scale
        scores = scores.reshape(HEADS, tok, -1)
        scores = jnp.where(allowed[b][None] > 0, scores, -1e30)
        highest = jnp.max(scores, axis=-1, keepdims=True)
        raised = jnp.exp(scores - highest)
        total = jnp.sum(raised, axis=-1, keepdims=True)
        lse[b, pl.ds(g, HEADS)] = highest + jnp.log(total)
        probs = (raised * (1.0 / total)).astype(BF).reshape(HEADS * tok, -1)
        mix = multiply(probs, keys[b, :, :LAT]).astype(BF)
        mixed[b, pl.ds(g, HEADS)] = mix.reshape(HEADS, tok, LAT)
        return carry

    lax.fori_loop(0, trees * (H // HEADS), group, 0)
    for h in range(H):
        mix = jnp.concatenate([mixed[b, h] for b in range(trees)], axis=0)
        value = expand[:, h * (DN + DV) + DN : (h + 1) * (DN + DV)]
        heads[:, h * DV : (h + 1) * DV] = multiply(mix, value).astype(BF)
    copy.wait()
    for start in range(0, D, 512):
        cut = slice(start, start + 512)
        residual[:, cut] = tokens[:, cut].astype(F32) + multiply(heads[...], w_out[:, cut])


def attend(hidden, cosine, sine, keys, allowed, expand, tokens, w_query, w_output, tok, scale):
    rows = tokens.shape[0]
    trees = rows // tok
    vmem, far = pl.BlockSpec(memory_space=pltpu.VMEM), pl.BlockSpec(memory_space=pl.ANY)
    length, width = keys.shape[1:]
    return pl.pallas_call(
        functools.partial(attend_kernel, scale),
        out_shape=[
            jax.ShapeDtypeStruct((trees, H, tok, width), BF),
            jax.ShapeDtypeStruct((trees, H, tok, 1), F32),
            jax.ShapeDtypeStruct((trees, H, tok, LAT), BF),
            jax.ShapeDtypeStruct((rows, H * DV), BF),
            jax.ShapeDtypeStruct((rows, D), F32),
            jax.ShapeDtypeStruct((rows, H * DN), BF),
        ],
        in_specs=[vmem] * 7 + [far] * 2,
        out_specs=[vmem] * 6,
        scratch_shapes=[
            pltpu.VMEM(w_output.shape, BF),
            pltpu.VMEM((2, D, 2 * (DN + DR)), BF),
            pltpu.VMEM((rows, 2 * (DN + DR)), F32),
            pltpu.SemaphoreType.DMA,
            pltpu.SemaphoreType.DMA((2,)),
        ],
        compiler_params=pltpu.CompilerParams(vmem_limit_bytes=56 << 20),
        cost_estimate=pl.CostEstimate(
            flops=2 * rows * H * length * 1152, bytes_accessed=30 << 20, transcendentals=rows * H * length
        ),
        name="attend",
    )(hidden, cosine, sine, keys, allowed, expand, tokens, w_query, w_output)


def attend_back_kernel(
    scale, grad, w_out, expand, cat, keys, lse, allowed, mixed, nope, cosine, sine, wq_hbm, keys_grad,
    query_grad, hidden_grad, expand_grad, heads_grad, mix_grad, low_probs, score_grad, cat_grad,
    rope_grad, w_part, part_sem,
):
    trees, tok = cat.shape[0], cat.shape[2]
    size = w_part.shape[1]
    parts = D // size

    def part(i):
        return pltpu.make_async_copy(
            wq_hbm.at[pl.ds(i * size, size), :], w_part.at[i % 2], part_sem.at[i % 2]
        )

    part(0).start()
    for start in range(0, H * DV, 512):
        heads_grad[:, start : start + 512] = nt(grad[...], w_out[start : start + 512, :]).astype(BF)
    for h in range(H):
        value = expand[:, h * (DN + DV) + DN : (h + 1) * (DN + DV)]
        own = heads_grad[:, h * DV : (h + 1) * DV]
        back = nt(own, value).astype(BF)
        for b in range(trees):
            mix_grad[b, h] = back[b * tok : (b + 1) * tok]
        mix = jnp.concatenate([mixed[b, h] for b in range(trees)], axis=0)
        expand_grad[:, h * (DN + DV) + DN : (h + 1) * (DN + DV)] = tn(mix, own).astype(BF)
    for b in range(trees):

        def group(i, carry, b=b):
            g = i * HEADS
            rows = pl.ds(pl.multiple_of(g * tok, HEADS * tok), HEADS * tok)
            query = cat[b, pl.ds(g, HEADS)].reshape(HEADS * tok, -1)
            mix = mix_grad[b, pl.ds(g, HEADS)].reshape(HEADS * tok, -1)
            scores = (nt(query, keys[b]) * scale).reshape(HEADS, tok, -1)
            probs = jnp.where(
                allowed[b][None] > 0, jnp.exp(scores - lse[b, pl.ds(g, HEADS)]), 0.0
            ).reshape(HEADS * tok, -1)
            prob_grad = nt(mix, keys[b, :, :LAT])
            centre = jnp.sum(probs * prob_grad, axis=-1, keepdims=True)
            low_probs[rows, :] = probs.astype(BF)
            own = (probs * (prob_grad - centre)).astype(BF)
            score_grad[rows, :] = own
            back = (multiply(own, keys[b]) * scale).reshape(HEADS, tok, -1)
            cat_grad[b, pl.ds(g, HEADS)] = back[..., :LAT].astype(BF)
            for k in range(HEADS):
                rope_grad[b, g + k] = back[k, :, LAT:]
            return carry

        lax.fori_loop(0, H // HEADS, group, 0)
        query = cat[b].reshape(H * tok, -1)
        mix = mix_grad[b].reshape(H * tok, -1)
        length = keys.shape[1]
        for start in range(0, length, 256):
            cut = slice(start, start + 256)
            total = tn(score_grad[:, cut], query) * scale
            keys_grad[b, cut, :LAT] = (total[:, :LAT] + tn(low_probs[:, cut], mix)).astype(BF)
            keys_grad[b, cut, LAT:] = total[:, LAT:].astype(BF)
    half = DR // 2
    for h in range(H):
        low = jnp.concatenate([cat_grad[b, h] for b in range(trees)], axis=0)
        key = expand[:, h * (DN + DV) : h * (DN + DV) + DN]
        first = h * (DN + DR)
        query_grad[:, first : first + DN] = multiply(low, key).astype(BF)
        for b in range(trees):
            rows = slice(b * tok, (b + 1) * tok)
            former, latter = rope_grad[b, h, :, :half], rope_grad[b, h, :, half:DR]
            query_grad[rows, first + DN : first + DN + half] = (
                former * cosine[rows, :] + latter * sine[rows, :]
            ).astype(BF)
            query_grad[rows, first + DN + half : first + DN + DR] = (
                latter * cosine[rows, :] - former * sine[rows, :]
            ).astype(BF)
        expand_grad[:, h * (DN + DV) : h * (DN + DV) + DN] = tn(
            low, nope[:, h * DN : (h + 1) * DN]
        ).astype(BF)
    for i in range(parts):
        part(i).wait()
        if i + 1 < parts:
            part(i + 1).start()
        hidden_grad[:, i * size : (i + 1) * size] = nt(query_grad[...], w_part[i % 2])


def attend_back(grad, w_output, expand, cat, keys, lse, allowed, mixed, nope, cosine, sine, w_query, scale):
    trees, _, tok, width = cat.shape
    length, rows = keys.shape[1], grad.shape[0]
    vmem = pl.BlockSpec(memory_space=pltpu.VMEM)
    return pl.pallas_call(
        functools.partial(attend_back_kernel, scale),
        out_shape=[
            jax.ShapeDtypeStruct(keys.shape, BF),
            jax.ShapeDtypeStruct((rows, H * (DN + DR)), BF),
            jax.ShapeDtypeStruct((rows, D), F32),
            jax.ShapeDtypeStruct(expand.shape, BF),
        ],
        in_specs=[vmem] * 11 + [pl.BlockSpec(memory_space=pl.ANY)],
        out_specs=[vmem] * 4,
        scratch_shapes=[
            pltpu.VMEM((rows, H * DV), BF),
            pltpu.VMEM((trees, H, tok, LAT), BF),
            pltpu.VMEM((H * tok, length), BF),
            pltpu.VMEM((H * tok, length), BF),
            pltpu.VMEM((trees, H, tok, LAT), BF),
            pltpu.VMEM((trees, H, tok, width - LAT), F32),
            pltpu.VMEM((2, 256, H * (DN + DR)), BF),
            pltpu.SemaphoreType.DMA((2,)),
        ],
        compiler_params=pltpu.CompilerParams(vmem_limit_bytes=60 << 20),
        cost_estimate=pl.CostEstimate(flops=0, bytes_accessed=1 << 20, transcendentals=0),
        name="attend_back",
    )(grad, w_output, expand, cat, keys, lse, allowed, mixed, nope, cosine, sine, w_query)


def body(
    tokens,
    out_grad,
    segments,
    path_mask,
    expert_ids,
    norm_attn,
    attn_q,
    attn_kva,
    norm_latent,
    attn_kvb,
    attn_out,
    norm_ffn,
    router,
    expert_gate,
    expert_up,
    expert_down,
    shared_gate,
    shared_up,
    shared_down,
):
    trees, tok_loc = tokens.shape[:2]
    row_total = trees * tok_loc
    nc, nf = lax.axis_size("ctx"), lax.axis_size("fsdp")
    mine, group = lax.axis_index("ctx"), lax.axis_index("fsdp")
    experts = nc
    ring = Ring(nf, nc)
    tree_len = tok_loc * nc
    group_rows = trees * tree_len
    first_row = mine * tok_loc
    capacity = min(tok_loc, tok_loc * TOP * 4 // (3 * experts))
    slot_total = nc * trees * capacity
    score_scale = 1.0 / math.sqrt(DN + DR)
    frequency = rope_base ** (-(jnp.arange(DR // 2, dtype=F32) * 2.0 / DR))
    labels = jnp.arange(experts, dtype=jnp.int32)
    both = ("fsdp", "ctx")
    part = D // nf

    def roll_in(x):
        return lax.dynamic_slice_in_dim(jnp.concatenate([x, x], axis=-1), group * part, D, x.ndim - 1)

    def roll_out(x):
        return lax.dynamic_slice_in_dim(
            jnp.concatenate([x, x], axis=-1), (nf - group) % nf * part, D, x.ndim - 1
        )

    def fetch(w):
        pieces = [w]
        for k in range(1, nf):
            pieces.append(lax.ppermute(w, "fsdp", [(i, (i - k) % nf) for i in range(nf)]))
        return pieces

    fs = shared_gate.shape[1]
    fp = -(-fs // 128) * 128
    shared_w = jnp.concatenate(
        [jnp.pad(w, ((0, 0), (0, fp - fs))) for w in (shared_gate, shared_up, shared_down)], axis=1
    )
    def one_mask(segment_ids, path_table):
        return tree_mask(segment_ids, path_table, first_row, tok_loc)

    allowed, positions = jax.vmap(one_mask)(segments, path_mask)
    rotation = positions.astype(F32)[:, :, None] * frequency[None, None, :]
    cosine, sine = jnp.cos(rotation), jnp.sin(rotation)
    inputs = tokens.astype(F32).reshape(row_total, D)
    inverse_in = lax.rsqrt(jnp.mean(inputs * inputs, axis=-1, keepdims=True) + epsilon)
    normed_in = inputs * inverse_in

    r_one, r_lat, r_router = norm_attn.shape[0], norm_latent.shape[0], router.size
    small = jnp.concatenate(
        [
            jnp.tile(norm_attn, 128 // r_one),
            jnp.tile(norm_latent, 128 // r_lat),
            norm_attn,
            norm_ffn,
            norm_latent,
            router.reshape(-1),
            expert_ids.astype(BF).reshape(-1),
        ]
    )
    small = jnp.pad(small, (0, 2 * PACK - small.shape[0])).reshape(2 * PACK // 128, 128)
    if nf == 2:
        small_all, w_latent, w_query, w_expand, w_output, other_gate, other_up, keys, hidden_in, latent_all = front(
            ring,
            0,
            [small, attn_kva, attn_q, attn_kvb, attn_out],
            [expert_gate, expert_up],
            normed_in,
            cosine.reshape(row_total, -1),
            sine.reshape(row_total, -1),
            r_lat,
            trees,
            tok_loc,
        )
        e_gate, e_up = [expert_gate, other_gate], [expert_up, other_up]
        later_shared, later_down, later_grads, small_all = lax.optimization_barrier(
            (shared_w, expert_down, out_grad, small_all)
        )
    else:
        w_latent, w_query, w_expand, small_all, w_output = (
            lax.all_gather(w, both, axis=0) for w in (attn_kva, attn_q, attn_kvb, small, attn_out)
        )
        e_gate, e_up = fetch(expert_gate), fetch(expert_up)
        later_shared, later_down, later_grads = shared_w, expert_down, out_grad
    s_all, e_down = fetch(later_shared), fetch(later_down)
    w_output = w_output.reshape(H * DV, D)
    w_latent, w_query = w_latent.reshape(D, -1), w_query.reshape(D, -1)
    w_expand = w_expand.reshape(LAT, -1)
    small_all = small_all.reshape(nf * nc, 2 * PACK)[:, 256:]
    cuts = [0, r_one, 2 * r_one, 2 * r_one + r_lat, 2 * r_one + r_lat + r_router]
    gain_attn = small_all[:, cuts[0] : cuts[1]].reshape(-1).astype(F32)
    gain_ffn = small_all[:, cuts[1] : cuts[2]].reshape(-1).astype(F32)
    gain_latent = small_all[:, cuts[2] : cuts[3]].reshape(-1).astype(F32)
    w_router = small_all[:, cuts[3] : cuts[4]].reshape(D, experts)
    ids_all = lax.dynamic_slice_in_dim(small_all.reshape(nf, nc, -1), group, 1, 0)[0]
    ids_all = ids_all[:, cuts[4] : cuts[4] + expert_ids.size].reshape(nc, trees, tok_loc, TOP)
    ids_all = ids_all.transpose(1, 0, 2, 3).reshape(group_rows, TOP)

    upstream_low = out_grad.reshape(row_total, D)
    upstream = upstream_low.astype(F32)
    tree_grads = lax.all_gather(roll_in(later_grads), "ctx", axis=1, tiled=True).reshape(group_rows, D)

    if nf != 2:
        hidden_in = (normed_in * gain_attn).astype(BF)
        latent_all = multiply(hidden_in, w_latent)
    latent_normed, latent_inverse, latent_gained = normalize(latent_all[:, :LAT], gain_latent)
    if nf != 2:
        key_latent = latent_gained.astype(BF).reshape(trees, tok_loc, LAT)
        key_rope = rotate(latent_all[:, LAT:].reshape(trees, tok_loc, DR), cosine, sine).astype(BF)
        key_pad = jnp.zeros((trees, tok_loc, 128 - DR), BF)
        (keys,) = ring_gather(
            ring, 1, [jnp.concatenate([key_latent, key_rope, key_pad], axis=-1)], [False]
        )
    keys = keys.reshape(trees, tree_len, LAT + 128)
    allowed = allowed.astype(F32)
    query_cat, log_total, mixed, heads, residual, query_nope = attend(
        hidden_in,
        cosine.reshape(row_total, -1),
        sine.reshape(row_total, -1),
        keys,
        allowed,
        w_expand,
        tokens.reshape(row_total, D),
        w_query,
        w_output,
        tok_loc,
        score_scale,
    )
    normed_mid, inverse_mid, gained_mid = normalize(residual, gain_ffn)
    hidden_mid = gained_mid.astype(BF)
    expert_probs = jax.nn.softmax(multiply(hidden_mid, w_router), axis=-1)

    probs_parts = jnp.concatenate(three_parts(expert_probs), axis=-1)
    probs_parts = jnp.pad(probs_parts, ((0, 0), (0, 128 - 3 * experts)))
    tree_rows, tree_probs = ring_gather(
        ring,
        2,
        [roll_in(hidden_mid).reshape(trees, tok_loc, D), probs_parts.reshape(trees, tok_loc, 128)],
        [False, False],
    )
    tree_rows = tree_rows.reshape(group_rows, D)
    tree_probs = tree_probs.reshape(group_rows, 128)

    member = jnp.any(ids_all == mine.astype(BF), axis=1)
    blocks = trees * nc
    bundle = 4 if blocks % 4 == 0 else 1
    bundles = blocks // bundle
    grid = member.astype(BF).reshape(blocks, tok_loc)
    upper = (jnp.arange(tok_loc)[:, None] <= jnp.arange(tok_loc)[None, :]).astype(BF)
    slot = multiply(grid, upper).astype(jnp.int32) - 1
    slot = slot + (jnp.arange(blocks, dtype=jnp.int32) % bundle * capacity)[:, None]
    slot = jnp.where(grid > 0, slot, -1).reshape(bundles, bundle * tok_loc)
    back, out_part, delta_out, e_rows, e_grads, e_hidden, e_gg, e_ug, s_act = run_experts(
        nf,
        experts,
        capacity,
        tok_loc,
        tree_rows,
        tree_grads,
        tree_probs,
        slot,
        list(zip(e_gate, e_up, e_down, s_all)),
    )

    def weight_grads(k, e_gg, e_ug, e_hidden, s_act):
        cut = slice(k * part, (k + 1) * part)
        return (
            transposed_multiply(tree_rows[:, cut], s_act[:, : 2 * fp]),
            transposed_multiply(tree_grads[:, cut], s_act[:, 2 * fp :]),
            transposed_multiply(e_rows[:, cut], e_gg),
            transposed_multiply(e_rows[:, cut], e_ug),
            transposed_multiply(e_grads[:, cut], e_hidden),
        )

    job_arrays = [e_rows, e_grads, tree_rows, tree_grads], [e_gg, e_ug, e_hidden, s_act]
    job_pairs = [
        (2, 3, 0, 2 * fp),
        (3, 3, 2 * fp, fp),
        (0, 0, 0, e_gg.shape[1]),
        (0, 1, 0, e_gg.shape[1]),
        (1, 2, 0, e_gg.shape[1]),
    ]

    def job_cuts(k):
        return [(k * part, part)] * 4

    def by_owner(x):
        return x.reshape(trees, nc, tok_loc, x.shape[-1])

    if nf == 2:
        back_sum, delta_sum, *sent = ring_reduce(
            ring,
            3,
            [by_owner(back), by_owner(delta_out)],
            [False] * 2,
            *job_arrays,
            job_cuts(1),
            job_pairs,
            (0, 1),
        )
        there, sent = sent[5:], sent[2:5]
    else:
        back_sum, delta_sum = ring_reduce(
            ring, 3, [by_owner(back), by_owner(delta_out)], [False] * 2
        )
    back_sum, out_part = lax.optimization_barrier((back_sum, out_part))
    back_sum = roll_out(back_sum.reshape(row_total, D))
    prob_delta = jnp.sum(
        delta_sum.reshape(row_total, 128)[:, : 3 * experts].reshape(row_total, 3, experts), axis=1
    )
    out_sum = lax.psum_scatter(
        out_part.reshape(trees, tree_len, D), "ctx", scatter_dimension=1, tiled=True
    )

    came = []
    for k in range(1, nf):
        perm = [(i, (i + k) % nf) for i in range(nf)]
        grads = sent if nf == 2 else weight_grads(k, e_gg, e_ug, e_hidden, s_act)
        came.append([lax.ppermute(g.astype(BF), "fsdp", perm) for g in grads])
    if nf == 2:
        came[0] = list(there) + came[0]

    logit_grad = (
        expert_probs * (prob_delta - jnp.sum(expert_probs * prob_delta, axis=-1, keepdims=True))
    ).astype(BF)
    grad_router = transposed_multiply(hidden_mid, logit_grad)
    mid_grad = back_sum + multiply_transposed(logit_grad, w_router)
    mid_input, grad_gain_ffn = normalize_back(mid_grad, normed_mid, inverse_mid, gain_ffn)
    residual_grad = upstream + mid_input
    residual_low = residual_grad.astype(BF)
    keys_grad, query_grad, hidden_grad, grad_expand = attend_back(
        residual_low,
        w_output,
        w_expand,
        query_cat,
        keys,
        log_total,
        allowed,
        mixed,
        query_nope,
        cosine.reshape(row_total, -1),
        sine.reshape(row_total, -1),
        w_query,
        score_scale,
    )
    own_keys_grad, grad_query, grad_output = ring_reduce(
        ring,
        4,
        [keys_grad.reshape(trees, nc, tok_loc, LAT + 128)],
        [False],
        [hidden_in, heads],
        [query_grad, residual_low],
        [(0, D), (0, H * DV)],
        [(0, 0, 0, query_grad.shape[1]), (1, 1, 0, D)],
    )
    latent_in_grad, grad_gain_latent = normalize_back(
        own_keys_grad[..., :LAT].reshape(row_total, LAT), latent_normed, latent_inverse, gain_latent
    )
    rope_back = rotate(own_keys_grad[..., LAT : LAT + DR], cosine, -sine).reshape(row_total, DR)
    latent_grad = jnp.concatenate([latent_in_grad, rope_back], axis=-1).astype(BF)
    grad_latent = transposed_multiply(hidden_in, latent_grad)
    hidden_grad = hidden_grad + multiply_transposed(latent_grad, w_latent)
    input_part, grad_gain_attn = normalize_back(hidden_grad, normed_in, inverse_in, gain_attn)
    input_grad = (input_part + residual_grad).reshape(trees, tok_loc, D)

    grad_small = jnp.concatenate(
        [
            grad_gain_attn.reshape(nf * nc, r_one),
            grad_gain_ffn.reshape(nf * nc, r_one),
            grad_gain_latent.reshape(nf * nc, r_lat),
            grad_router.reshape(nf * nc, r_router),
        ],
        axis=1,
    ).astype(BF)
    grad_small = jnp.pad(grad_small, ((0, 0), (0, PACK - grad_small.shape[1])))
    parts = [
        grad_query.reshape(nf, nc, -1, w_query.shape[1]),
        grad_expand.reshape(nf, nc, -1, w_expand.shape[1]),
        grad_latent.astype(BF).reshape(nf, nc, -1, w_latent.shape[1]),
        grad_small.reshape(nf, nc, 16, PACK // 16),
        grad_output.reshape(nf, nc, -1, D),
    ]
    if nf == 2:
        t_query, t_expand, t_latent, t_small, out_total, *ffn_sums = ring_reduce(
            ring, 5, parts, [True] * 5, *job_arrays, job_cuts(0), job_pairs
        )
        came, ffn_sums = lax.optimization_barrier((came, ffn_sums))
    else:
        t_query, t_expand, t_latent, t_small, out_total = (
            lax.psum_scatter(
                x.reshape((nf * nc,) + x.shape[2:]), both, scatter_dimension=0, tiled=True
            )[0].astype(F32)
            for x in parts
        )
        ffn_sums = weight_grads(0, e_gg, e_ug, e_hidden, s_act)
    t_small, out_sum = lax.optimization_barrier((t_small, out_sum))
    out_sum = roll_out(out_sum.reshape(row_total, D).astype(F32))
    output = (residual + out_sum).astype(BF).reshape(trees, tok_loc, D)
    t_small = t_small.reshape(PACK)
    for one in came:
        ffn_sums = [a.astype(F32) + b.astype(F32) for a, b in zip(ffn_sums, one)]
    e_sums = ffn_sums[2:]
    s_sums = [ffn_sums[0][:, :fs], ffn_sums[0][:, fp : fp + fs], ffn_sums[1][:, :fs]]
    return (
        output,
        input_grad,
        t_small[cuts[0] : cuts[1]],
        t_query,
        t_latent,
        t_small[cuts[2] : cuts[3]],
        t_expand,
        out_total,
        t_small[cuts[1] : cuts[2]],
        t_small[cuts[3] : cuts[4]].reshape(-1, experts),
        *e_sums,
        *s_sums,
    )


def solution(mesh):
    placed = (
        P("fsdp", "ctx", None),
        P("fsdp", "ctx", None),
        P("fsdp", None),
        P("fsdp", None, None),
        P("fsdp", "ctx", None),
        P(("fsdp", "ctx")),
        P(("fsdp", "ctx"), None),
        P(("fsdp", "ctx"), None),
        P(("fsdp", "ctx")),
        P(("fsdp", "ctx"), None),
        P(("fsdp", "ctx"), None),
        P(("fsdp", "ctx")),
        P(("fsdp", "ctx"), None),
        P("fsdp", "ctx"),
        P("fsdp", "ctx"),
        P("fsdp", "ctx"),
        P("fsdp", "ctx"),
        P("fsdp", "ctx"),
        P("fsdp", "ctx"),
    )
    return jax.shard_map(
        body,
        mesh=mesh,
        in_specs=placed,
        out_specs=(
            P("fsdp", "ctx", None),
            P("fsdp", "ctx", None),
            P(("fsdp", "ctx")),
            P(("fsdp", "ctx"), None),
            P(("fsdp", "ctx"), None),
            P(("fsdp", "ctx")),
            P(("fsdp", "ctx"), None),
            P(("fsdp", "ctx"), None),
            P(("fsdp", "ctx")),
            P(("fsdp", "ctx"), None),
            P("fsdp", "ctx"),
            P("fsdp", "ctx"),
            P("fsdp", "ctx"),
            P("fsdp", "ctx"),
            P("fsdp", "ctx"),
            P("fsdp", "ctx"),
        ),
        check_vma=False,
    )
```

```python
import functools
import math

import jax
import jax.numpy as jnp
from jax import lax
from jax.experimental import pallas as pl
from jax.experimental.pallas import tpu as pltpu
from jax.sharding import PartitionSpec as P

D = 2048
H = 16
DN = 128
DR = 64
DV = 128
LAT = 512
TOP = 6
SEGS = 13
PACK = 2048

MESH = pl.DeviceIdType.MESH
BF = jnp.bfloat16
F32 = jnp.float32

epsilon = 1e-06
rope_base = 10000.0


def multiply(left, right):
    return jnp.dot(left, right, preferred_element_type=F32)


def multiply_transposed(left, right):
    return lax.dot_general(left, right, (((1,), (1,)), ((), ())), preferred_element_type=F32)


def transposed_multiply(left, right):
    return lax.dot_general(left, right, (((0,), (0,)), ((), ())), preferred_element_type=F32)


def normalize(tensor_in, gain_vec):
    inverse = lax.rsqrt(jnp.mean(tensor_in * tensor_in, axis=-1, keepdims=True) + epsilon)
    normed = tensor_in * inverse
    return (normed, inverse, normed * gain_vec)


def normalize_back(grad_out, normed, inverse, gain_vec):
    weighted = grad_out * gain_vec
    centre = jnp.mean(weighted * normed, axis=-1, keepdims=True)
    return (inverse * (weighted - normed * centre), jnp.sum(grad_out * normed, axis=0))


def rotate(tensor_in, cosine, sine):
    half_width = tensor_in.shape[-1] // 2
    former = tensor_in[..., :half_width]
    latter = tensor_in[..., half_width:]
    return jnp.concatenate(
        [former * cosine - latter * sine, latter * cosine + former * sine], axis=-1
    )


def tree_mask(segment_ids, path_table, first_row, row_count):
    labels = jnp.arange(SEGS, dtype=jnp.int32)
    own_ids = lax.dynamic_slice_in_dim(segment_ids, first_row, row_count)
    own_hot = (own_ids[:, None] == labels[None, :]).astype(BF)
    all_hot = (segment_ids[:, None] == labels[None, :]).astype(BF)
    ancestry = multiply(own_hot, path_table.astype(BF)).astype(BF)
    related = multiply_transposed(ancestry, all_hot)
    places = jnp.arange(segment_ids.shape[0], dtype=jnp.int32)
    queries = first_row + jnp.arange(row_count, dtype=jnp.int32)
    allowed = (related > 0) & (places[None, :] <= queries[:, None])
    positions = jnp.sum(allowed.astype(jnp.int32), axis=1) - 1
    return (allowed, positions)


def three_parts(value):
    first = lax.reduce_precision(value, 8, 7)
    second = lax.reduce_precision(value - first, 8, 7)
    third = value - first - second
    return (first.astype(BF), second.astype(BF), third.astype(BF))


class Ring:
    def __init__(self, nf, nc):
        self.nf, self.chips = nf, nc // 2
        half = self.chips // 2
        if nf == 2:
            self.place = lambda p: (1 - p // half) * 2 * p + (p // half) * (4 * half - 1 - 2 * p)
            self.where = lambda j: (1 - j % 2) * (j // 2) + (j % 2) * (2 * half - 1 - j // 2)
        else:
            self.place = lambda p: (1 - p // half) * p + (p // half) * (3 * half - 1 - p)
            self.where = self.place

    def here(self):
        f, c = lax.axis_index("fsdp"), lax.axis_index("ctx")
        core = c % 2
        return f, c, core, self.where(c // 2), 1 - 2 * core

    def device(self, position, core):
        return self.place((position + 2 * self.chips) % self.chips) * 2 + core


def greet(ring, f, c, core, p, way, over_fsdp):
    barrier = pltpu.get_barrier_semaphore()
    targets = [(f, ring.device(p - way, core)), (f, c + 1 - 2 * core)]
    if over_fsdp:
        targets += [((f + k) % ring.nf, c) for k in range(1, ring.nf)]
    for target in targets:
        pl.semaphore_signal(barrier, inc=1, device_id=target, device_id_type=MESH)
    pl.semaphore_wait(barrier, len(targets))


def gather_kernel(ring, wide, leads, count, swaps, *refs):
    swap_ins, swap_outs = refs[count : count + swaps], refs[2 * count + swaps : 2 * (count + swaps)]
    ins, outs = refs[:count], refs[count + swaps : 2 * count + swaps]
    own_sem, yss, yrs, rss, rrs, sss, srs, wss, wrs = refs[2 * (count + swaps) :]
    f, c, core, p, way = ring.here()
    n, nf = ring.chips, ring.nf
    greet(ring, f, c, core, p, way, any(wide))
    to_next = (f, ring.device(p + way, core))
    to_twin = (f, c + 1 - 2 * core)
    started, own = [], []

    def remote(src, dst, ss, rs, dev):
        return pltpu.make_async_remote_copy(
            src_ref=src, dst_ref=dst, send_sem=ss, recv_sem=rs, device_id=dev, device_id_type=MESH
        )

    streams, late = [], []
    number = 0
    for i in range(count):
        if wide[i]:
            streams.append((number, i, f, ins[i]))
            number += 1
        else:
            for a in range(leads[i]):
                streams.append((number, i, a, ins[i].at[a]))
                number += 1
    first = len(streams)
    yn = 0
    for i in range(count):
        if wide[i]:
            for k in range(1, nf):
                late.append((number, i, (f - k + nf) % nf, k, yn))
                number += 1
                yn += 1

    def send_ring(s, number, i, lead, owner, src):
        cp = remote(src, outs[i].at[lead, owner], rss.at[s, number], rrs.at[s, number], to_next)
        cp.start()
        started.append(cp)

    def send_twin(s, number, i, lead, owner, src):
        cp = remote(src, outs[i].at[lead, owner], sss.at[s, number], srs.at[s, number], to_twin)
        cp.start()
        started.append(cp)

    for number, i, lead, k, y in late:
        cp = remote(ins[i], outs[i].at[f, c], yss.at[y], yrs.at[y], ((f + k) % nf, c))
        cp.start()
        started.append(cp)
    for number, i, lead, src in streams:
        send_ring(0, number, i, lead, c, src)
    for number, i, lead, src in streams:
        send_twin(0, number, i, lead, c, src)
        cp = pltpu.make_async_copy(src, outs[i].at[lead, c], own_sem.at[number])
        cp.start()
        own.append(cp)
    everything = [(number, i, lead) for number, i, lead, _ in streams]
    everything += [(number, i, lead) for number, i, lead, _, _ in late]
    for number, i, lead, k, y in late:
        here = outs[i].at[lead, c]
        remote(here, here, yss.at[y], yrs.at[y], to_next).wait_recv()
        send_ring(0, number, i, lead, c, here)
        send_twin(0, number, i, lead, c, here)
    swapped = []
    for i in range(swaps):
        cp = remote(swap_ins[i], swap_outs[i], wss.at[i], wrs.at[i], ((f + 1) % nf, c))
        cp.start()
        swapped.append(cp)
    for s in range(1, n):
        owner = ring.device(p - way * s, core)
        for number, i, lead in everything:
            here = outs[i].at[lead, owner]
            remote(here, here, rss.at[s - 1, number], rrs.at[s - 1, number], to_next).wait_recv()
            if s < n - 1:
                send_ring(s, number, i, lead, owner, here)
            send_twin(s, number, i, lead, owner, here)
    for s in range(n):
        owner = ring.device(p + way * s, 1 - core)
        for number, i, lead in everything:
            here = outs[i].at[lead, owner]
            remote(here, here, sss.at[s, number], srs.at[s, number], to_twin).wait_recv()
    for cp in own:
        cp.wait()
    for cp in started:
        cp.wait_send()
    for cp in swapped:
        cp.wait()


def ring_gather(ring, number, arrays, wide, swaps=()):
    n, nf = ring.chips, ring.nf
    leads = [1 if w else a.shape[0] for a, w in zip(arrays, wide)]
    shapes, streams, late, size = [], 0, 0, 0
    for a, w in zip(arrays, wide):
        if w:
            shapes.append(jax.ShapeDtypeStruct((nf, 2 * n) + a.shape, a.dtype))
            streams += nf
            late += nf - 1
        else:
            shapes.append(jax.ShapeDtypeStruct((a.shape[0], 2 * n) + a.shape[1:], a.dtype))
            streams += a.shape[0]
        size += shapes[-1].size * 2
    dma = pltpu.SemaphoreType.DMA
    shapes += [jax.ShapeDtypeStruct(a.shape, a.dtype) for a in swaps]
    return pl.pallas_call(
        functools.partial(
            gather_kernel, ring, tuple(wide), tuple(leads), len(arrays), len(swaps)
        ),
        out_shape=shapes,
        in_specs=[pl.BlockSpec(memory_space=pl.ANY)] * len(shapes),
        out_specs=[pl.BlockSpec(memory_space=pl.ANY)] * len(shapes),
        scratch_shapes=[
            dma((streams,)),
            dma((max(1, late),)),
            dma((max(1, late),)),
            dma((n - 1, streams)),
            dma((n - 1, streams)),
            dma((n, streams)),
            dma((n, streams)),
            dma((max(1, len(swaps)),)),
            dma((max(1, len(swaps)),)),
        ],
        compiler_params=pltpu.CompilerParams(collective_id=number, has_side_effects=True),
        cost_estimate=pl.CostEstimate(flops=0, bytes_accessed=2 * size, transcendentals=0),
        name="ring_gather_%d" % number,
    )(*arrays, *swaps)


def front_kernel(ring, latent_part, *refs):
    ins, swap_ins, (normed, cosine, sine) = refs[:5], refs[5:7], refs[7:10]
    outs, swap_outs, (keys, hidden, latent) = refs[10:15], refs[15:17], refs[17:20]
    small_held, kva_held, own_keys = refs[20:23]
    own_sem, yss, yrs, rss, rrs, sss, srs, wss, wrs, load_sem = refs[23:]
    f, c, core, p, way = ring.here()
    n, nf = ring.chips, ring.nf
    nc = 2 * n
    greet(ring, f, c, core, p, way, True)
    to_next, to_twin = (f, ring.device(p + way, core)), (f, c + 1 - 2 * core)
    to_other, other = ((f + 1) % nf, c), (f + 1) % nf
    started, own = [], {}

    def remote(src, dst, ss, rs, dev):
        return pltpu.make_async_remote_copy(
            src_ref=src, dst_ref=dst, send_sem=ss, recv_sem=rs, device_id=dev, device_id_type=MESH
        )

    def place(number, owner):
        if number < 10:
            return outs[number // 2].at[(f + number % 2) % nf, owner]
        return keys.at[number - 10, owner]

    def send(s, number, owner, src, ring_too=True):
        dst = place(number, owner)
        if ring_too:
            cp = remote(src, dst, rss.at[s, number], rrs.at[s, number], to_next)
            cp.start()
            started.append(cp)
        cp = remote(src, dst, sss.at[s, number], srs.at[s, number], to_twin)
        cp.start()
        started.append(cp)

    def keep(number, src):
        own[number] = pltpu.make_async_copy(src, place(number, c), own_sem.at[number])
        own[number].start()

    def pass_on(s, number):
        owner = ring.device(p - way * s, core)
        here = place(number, owner)
        remote(here, here, rss.at[s - 1, number], rrs.at[s - 1, number], to_next).wait_recv()
        send(s, number, owner, here, s < n - 1)

    def late(i):
        here = outs[i].at[other, c]
        remote(here, here, yss.at[i], yrs.at[i], to_next).wait_recv()
        send(0, 2 * i + 1, c, here)

    def from_twin(s, number):
        here = place(number, ring.device(p + way * s, 1 - core))
        remote(here, here, sss.at[s, number], srs.at[s, number], to_twin).wait_recv()

    for i in range(5):
        cp = remote(ins[i], outs[i].at[f, c], yss.at[i], yrs.at[i], to_other)
        cp.start()
        started.append(cp)
        send(0, 2 * i, c, ins[i])
        keep(2 * i, ins[i])
    swapped = []

    def swap():
        for i in range(2):
            cp = remote(swap_ins[i], swap_outs[i], wss.at[i], wrs.at[i], to_other)
            cp.start()
            swapped.append(cp)

    bulk = [functools.partial(late, i) for i in (2, 3, 4)] + [swap]
    bulk += [functools.partial(pass_on, s, number) for s in range(1, n) for number in range(4, 10)]

    def some(count):
        for work in bulk[:count]:
            work()
        del bulk[:count]

    late(0)
    late(1)
    for s in range(1, n):
        for number in range(4):
            pass_on(s, number)
        some(3)
    for number in range(4):
        for s in range(n):
            from_twin(s, number)
    for number in (0, 2):
        own[number].wait()
    loads = [
        pltpu.make_async_copy(outs[i], held, load_sem.at[i])
        for i, held in enumerate((small_held, kva_held))
    ]
    for cp in loads:
        cp.start()
    for cp in loads:
        cp.wait()
    lane = lax.broadcasted_iota(jnp.int32, (1, 128), 1)

    def gain(row, first, each):
        total = jnp.zeros((1, 128), F32)
        for k in range(128 // each):
            d = first // each + k
            own_row = small_held[d // nc, d % nc, row : row + 1, :].astype(F32)
            total = jnp.where(lane // each == k, own_row, total)
        return total

    for start in range(0, D, 128):
        cut = slice(start, start + 128)
        hidden[:, cut] = (normed[:, cut] * gain(0, start, D // (nf * nc))).astype(BF)
    latent[:, LAT:] = jnp.zeros((latent.shape[0], 128), F32)
    latent[:, : LAT + DR] = multiply(hidden[...], kva_held[...].reshape(D, LAT + DR))
    trees, tok = own_keys.shape[:2]
    low = latent[:, :LAT]
    inverse = lax.rsqrt(jnp.mean(low * low, axis=-1, keepdims=True) + epsilon)
    for start in range(0, LAT, 128):
        cut = slice(start, start + 128)
        key = (latent[:, cut] * inverse * gain(1, start, latent_part)).astype(BF)
        for a in range(trees):
            own_keys[a, :, cut] = key[a * tok : (a + 1) * tok]
    half = DR // 2
    former, latter = latent[:, LAT : LAT + half], latent[:, LAT + half : LAT + DR]
    turned = (
        (former * cosine[...] - latter * sine[...]).astype(BF),
        (latter * cosine[...] + former * sine[...]).astype(BF),
    )
    own_keys[:, :, LAT:] = jnp.zeros((trees, tok, 128), BF)
    for a in range(trees):
        for k in range(2):
            own_keys[a, :, LAT + k * half : LAT + (k + 1) * half] = turned[k][a * tok : (a + 1) * tok]
    for a in range(trees):
        send(0, 10 + a, c, own_keys.at[a])
        keep(10 + a, own_keys.at[a])
    for s in range(1, n):
        some(3)
        for a in range(trees):
            pass_on(s, 10 + a)
    some(len(bulk))
    for number in range(4, 10 + trees):
        for s in range(n):
            from_twin(s, number)
    for number in own:
        if number not in (0, 2):
            own[number].wait()
    for cp in started:
        cp.wait_send()
    for cp in swapped:
        cp.wait()


def front(ring, number, arrays, swaps, normed, cosine, sine, latent_part, trees, tok):
    n, nf = ring.chips, ring.nf
    rows = normed.shape[0]
    shapes = [jax.ShapeDtypeStruct((nf, 2 * n) + a.shape, a.dtype) for a in arrays]
    size = sum(a.size * 2 for a in shapes)
    shapes += [jax.ShapeDtypeStruct(a.shape, a.dtype) for a in swaps]
    shapes += [
        jax.ShapeDtypeStruct((trees, 2 * n, tok, LAT + 128), BF),
        jax.ShapeDtypeStruct((rows, D), BF),
        jax.ShapeDtypeStruct((rows, LAT + 128), F32),
    ]
    dma = pltpu.SemaphoreType.DMA
    streams = 10 + trees
    vmem, far = pl.BlockSpec(memory_space=pltpu.VMEM), pl.BlockSpec(memory_space=pl.ANY)
    return pl.pallas_call(
        functools.partial(front_kernel, ring, latent_part),
        out_shape=shapes,
        in_specs=[far] * 7 + [vmem] * 3,
        out_specs=[far] * 8 + [vmem] * 2,
        scratch_shapes=[
            pltpu.VMEM(shapes[0].shape, BF),
            pltpu.VMEM(shapes[1].shape, BF),
            pltpu.VMEM((trees, tok, LAT + 128), BF),
            dma((streams,)),
            dma((5,)),
            dma((5,)),
            dma((n - 1, streams)),
            dma((n - 1, streams)),
            dma((n, streams)),
            dma((n, streams)),
            dma((2,)),
            dma((2,)),
            dma((2,)),
        ],
        compiler_params=pltpu.CompilerParams(
            collective_id=number, has_side_effects=True, vmem_limit_bytes=60 << 20
        ),
        cost_estimate=pl.CostEstimate(flops=0, bytes_accessed=2 * size, transcendentals=0),
        name="front",
    )(*arrays, *swaps, normed, cosine, sine)


def add_rows(shape, work):
    rows = shape[0]
    step = 16 if rows % 16 == 0 else rows

    def one(r, carry):
        work(pl.ds(pl.multiple_of(r * step, step), step))
        return carry

    lax.fori_loop(0, rows // step, one, 0)


class Products:
    tile = 256

    def __init__(self, cuts, pairs, lefts, rights, outs, held, *rest):
        self.cuts, self.pairs, self.lefts, self.rights, self.outs = cuts, pairs, lefts, rights, outs
        self.held = held
        self.tiles, self.stage, self.load_sem, self.tile_sem, self.store_sem = rest
        self.units = [
            (j, m) for j in range(len(pairs)) for m in range(0, cuts[pairs[j][0]][1], self.tile)
        ]
        self.done, self.loaded, self.stores = 0, set(), [None, None]
        self.ship, self.shipped = {}, []

    def deliver(self):
        for j in sorted(self.ship):
            last = max(i for i, unit in enumerate(self.units) if unit[0] == j)
            if self.done > last + 2 or (self.done == len(self.units) and self.stores == []):
                cp = self.ship.pop(j)()
                cp.start()
                self.shipped.append(cp)

    def fetch(self, number):
        j, m = self.units[number]
        left = self.pairs[j][0]
        source, slot = self.lefts[left], number % 2
        return pltpu.make_async_copy(
            source.at[:, pl.ds(self.cuts[left][0] + m, self.tile)],
            self.tiles.at[slot, pl.ds(0, source.shape[0]), :],
            self.tile_sem.at[slot],
        )

    def start(self):
        self.fetch(0).start()
        self.loads = []
        for i, source in enumerate(self.rights):
            cp = pltpu.make_async_copy(source, self.held[i], self.load_sem.at[i])
            cp.start()
            self.loads.append(cp)

    def run(self, upto):
        while self.done < min(upto, len(self.units)):
            j, m = self.units[self.done]
            left, right, first, width = self.pairs[j]
            if right not in self.loaded:
                self.loads[right].wait()
                self.loaded.add(right)
            self.fetch(self.done).wait()
            if self.done + 1 < len(self.units):
                self.fetch(self.done + 1).start()
            slot = self.done % 2
            value = lax.dot_general(
                self.tiles[slot, pl.ds(0, self.lefts[left].shape[0]), :],
                self.held[right][:, pl.ds(first, width)],
                (((0,), (0,)), ((), ())),
                preferred_element_type=F32,
            )
            if self.stores[slot] is not None:
                self.stores[slot].wait()
            self.stage[slot, :, pl.ds(0, width)] = value.astype(BF)
            cp = pltpu.make_async_copy(
                self.stage.at[slot, :, pl.ds(0, width)],
                self.outs[j].at[pl.ds(m, self.tile), :],
                self.store_sem.at[slot],
            )
            cp.start()
            self.stores[slot] = cp
            self.done += 1
            self.deliver()

    def finish(self):
        self.run(len(self.units))
        for cp in self.stores:
            if cp is not None:
                cp.wait()
        self.stores = []
        self.deliver()
        for cp in self.shipped:
            cp.wait()


def reduce_kernel(ring, wide, leads, count, cuts, pairs, ships, *refs):
    njobs = len(pairs)
    nleft = len(cuts)
    nright = 1 + max([p[1] for p in pairs], default=-1)
    nops = nleft + nright
    ins, sources, refs = refs[:count], refs[count : count + nops], refs[count + nops :]
    outs, job_outs, refs = refs[:count], refs[count : count + njobs], refs[count + njobs :]
    ship_outs, refs = refs[: len(ships)], refs[len(ships) :]
    own, twin, got = (refs[k * count : (1 + k) * count] for k in range(3))
    refs = refs[3 * count :]
    wides = sum(wide)
    finals, ygots = refs[:wides], refs[wides : 2 * wides]
    own_sem, tss, trs, rss, rrs, yss, yrs = refs[2 * wides : 2 * wides + 7]
    refs = refs[2 * wides + 7 :]
    jobs = None
    if njobs:
        jobs = Products(
            cuts, pairs, sources[:nleft], sources[nleft:], job_outs, refs[:nright], *refs[nright : nright + 5]
        )
    f, c, core, p, way = ring.here()
    n, nf = ring.chips, ring.nf
    greet(ring, f, c, core, p, way, any(wide) or len(ships) > 0)
    to_next = (f, ring.device(p + way, core))
    to_twin = (f, c + 1 - 2 * core)

    def remote(src, dst, ss, rs, dev):
        return pltpu.make_async_remote_copy(
            src_ref=src, dst_ref=dst, send_sem=ss, recv_sem=rs, device_id=dev, device_id_type=MESH
        )

    streams = []
    for k in range(max(leads)):
        for i in range(count):
            if k < leads[i]:
                lead = (f + 1 + k) % nf if wide[i] else k
                streams.append((len(streams), i, k, lead))
    started, loads = [], {}
    for s in range(n):
        theirs = ring.device(p + way * (1 + s), 1 - core)
        mine = ring.device(p - way * (1 + s), core)
        for number, i, k, lead in streams:
            cp = remote(
                ins[i].at[lead, theirs], twin[i].at[s, k], tss.at[s, number], trs.at[s, number], to_twin
            )
            cp.start()
            started.append(cp)
            cp = pltpu.make_async_copy(
                ins[i].at[lead, mine], own[i].at[s, k], own_sem.at[s, number]
            )
            cp.start()
            loads[s, number] = cp

    if jobs:
        for w, j in enumerate(ships):
            jobs.ship[j] = functools.partial(
                remote, job_outs[j], ship_outs[w], refs[-2].at[w], refs[-1].at[w], ((f + 1) % nf, c)
            )
        jobs.start()

    def wait_parts(s, number, i, k):
        loads[s, number].wait()
        here = twin[i].at[s, k]
        remote(here, here, tss.at[s, number], trs.at[s, number], to_twin).wait_recv()

    def pass_on(s, number, i, k, src):
        cp = remote(src, got[i].at[s, k], rss.at[s, number], rrs.at[s, number], to_next)
        cp.start()
        started.append(cp)

    turn, turns = 0, (n - 1) * len(streams)
    for s in range(n):
        for number, i, k, lead in streams:
            if jobs and s > 0:
                jobs.run(-(-len(jobs.units) * turn // turns))
                turn += 1
            wait_parts(s, number, i, k)
            mine, other = own[i].at[s, k], twin[i].at[s, k]
            if s == 0:

                def start(rows, mine=mine, other=other):
                    mine[rows, :] = (mine[rows, :].astype(F32) + other[rows, :].astype(F32)).astype(BF)

                add_rows(mine.shape, start)
                pass_on(0, number, i, k, mine)
                continue
            came = got[i].at[s - 1, k]
            remote(came, came, rss.at[s - 1, number], rrs.at[s - 1, number], to_next).wait_recv()
            if s < n - 1:

                def middle(rows, mine=mine, other=other, came=came):
                    total = mine[rows, :].astype(F32) + other[rows, :].astype(F32)
                    came[rows, :] = (came[rows, :].astype(F32) + total).astype(BF)

                add_rows(mine.shape, middle)
                pass_on(s, number, i, k, came)
                continue
            if not wide[i]:
                target = outs[i].at[k]
            elif k == nf - 1:
                target = outs[i]
            else:
                target = finals[sum(wide[:i])].at[k]

            def last(rows, mine=mine, other=other, came=came, target=target):
                total = mine[rows, :].astype(F32) + other[rows, :].astype(F32)
                target[rows, :] = (came[rows, :].astype(F32) + total).astype(target.dtype)

            add_rows(mine.shape, last)
            if wide[i] and k < nf - 1:
                w = sum(wide[:i])
                cp = remote(target, ygots[w].at[k], yss.at[w, k], yrs.at[w, k], ((f + 1 + k) % nf, c))
                cp.start()
                started.append(cp)
    for i in range(count):
        if wide[i]:
            w = sum(wide[:i])
            for k in range(nf - 1):
                here = ygots[w].at[k]
                remote(here, here, yss.at[w, k], yrs.at[w, k], to_next).wait_recv()

                def finish(rows, here=here, target=outs[i]):
                    target[rows, :] = target[rows, :] + here[rows, :].astype(F32)

                add_rows(here.shape, finish)
    if jobs:
        jobs.finish()
    for cp in started:
        cp.wait_send()


def ring_reduce(ring, number, arrays, wide, lefts=(), rights=(), cuts=(), pairs=(), ships=()):
    n, nf = ring.chips, ring.nf
    leads = [a.shape[0] for a in arrays]
    more = [jax.ShapeDtypeStruct((cuts[l][1], width), BF) for l, _, _, width in pairs]
    streams = sum(leads)
    block = [a.shape[2:] for a in arrays]
    shapes = [
        jax.ShapeDtypeStruct(b if w else (l,) + b, F32) for b, w, l in zip(block, wide, leads)
    ]
    dma = pltpu.SemaphoreType.DMA
    scratch = [pltpu.VMEM((n, l) + b, BF) for b, l in zip(block, leads)] * 2
    scratch += [pltpu.VMEM((n - 1, l) + b, BF) for b, l in zip(block, leads)]
    scratch += [pltpu.VMEM((nf - 1,) + b, BF) for b, w in zip(block, wide) if w] * 2
    more += [more[j] for j in ships]
    wides = max(1, sum(wide))
    extra = []
    if pairs:
        extra = [pltpu.VMEM(a.shape, BF) for a in rights]
        extra += [
            pltpu.VMEM((2, max(a.shape[0] for a in lefts), Products.tile), BF),
            pltpu.VMEM((2, Products.tile, max(p[3] for p in pairs)), BF),
            dma((len(rights),)),
            dma((2,)),
            dma((2,)),
        ]
    if ships:
        extra += [dma((len(ships),)), dma((len(ships),))]
    return pl.pallas_call(
        functools.partial(
            reduce_kernel, ring, tuple(wide), tuple(leads), len(arrays), tuple(cuts), tuple(pairs), tuple(ships)
        ),
        out_shape=shapes + more,
        in_specs=[pl.BlockSpec(memory_space=pl.ANY)] * (len(arrays) + len(lefts) + len(rights)),
        out_specs=[pl.BlockSpec(memory_space=pltpu.VMEM)] * len(arrays)
        + [pl.BlockSpec(memory_space=pl.ANY)] * len(more),
        scratch_shapes=scratch
        + [
            dma((n, streams)),
            dma((n, streams)),
            dma((n, streams)),
            dma((n - 1, streams)),
            dma((n - 1, streams)),
            dma((wides, max(1, nf - 1))),
            dma((wides, max(1, nf - 1))),
        ]
        + extra,
        compiler_params=pltpu.CompilerParams(
            collective_id=number, has_side_effects=True, vmem_limit_bytes=60 << 20
        ),
        cost_estimate=pl.CostEstimate(flops=0, bytes_accessed=1 << 20, transcendentals=0),
        name="ring_reduce_%d" % number,
    )(*arrays, *lefts, *rights)


def expert_kernel(nf, experts, fp, bundle_slots, *refs):
    x_ref, g_ref, probs_ref, slot_ref, column_ref = refs[:5]
    weights, refs = refs[5 : 5 + 4 * nf], refs[5 + 4 * nf :]
    back_ref, out_ref, delta_ref, rows_ref, grads_ref, hid_ref, gg_ref, ug_ref, act_ref = refs[:9]
    w_gate, w_up, w_down, w_shared, pre_gate, pre_up, pre_in, pre_s, raw, sems = refs[9:]
    mine = lax.axis_index("ctx")
    held = (w_gate, w_up, w_down, w_shared)
    part = w_gate.shape[0] // nf
    wide = w_gate.shape[0]
    copies = [
        [
            pltpu.make_async_copy(
                weights[4 * k + i], held[i].at[pl.ds(k * part, part)], sems.at[i, k]
            )
            for k in range(nf)
        ]
        for i in range(4)
    ]
    first = pl.program_id(0) == 0

    def ready(i):
        @pl.when(first)
        def _():
            for cp in copies[i]:
                cp.wait()

    @pl.when(first)
    def _():
        for i in (3, 0, 1, 2):
            for cp in copies[i]:
                cp.start()

    def nt(left, right):
        return lax.dot_general(left, right, (((1,), (1,)), ((), ())), preferred_element_type=F32)

    bundles, _, rows = slot_ref.shape
    lane = lax.broadcasted_iota(jnp.int32, (rows, 128), 1)
    own_lane = (lane % experts == mine) & (lane < 3 * experts)
    puts, row_gates = [], []
    for b in range(bundles):
        cut, spot = pl.ds(b * rows, rows), pl.ds(b * bundle_slots, bundle_slots)
        takes = (
            slot_ref[b] == lax.broadcasted_iota(jnp.int32, (bundle_slots, rows), 0)
        ).astype(F32).astype(BF)
        puts.append(
            (
                column_ref[cut, :] == lax.broadcasted_iota(jnp.int32, (rows, bundle_slots), 1)
            ).astype(F32).astype(BF)
        )
        own = jnp.where(own_lane, probs_ref[cut, :].astype(F32), 0.0)
        row_gates.append(jnp.sum(own, axis=1, keepdims=True))
        gate = jnp.sum(multiply(takes, own.astype(BF)), axis=1, keepdims=True)
        for start in range(0, wide, 512):
            piece = pl.ds(start, 512)
            rows_ref[spot, piece] = multiply(takes, x_ref[cut, piece]).astype(BF)
            taken = multiply(takes, g_ref[cut, piece])
            raw[spot, piece] = taken.astype(BF)
            grads_ref[spot, piece] = (gate * taken).astype(BF)

    ready(3)
    pre_s[:, : 2 * fp] = multiply(x_ref[...], w_shared[:, : 2 * fp])
    pre_s[:, 2 * fp :] = multiply(g_ref[...], w_shared[:, 2 * fp :])

    def activate(gate_pre, up_pre, inner):
        sig = jax.nn.sigmoid(gate_pre)
        activated = gate_pre * sig
        hidden = activated * up_pre
        gate_grad = inner * up_pre * sig * (1.0 + gate_pre * (1.0 - sig))
        return hidden.astype(BF), gate_grad.astype(BF), (inner * activated).astype(BF)

    step = 32

    def shared_rows(r, carry):
        at = pl.ds(pl.multiple_of(r * step, step), step)
        for start in range(0, fp, 128):
            cuts = [pl.ds(i * fp + start, 128) for i in range(3)]
            hidden, gate_grad, up_grad = activate(*(pre_s[at, c] for c in cuts))
            act_ref[at, cuts[0]] = gate_grad
            act_ref[at, cuts[1]] = up_grad
            act_ref[at, cuts[2]] = hidden
        return carry

    lax.fori_loop(0, pre_s.shape[0] // step, shared_rows, 0)

    ready(0)
    pre_gate[...] = multiply(rows_ref[...], w_gate[...])
    ready(1)
    pre_up[...] = multiply(rows_ref[...], w_up[...])
    ready(2)
    pre_in[...] = multiply(grads_ref[...], w_down[...])

    def expert_rows(r, carry):
        at = pl.ds(pl.multiple_of(r * step, step), step)
        for start in range(0, hid_ref.shape[1], 128):
            c = pl.ds(start, 128)
            hidden, gate_grad, up_grad = activate(pre_gate[at, c], pre_up[at, c], pre_in[at, c])
            hid_ref[at, c] = hidden
            gg_ref[at, c] = gate_grad
            ug_ref[at, c] = up_grad
        return carry

    lax.fori_loop(0, hid_ref.shape[0] // step, expert_rows, 0)

    delta = 0.0
    for start in range(0, wide, 512):
        piece = pl.ds(start, 512)
        e_back = nt(gg_ref[...], w_gate[piece, :]) + nt(ug_ref[...], w_up[piece, :])
        e_back = e_back.astype(BF)
        e_out = nt(hid_ref[...], w_down[piece, :]).astype(BF)
        delta = delta + jnp.sum(
            raw[:, piece].astype(F32) * e_out.astype(F32), axis=1, keepdims=True
        )
        for b in range(bundles):
            cut = pl.ds(b * rows, rows)
            spot = slice(b * bundle_slots, (b + 1) * bundle_slots)
            s_back = nt(act_ref[cut, : 2 * fp], w_shared[piece, : 2 * fp])
            back_ref[cut, piece] = (multiply(puts[b], e_back[spot]) + s_back).astype(BF)
            s_out = nt(act_ref[cut, 2 * fp :], w_shared[piece, 2 * fp :])
            out_ref[cut, piece] = (row_gates[b] * multiply(puts[b], e_out[spot]) + s_out).astype(BF)
    for b in range(bundles):
        own = delta[b * bundle_slots : (b + 1) * bundle_slots]
        high = own.astype(BF).astype(F32)
        middle = (own - high).astype(BF).astype(F32)
        low = own - high - middle
        spread = jnp.where(lane[:bundle_slots] < experts, high, jnp.where(lane[:bundle_slots] < 2 * experts, middle, low))
        spread = jnp.where(own_lane[:bundle_slots], spread, 0.0).astype(BF)
        delta_ref[pl.ds(b * rows, rows), :] = multiply(puts[b], spread).astype(BF)


def run_experts(nf, experts, capacity, tok_loc, tree_rows, tree_grads, tree_probs, slot, weights):
    rows, wide = tree_rows.shape
    bundles, per = slot.shape
    bundle_slots = capacity * (per // tok_loc)
    hidden, fp = weights[0][0].shape[1], weights[0][3].shape[1] // 3
    group = 2 if bundles % 2 == 0 else 1
    steps = bundles // group
    block, slots = rows // steps, group * bundle_slots
    flat = [w for piece in weights for w in piece]
    by_row = lambda width: pl.BlockSpec((block, width), lambda i: (i, 0))
    by_slot = lambda width: pl.BlockSpec((slots, width), lambda i: (i, 0))
    any_spec = pl.BlockSpec(memory_space=pl.ANY)
    shape = lambda n, width: jax.ShapeDtypeStruct((n, width), BF)
    total = steps * slots
    flops = 2 * (6 * total * wide * hidden + 6 * rows * wide * fp + 4 * rows * bundle_slots * wide)
    return pl.pallas_call(
        functools.partial(expert_kernel, nf, experts, fp, bundle_slots),
        grid=(steps,),
        out_shape=[shape(rows, wide), shape(rows, wide), shape(rows, 128)]
        + [shape(total, wide)] * 2
        + [shape(total, hidden)] * 3
        + [shape(rows, 3 * fp)],
        in_specs=[
            by_row(wide),
            by_row(wide),
            by_row(128),
            pl.BlockSpec((group, 1, per), lambda i: (i, 0, 0)),
            pl.BlockSpec((block, 1), lambda i: (i, 0)),
        ]
        + [any_spec] * len(flat),
        out_specs=[by_row(wide), by_row(wide), by_row(128)]
        + [by_slot(wide)] * 2
        + [by_slot(hidden)] * 3
        + [by_row(3 * fp)],
        scratch_shapes=[pltpu.VMEM((wide, hidden), BF)] * 3
        + [pltpu.VMEM((wide, 3 * fp), BF)]
        + [pltpu.VMEM((slots, hidden), F32)] * 3
        + [pltpu.VMEM((block, 3 * fp), F32), pltpu.VMEM((slots, wide), BF)]
        + [pltpu.SemaphoreType.DMA((4, nf))],
        compiler_params=pltpu.CompilerParams(vmem_limit_bytes=61 << 20),
        cost_estimate=pl.CostEstimate(
            flops=flops, bytes_accessed=10 * rows * wide, transcendentals=total * hidden
        ),
        name="experts",
    )(tree_rows, tree_grads, tree_probs, slot[:, None, :], slot.reshape(rows, 1), *flat)


def nt(left, right):
    return lax.dot_general(left, right, (((1,), (1,)), ((), ())), preferred_element_type=F32)


def tn(left, right):
    return lax.dot_general(left, right, (((0,), (0,)), ((), ())), preferred_element_type=F32)


HEADS = 4


def attend_kernel(
    scale, hidden, cosine, sine, keys, allowed, expand, tokens, wq_hbm, wo_hbm,
    cat, lse, mixed, heads, residual, nope, w_out, w_part, query, sem, part_sem,
):
    trees, tok = cat.shape[0], cat.shape[2]
    copy = pltpu.make_async_copy(wo_hbm, w_out, sem)
    pair = 2 * (DN + DR)

    def part(i):
        return pltpu.make_async_copy(
            wq_hbm.at[:, pl.ds(i * pair, pair)], w_part.at[i % 2], part_sem.at[i % 2]
        )

    part(0).start()
    cat[:, :, :, LAT + DR :] = jnp.zeros((trees, H, tok, 128 - DR), BF)
    half = DR // 2
    for i in range(H // 2):
        part(i).wait()
        if i + 1 < H // 2:
            part(i + 1).start()
        else:
            copy.start()
        query[...] = multiply(hidden[...], w_part[i % 2])
        for h in (2 * i, 2 * i + 1):
            first = h % 2 * (DN + DR)
            nope[:, h * DN : (h + 1) * DN] = query[:, first : first + DN].astype(BF)
            former = query[:, first + DN : first + DN + half]
            latter = query[:, first + DN + half : first + DN + DR]
            turned = (
                (former * cosine[...] - latter * sine[...]).astype(BF),
                (latter * cosine[...] + former * sine[...]).astype(BF),
            )
            low = nt(nope[:, h * DN : (h + 1) * DN], expand[:, h * (DN + DV) : h * (DN + DV) + DN])
            low = low.astype(BF)
            for b in range(trees):
                rows = slice(b * tok, (b + 1) * tok)
                cat[b, h, :, :LAT] = low[rows]
                cat[b, h, :, LAT : LAT + half] = turned[0][rows]
                cat[b, h, :, LAT + half : LAT + DR] = turned[1][rows]

    def group(i, carry):
        b, g = i // (H // HEADS), i % (H // HEADS) * HEADS
        query = cat[b, pl.ds(g, HEADS)].reshape(HEADS * tok, -1)
        scores = nt(query, keys[b]) * scale
        scores = scores.reshape(HEADS, tok, -1)
        scores = jnp.where(allowed[b][None] > 0, scores, -1e30)
        highest = jnp.max(scores, axis=-1, keepdims=True)
        raised = jnp.exp(scores - highest)
        total = jnp.sum(raised, axis=-1, keepdims=True)
        lse[b, pl.ds(g, HEADS)] = highest + jnp.log(total)
        probs = (raised * (1.0 / total)).astype(BF).reshape(HEADS * tok, -1)
        mix = multiply(probs, keys[b, :, :LAT]).astype(BF)
        mixed[b, pl.ds(g, HEADS)] = mix.reshape(HEADS, tok, LAT)
        return carry

    lax.fori_loop(0, trees * (H // HEADS), group, 0)
    for h in range(H):
        mix = jnp.concatenate([mixed[b, h] for b in range(trees)], axis=0)
        value = expand[:, h * (DN + DV) + DN : (h + 1) * (DN + DV)]
        heads[:, h * DV : (h + 1) * DV] = multiply(mix, value).astype(BF)
    copy.wait()
    for start in range(0, D, 512):
        cut = slice(start, start + 512)
        residual[:, cut] = tokens[:, cut].astype(F32) + multiply(heads[...], w_out[:, cut])


def attend(hidden, cosine, sine, keys, allowed, expand, tokens, w_query, w_output, tok, scale):
    rows = tokens.shape[0]
    trees = rows // tok
    vmem, far = pl.BlockSpec(memory_space=pltpu.VMEM), pl.BlockSpec(memory_space=pl.ANY)
    length, width = keys.shape[1:]
    return pl.pallas_call(
        functools.partial(attend_kernel, scale),
        out_shape=[
            jax.ShapeDtypeStruct((trees, H, tok, width), BF),
            jax.ShapeDtypeStruct((trees, H, tok, 1), F32),
            jax.ShapeDtypeStruct((trees, H, tok, LAT), BF),
            jax.ShapeDtypeStruct((rows, H * DV), BF),
            jax.ShapeDtypeStruct((rows, D), F32),
            jax.ShapeDtypeStruct((rows, H * DN), BF),
        ],
        in_specs=[vmem] * 7 + [far] * 2,
        out_specs=[vmem] * 6,
        scratch_shapes=[
            pltpu.VMEM(w_output.shape, BF),
            pltpu.VMEM((2, D, 2 * (DN + DR)), BF),
            pltpu.VMEM((rows, 2 * (DN + DR)), F32),
            pltpu.SemaphoreType.DMA,
            pltpu.SemaphoreType.DMA((2,)),
        ],
        compiler_params=pltpu.CompilerParams(vmem_limit_bytes=56 << 20),
        cost_estimate=pl.CostEstimate(
            flops=2 * rows * H * length * 1152, bytes_accessed=30 << 20, transcendentals=rows * H * length
        ),
        name="attend",
    )(hidden, cosine, sine, keys, allowed, expand, tokens, w_query, w_output)


def attend_back_kernel(
    scale, grad, w_out, expand, cat, keys, lse, allowed, mixed, nope, cosine, sine, wq_hbm, keys_grad,
    query_grad, hidden_grad, expand_grad, heads_grad, mix_grad, low_probs, score_grad, cat_grad,
    rope_grad, w_part, part_sem,
):
    trees, tok = cat.shape[0], cat.shape[2]
    size = w_part.shape[1]
    parts = D // size

    def part(i):
        return pltpu.make_async_copy(
            wq_hbm.at[pl.ds(i * size, size), :], w_part.at[i % 2], part_sem.at[i % 2]
        )

    part(0).start()
    for start in range(0, H * DV, 512):
        heads_grad[:, start : start + 512] = nt(grad[...], w_out[start : start + 512, :]).astype(BF)
    for h in range(H):
        value = expand[:, h * (DN + DV) + DN : (h + 1) * (DN + DV)]
        own = heads_grad[:, h * DV : (h + 1) * DV]
        back = nt(own, value).astype(BF)
        for b in range(trees):
            mix_grad[b, h] = back[b * tok : (b + 1) * tok]
        mix = jnp.concatenate([mixed[b, h] for b in range(trees)], axis=0)
        expand_grad[:, h * (DN + DV) + DN : (h + 1) * (DN + DV)] = tn(mix, own).astype(BF)
    for b in range(trees):

        def group(i, carry, b=b):
            g = i * HEADS
            rows = pl.ds(pl.multiple_of(g * tok, HEADS * tok), HEADS * tok)
            query = cat[b, pl.ds(g, HEADS)].reshape(HEADS * tok, -1)
            mix = mix_grad[b, pl.ds(g, HEADS)].reshape(HEADS * tok, -1)
            scores = (nt(query, keys[b]) * scale).reshape(HEADS, tok, -1)
            probs = jnp.where(
                allowed[b][None] > 0, jnp.exp(scores - lse[b, pl.ds(g, HEADS)]), 0.0
            ).reshape(HEADS * tok, -1)
            prob_grad = nt(mix, keys[b, :, :LAT])
            centre = jnp.sum(probs * prob_grad, axis=-1, keepdims=True)
            low_probs[rows, :] = probs.astype(BF)
            own = (probs * (prob_grad - centre)).astype(BF)
            score_grad[rows, :] = own
            back = (multiply(own, keys[b]) * scale).reshape(HEADS, tok, -1)
            cat_grad[b, pl.ds(g, HEADS)] = back[..., :LAT].astype(BF)
            for k in range(HEADS):
                rope_grad[b, g + k] = back[k, :, LAT:]
            return carry

        lax.fori_loop(0, H // HEADS, group, 0)
        query = cat[b].reshape(H * tok, -1)
        mix = mix_grad[b].reshape(H * tok, -1)
        length = keys.shape[1]
        for start in range(0, length, 256):
            cut = slice(start, start + 256)
            total = tn(score_grad[:, cut], query) * scale
            keys_grad[b, cut, :LAT] = (total[:, :LAT] + tn(low_probs[:, cut], mix)).astype(BF)
            keys_grad[b, cut, LAT:] = total[:, LAT:].astype(BF)
    half = DR // 2
    for h in range(H):
        low = jnp.concatenate([cat_grad[b, h] for b in range(trees)], axis=0)
        key = expand[:, h * (DN + DV) : h * (DN + DV) + DN]
        first = h * (DN + DR)
        query_grad[:, first : first + DN] = multiply(low, key).astype(BF)
        for b in range(trees):
            rows = slice(b * tok, (b + 1) * tok)
            former, latter = rope_grad[b, h, :, :half], rope_grad[b, h, :, half:DR]
            query_grad[rows, first + DN : first + DN + half] = (
                former * cosine[rows, :] + latter * sine[rows, :]
            ).astype(BF)
            query_grad[rows, first + DN + half : first + DN + DR] = (
                latter * cosine[rows, :] - former * sine[rows, :]
            ).astype(BF)
        expand_grad[:, h * (DN + DV) : h * (DN + DV) + DN] = tn(
            low, nope[:, h * DN : (h + 1) * DN]
        ).astype(BF)
    for i in range(parts):
        part(i).wait()
        if i + 1 < parts:
            part(i + 1).start()
        hidden_grad[:, i * size : (i + 1) * size] = nt(query_grad[...], w_part[i % 2])


def attend_back(grad, w_output, expand, cat, keys, lse, allowed, mixed, nope, cosine, sine, w_query, scale):
    trees, _, tok, width = cat.shape
    length, rows = keys.shape[1], grad.shape[0]
    vmem = pl.BlockSpec(memory_space=pltpu.VMEM)
    return pl.pallas_call(
        functools.partial(attend_back_kernel, scale),
        out_shape=[
            jax.ShapeDtypeStruct(keys.shape, BF),
            jax.ShapeDtypeStruct((rows, H * (DN + DR)), BF),
            jax.ShapeDtypeStruct((rows, D), F32),
            jax.ShapeDtypeStruct(expand.shape, BF),
        ],
        in_specs=[vmem] * 11 + [pl.BlockSpec(memory_space=pl.ANY)],
        out_specs=[vmem] * 4,
        scratch_shapes=[
            pltpu.VMEM((rows, H * DV), BF),
            pltpu.VMEM((trees, H, tok, LAT), BF),
            pltpu.VMEM((H * tok, length), BF),
            pltpu.VMEM((H * tok, length), BF),
            pltpu.VMEM((trees, H, tok, LAT), BF),
            pltpu.VMEM((trees, H, tok, width - LAT), F32),
            pltpu.VMEM((2, 256, H * (DN + DR)), BF),
            pltpu.SemaphoreType.DMA((2,)),
        ],
        compiler_params=pltpu.CompilerParams(vmem_limit_bytes=60 << 20),
        cost_estimate=pl.CostEstimate(flops=0, bytes_accessed=1 << 20, transcendentals=0),
        name="attend_back",
    )(grad, w_output, expand, cat, keys, lse, allowed, mixed, nope, cosine, sine, w_query)


def body(
    tokens,
    out_grad,
    segments,
    path_mask,
    expert_ids,
    norm_attn,
    attn_q,
    attn_kva,
    norm_latent,
    attn_kvb,
    attn_out,
    norm_ffn,
    router,
    expert_gate,
    expert_up,
    expert_down,
    shared_gate,
    shared_up,
    shared_down,
):
    trees, tok_loc = tokens.shape[:2]
    row_total = trees * tok_loc
    nc, nf = lax.axis_size("ctx"), lax.axis_size("fsdp")
    mine, group = lax.axis_index("ctx"), lax.axis_index("fsdp")
    experts = nc
    ring = Ring(nf, nc)
    tree_len = tok_loc * nc
    group_rows = trees * tree_len
    first_row = mine * tok_loc
    capacity = min(tok_loc, tok_loc * TOP * 4 // (3 * experts))
    slot_total = nc * trees * capacity
    score_scale = 1.0 / math.sqrt(DN + DR)
    frequency = rope_base ** (-(jnp.arange(DR // 2, dtype=F32) * 2.0 / DR))
    labels = jnp.arange(experts, dtype=jnp.int32)
    both = ("fsdp", "ctx")
    part = D // nf

    def roll_in(x):
        return lax.dynamic_slice_in_dim(jnp.concatenate([x, x], axis=-1), group * part, D, x.ndim - 1)

    def roll_out(x):
        return lax.dynamic_slice_in_dim(
            jnp.concatenate([x, x], axis=-1), (nf - group) % nf * part, D, x.ndim - 1
        )

    def fetch(w):
        pieces = [w]
        for k in range(1, nf):
            pieces.append(lax.ppermute(w, "fsdp", [(i, (i - k) % nf) for i in range(nf)]))
        return pieces

    fs = shared_gate.shape[1]
    fp = -(-fs // 128) * 128
    shared_w = jnp.concatenate(
        [jnp.pad(w, ((0, 0), (0, fp - fs))) for w in (shared_gate, shared_up, shared_down)], axis=1
    )
    def one_mask(segment_ids, path_table):
        return tree_mask(segment_ids, path_table, first_row, tok_loc)

    allowed, positions = jax.vmap(one_mask)(segments, path_mask)
    rotation = positions.astype(F32)[:, :, None] * frequency[None, None, :]
    cosine, sine = jnp.cos(rotation), jnp.sin(rotation)
    inputs = tokens.astype(F32).reshape(row_total, D)
    inverse_in = lax.rsqrt(jnp.mean(inputs * inputs, axis=-1, keepdims=True) + epsilon)
    normed_in = inputs * inverse_in

    r_one, r_lat, r_router = norm_attn.shape[0], norm_latent.shape[0], router.size
    small = jnp.concatenate(
        [
            jnp.tile(norm_attn, 128 // r_one),
            jnp.tile(norm_latent, 128 // r_lat),
            norm_attn,
            norm_ffn,
            norm_latent,
            router.reshape(-1),
            expert_ids.astype(BF).reshape(-1),
        ]
    )
    small = jnp.pad(small, (0, 2 * PACK - small.shape[0])).reshape(2 * PACK // 128, 128)
    if nf == 2:
        small_all, w_latent, w_query, w_expand, w_output, other_gate, other_up, keys, hidden_in, latent_all = front(
            ring,
            0,
            [small, attn_kva, attn_q, attn_kvb, attn_out],
            [expert_gate, expert_up],
            normed_in,
            cosine.reshape(row_total, -1),
            sine.reshape(row_total, -1),
            r_lat,
            trees,
            tok_loc,
        )
        e_gate, e_up = [expert_gate, other_gate], [expert_up, other_up]
        later_shared, later_down, later_grads, small_all = lax.optimization_barrier(
            (shared_w, expert_down, out_grad, small_all)
        )
    else:
        w_latent, w_query, w_expand, small_all, w_output = (
            lax.all_gather(w, both, axis=0) for w in (attn_kva, attn_q, attn_kvb, small, attn_out)
        )
        e_gate, e_up = fetch(expert_gate), fetch(expert_up)
        later_shared, later_down, later_grads = shared_w, expert_down, out_grad
    s_all, e_down = fetch(later_shared), fetch(later_down)
    w_output = w_output.reshape(H * DV, D)
    w_latent, w_query = w_latent.reshape(D, -1), w_query.reshape(D, -1)
    w_expand = w_expand.reshape(LAT, -1)
    small_all = small_all.reshape(nf * nc, 2 * PACK)[:, 256:]
    cuts = [0, r_one, 2 * r_one, 2 * r_one + r_lat, 2 * r_one + r_lat + r_router]
    gain_attn = small_all[:, cuts[0] : cuts[1]].reshape(-1).astype(F32)
    gain_ffn = small_all[:, cuts[1] : cuts[2]].reshape(-1).astype(F32)
    gain_latent = small_all[:, cuts[2] : cuts[3]].reshape(-1).astype(F32)
    w_router = small_all[:, cuts[3] : cuts[4]].reshape(D, experts)
    ids_all = lax.dynamic_slice_in_dim(small_all.reshape(nf, nc, -1), group, 1, 0)[0]
    ids_all = ids_all[:, cuts[4] : cuts[4] + expert_ids.size].reshape(nc, trees, tok_loc, TOP)
    ids_all = ids_all.transpose(1, 0, 2, 3).reshape(group_rows, TOP)

    upstream_low = out_grad.reshape(row_total, D)
    upstream = upstream_low.astype(F32)
    tree_grads = lax.all_gather(roll_in(later_grads), "ctx", axis=1, tiled=True).reshape(group_rows, D)

    if nf != 2:
        hidden_in = (normed_in * gain_attn).astype(BF)
        latent_all = multiply(hidden_in, w_latent)
    latent_normed, latent_inverse, latent_gained = normalize(latent_all[:, :LAT], gain_latent)
    if nf != 2:
        key_latent = latent_gained.astype(BF).reshape(trees, tok_loc, LAT)
        key_rope = rotate(latent_all[:, LAT:].reshape(trees, tok_loc, DR), cosine, sine).astype(BF)
        key_pad = jnp.zeros((trees, tok_loc, 128 - DR), BF)
        (keys,) = ring_gather(
            ring, 1, [jnp.concatenate([key_latent, key_rope, key_pad], axis=-1)], [False]
        )
    keys = keys.reshape(trees, tree_len, LAT + 128)
    allowed = allowed.astype(F32)
    query_cat, log_total, mixed, heads, residual, query_nope = attend(
        hidden_in,
        cosine.reshape(row_total, -1),
        sine.reshape(row_total, -1),
        keys,
        allowed,
        w_expand,
        tokens.reshape(row_total, D),
        w_query,
        w_output,
        tok_loc,
        score_scale,
    )
    normed_mid, inverse_mid, gained_mid = normalize(residual, gain_ffn)
    hidden_mid = gained_mid.astype(BF)
    expert_probs = jax.nn.softmax(multiply(hidden_mid, w_router), axis=-1)

    probs_parts = jnp.concatenate(three_parts(expert_probs), axis=-1)
    probs_parts = jnp.pad(probs_parts, ((0, 0), (0, 128 - 3 * experts)))
    tree_rows, tree_probs = ring_gather(
        ring,
        2,
        [roll_in(hidden_mid).reshape(trees, tok_loc, D), probs_parts.reshape(trees, tok_loc, 128)],
        [False, False],
    )
    tree_rows = tree_rows.reshape(group_rows, D)
    tree_probs = tree_probs.reshape(group_rows, 128)

    member = jnp.any(ids_all == mine.astype(BF), axis=1)
    blocks = trees * nc
    bundle = 4 if blocks % 4 == 0 else 1
    bundles = blocks // bundle
    grid = member.astype(BF).reshape(blocks, tok_loc)
    upper = (jnp.arange(tok_loc)[:, None] <= jnp.arange(tok_loc)[None, :]).astype(BF)
    slot = multiply(grid, upper).astype(jnp.int32) - 1
    slot = slot + (jnp.arange(blocks, dtype=jnp.int32) % bundle * capacity)[:, None]
    slot = jnp.where(grid > 0, slot, -1).reshape(bundles, bundle * tok_loc)
    back, out_part, delta_out, e_rows, e_grads, e_hidden, e_gg, e_ug, s_act = run_experts(
        nf,
        experts,
        capacity,
        tok_loc,
        tree_rows,
        tree_grads,
        tree_probs,
        slot,
        list(zip(e_gate, e_up, e_down, s_all)),
    )

    def weight_grads(k, e_gg, e_ug, e_hidden, s_act):
        cut = slice(k * part, (k + 1) * part)
        return (
            transposed_multiply(tree_rows[:, cut], s_act[:, : 2 * fp]),
            transposed_multiply(tree_grads[:, cut], s_act[:, 2 * fp :]),
            transposed_multiply(e_rows[:, cut], e_gg),
            transposed_multiply(e_rows[:, cut], e_ug),
            transposed_multiply(e_grads[:, cut], e_hidden),
        )

    job_arrays = [e_rows, e_grads, tree_rows, tree_grads], [e_gg, e_ug, e_hidden, s_act]
    job_pairs = [
        (2, 3, 0, 2 * fp),
        (3, 3, 2 * fp, fp),
        (0, 0, 0, e_gg.shape[1]),
        (0, 1, 0, e_gg.shape[1]),
        (1, 2, 0, e_gg.shape[1]),
    ]

    def job_cuts(k):
        return [(k * part, part)] * 4

    def by_owner(x):
        return x.reshape(trees, nc, tok_loc, x.shape[-1])

    if nf == 2:
        back_sum, delta_sum, *sent = ring_reduce(
            ring,
            3,
            [by_owner(back), by_owner(delta_out)],
            [False] * 2,
            *job_arrays,
            job_cuts(1),
            job_pairs,
        )
    else:
        back_sum, delta_sum = ring_reduce(
            ring, 3, [by_owner(back), by_owner(delta_out)], [False] * 2
        )
    back_sum, out_part = lax.optimization_barrier((back_sum, out_part))
    back_sum = roll_out(back_sum.reshape(row_total, D))
    prob_delta = jnp.sum(
        delta_sum.reshape(row_total, 128)[:, : 3 * experts].reshape(row_total, 3, experts), axis=1
    )
    out_sum = lax.psum_scatter(
        out_part.reshape(trees, tree_len, D), "ctx", scatter_dimension=1, tiled=True
    )

    came = []
    for k in range(1, nf):
        perm = [(i, (i + k) % nf) for i in range(nf)]
        grads = sent if nf == 2 else weight_grads(k, e_gg, e_ug, e_hidden, s_act)
        came.append([lax.ppermute(g.astype(BF), "fsdp", perm) for g in grads])

    logit_grad = (
        expert_probs * (prob_delta - jnp.sum(expert_probs * prob_delta, axis=-1, keepdims=True))
    ).astype(BF)
    grad_router = transposed_multiply(hidden_mid, logit_grad)
    mid_grad = back_sum + multiply_transposed(logit_grad, w_router)
    mid_input, grad_gain_ffn = normalize_back(mid_grad, normed_mid, inverse_mid, gain_ffn)
    residual_grad = upstream + mid_input
    residual_low = residual_grad.astype(BF)
    keys_grad, query_grad, hidden_grad, grad_expand = attend_back(
        residual_low,
        w_output,
        w_expand,
        query_cat,
        keys,
        log_total,
        allowed,
        mixed,
        query_nope,
        cosine.reshape(row_total, -1),
        sine.reshape(row_total, -1),
        w_query,
        score_scale,
    )
    own_keys_grad, grad_query, grad_output = ring_reduce(
        ring,
        4,
        [keys_grad.reshape(trees, nc, tok_loc, LAT + 128)],
        [False],
        [hidden_in, heads],
        [query_grad, residual_low],
        [(0, D), (0, H * DV)],
        [(0, 0, 0, query_grad.shape[1]), (1, 1, 0, D)],
    )
    latent_in_grad, grad_gain_latent = normalize_back(
        own_keys_grad[..., :LAT].reshape(row_total, LAT), latent_normed, latent_inverse, gain_latent
    )
    rope_back = rotate(own_keys_grad[..., LAT : LAT + DR], cosine, -sine).reshape(row_total, DR)
    latent_grad = jnp.concatenate([latent_in_grad, rope_back], axis=-1).astype(BF)
    grad_latent = transposed_multiply(hidden_in, latent_grad)
    hidden_grad = hidden_grad + multiply_transposed(latent_grad, w_latent)
    input_part, grad_gain_attn = normalize_back(hidden_grad, normed_in, inverse_in, gain_attn)
    input_grad = (input_part + residual_grad).reshape(trees, tok_loc, D)

    grad_small = jnp.concatenate(
        [
            grad_gain_attn.reshape(nf * nc, r_one),
            grad_gain_ffn.reshape(nf * nc, r_one),
            grad_gain_latent.reshape(nf * nc, r_lat),
            grad_router.reshape(nf * nc, r_router),
        ],
        axis=1,
    ).astype(BF)
    grad_small = jnp.pad(grad_small, ((0, 0), (0, PACK - grad_small.shape[1])))
    parts = [
        grad_query.reshape(nf, nc, -1, w_query.shape[1]),
        grad_expand.reshape(nf, nc, -1, w_expand.shape[1]),
        grad_latent.astype(BF).reshape(nf, nc, -1, w_latent.shape[1]),
        grad_small.reshape(nf, nc, 16, PACK // 16),
        grad_output.reshape(nf, nc, -1, D),
    ]
    if nf == 2:
        t_query, t_expand, t_latent, t_small, out_total, *ffn_sums = ring_reduce(
            ring, 5, parts, [True] * 5, *job_arrays, job_cuts(0), job_pairs
        )
        came, ffn_sums = lax.optimization_barrier((came, ffn_sums))
    else:
        t_query, t_expand, t_latent, t_small, out_total = (
            lax.psum_scatter(
                x.reshape((nf * nc,) + x.shape[2:]), both, scatter_dimension=0, tiled=True
            )[0].astype(F32)
            for x in parts
        )
        ffn_sums = weight_grads(0, e_gg, e_ug, e_hidden, s_act)
    t_small, out_sum = lax.optimization_barrier((t_small, out_sum))
    out_sum = roll_out(out_sum.reshape(row_total, D).astype(F32))
    output = (residual + out_sum).astype(BF).reshape(trees, tok_loc, D)
    t_small = t_small.reshape(PACK)
    for one in came:
        ffn_sums = [a.astype(F32) + b.astype(F32) for a, b in zip(ffn_sums, one)]
    e_sums = ffn_sums[2:]
    s_sums = [ffn_sums[0][:, :fs], ffn_sums[0][:, fp : fp + fs], ffn_sums[1][:, :fs]]
    return (
        output,
        input_grad,
        t_small[cuts[0] : cuts[1]],
        t_query,
        t_latent,
        t_small[cuts[2] : cuts[3]],
        t_expand,
        out_total,
        t_small[cuts[1] : cuts[2]],
        t_small[cuts[3] : cuts[4]].reshape(-1, experts),
        *e_sums,
        *s_sums,
    )


def solution(mesh):
    placed = (
        P("fsdp", "ctx", None),
        P("fsdp", "ctx", None),
        P("fsdp", None),
        P("fsdp", None, None),
        P("fsdp", "ctx", None),
        P(("fsdp", "ctx")),
        P(("fsdp", "ctx"), None),
        P(("fsdp", "ctx"), None),
        P(("fsdp", "ctx")),
        P(("fsdp", "ctx"), None),
        P(("fsdp", "ctx"), None),
        P(("fsdp", "ctx")),
        P(("fsdp", "ctx"), None),
        P("fsdp", "ctx"),
        P("fsdp", "ctx"),
        P("fsdp", "ctx"),
        P("fsdp", "ctx"),
        P("fsdp", "ctx"),
        P("fsdp", "ctx"),
    )
    return jax.shard_map(
        body,
        mesh=mesh,
        in_specs=placed,
        out_specs=(
            P("fsdp", "ctx", None),
            P("fsdp", "ctx", None),
            P(("fsdp", "ctx")),
            P(("fsdp", "ctx"), None),
            P(("fsdp", "ctx"), None),
            P(("fsdp", "ctx")),
            P(("fsdp", "ctx"), None),
            P(("fsdp", "ctx"), None),
            P(("fsdp", "ctx")),
            P(("fsdp", "ctx"), None),
            P("fsdp", "ctx"),
            P("fsdp", "ctx"),
            P("fsdp", "ctx"),
            P("fsdp", "ctx"),
            P("fsdp", "ctx"),
            P("fsdp", "ctx"),
        ),
        check_vma=False,
    )
```
